32 devices in a mesh: fsdp: 4 (over x, core), ctx: 2 (over y), tp: 4 (over z).
Axes of the slice: x: 2, y: 2, z: 4, core: 2. Of those that a mesh axis runs over, the one named last changes fastest.
Arguments:
- tokens: bfloat16 [8, 1024, 2048], P('fsdp', 'ctx'), may hold values from -6 to 6
- w_query: bfloat16 [2048, 2048], P(('fsdp', 'ctx'), 'tp'), may hold values from -0.125 to 0.125
- w_key: bfloat16 [2048, 2048], P(('fsdp', 'ctx'), 'tp'), may hold values from -0.125 to 0.125
- w_value: bfloat16 [2048, 2048], P(('fsdp', 'ctx'), 'tp'), may hold values from -0.125 to 0.125
- w_output: bfloat16 [2048, 2048], P('tp', ('fsdp', 'ctx')), may hold values from -0.125 to 0.125
- w_gate: bfloat16 [2048, 8192], P(('fsdp', 'ctx'), 'tp'), may hold values from -0.125 to 0.125
- w_up: bfloat16 [2048, 8192], P(('fsdp', 'ctx'), 'tp'), may hold values from -0.125 to 0.125
- w_down: bfloat16 [8192, 2048], P('tp', ('fsdp', 'ctx')), may hold values from -0.0625 to 0.0625
- gain_query: bfloat16 [2048], P('tp'), may hold values from 0.25 to 1.75
- gain_key: bfloat16 [2048], P('tp'), may hold values from 0.25 to 1.75
- gain_attn: bfloat16 [2048], replicated, may hold values from 0.25 to 1.75
- gain_mlp: bfloat16 [2048], replicated, may hold values from 0.25 to 1.75
- cotangent: bfloat16 [8, 1024, 2048], P('fsdp', 'ctx'), may hold values from -6 to 6
Outputs:
- output: bfloat16 [8, 1024, 2048], P('fsdp', 'ctx')
- grad_tokens: bfloat16 [8, 1024, 2048], P('fsdp', 'ctx')
- grad_w_query: float32 [2048, 2048], P(('fsdp', 'ctx'), 'tp')
- grad_w_key: float32 [2048, 2048], P(('fsdp', 'ctx'), 'tp')
- grad_w_value: float32 [2048, 2048], P(('fsdp', 'ctx'), 'tp')
- grad_w_output: float32 [2048, 2048], P('tp', ('fsdp', 'ctx'))
- grad_w_gate: float32 [2048, 8192], P(('fsdp', 'ctx'), 'tp')
- grad_w_up: float32 [2048, 8192], P(('fsdp', 'ctx'), 'tp')
- grad_w_down: float32 [8192, 2048], P('tp', ('fsdp', 'ctx'))
- grad_gain_query: float32 [2048], P('tp')
- grad_gain_key: float32 [2048], P('tp')
- grad_gain_attn: float32 [2048], replicated
- grad_gain_mlp: float32 [2048], replicated
The draws below stay inside these ranges and needn't reach their ends.
All inputs are finite; a program needn't handle non-finite values.
Results may differ from the reference program's by a relative error of at most 0.025.
Values may be sent and summed in bfloat16 or wider, within the bound.
A program may use at most 256 MiB of HBM per device.

```python
import jax
import jax.numpy as jnp
from jax import lax

D = 2048
HEADS = 16
HD = 128
FF = 8192
LENGTH = 1024
SEQS = 8


def block_levels(rng, shape, split, least, high):
    factor_of, own = 1.0, jax.random.fold_in(rng, 6)
    for axis_at, shards_of in split:
        draws = jnp.exp(jax.random.uniform(jax.random.fold_in(own, axis_at), (shards_of,), jnp.float32, least / len(split), high / len(split)))
        factor_of = factor_of * jnp.repeat(draws, shape[axis_at] // shards_of).reshape([-1 if axis == axis_at else 1 for axis in range(len(shape))])
    return factor_of


def gaussian(stream_key, dims, deviation, bound, split=(), held_as=jnp.bfloat16):
    values = jax.random.normal(stream_key, dims, jnp.float32) * deviation
    if len(split) > 0:
        values = block_levels(stream_key, dims, split, -0.22, 0.18) * values
    return jnp.clip(values, min=-bound, max=bound).astype(held_as)


def setup_inputs(seed: int = 0) -> dict:
    arg_keys = jax.random.split(jax.random.key(seed), 14)
    tokens = gaussian(arg_keys[0], (SEQS, LENGTH, D), 1.0, 6.0, ((0, 4), (1, 2)))
    w_query = gaussian(arg_keys[1], (D, D), D ** -0.5, 0.125, ((0, 8), (1, 4)))
    w_key = gaussian(arg_keys[2], (D, D), D ** -0.5, 0.125, ((0, 8), (1, 4)))
    w_value = gaussian(arg_keys[3], (D, D), D ** -0.5, 0.125, ((0, 8), (1, 4)))
    w_output = gaussian(arg_keys[4], (D, D), D ** -0.5, 0.125, ((0, 4), (1, 8)))
    w_gate = gaussian(arg_keys[5], (D, FF), D ** -0.5, 0.125, ((0, 8), (1, 4)))
    w_up = gaussian(arg_keys[6], (D, FF), D ** -0.5, 0.125, ((0, 8), (1, 4)))
    w_down = gaussian(arg_keys[7], (FF, D), FF ** -0.5, 0.0625, ((0, 4), (1, 8)))
    gain_query = jnp.clip(1.0 + 0.15 * jax.random.normal(arg_keys[8], (D,), jnp.float32), 0.25, 1.75).astype(jnp.bfloat16)
    gain_key = jnp.clip(1.0 + 0.15 * jax.random.normal(arg_keys[9], (D,), jnp.float32), 0.25, 1.75).astype(jnp.bfloat16)
    gain_attn = jnp.clip(1.0 + 0.15 * jax.random.normal(arg_keys[10], (D,), jnp.float32), 0.25, 1.75).astype(jnp.bfloat16)
    gain_mlp = jnp.clip(1.0 + 0.15 * jax.random.normal(arg_keys[11], (D,), jnp.float32), 0.25, 1.75).astype(jnp.bfloat16)
    cotangent = gaussian(arg_keys[12], (SEQS, LENGTH, D), 1.0, 6.0, ((0, 4), (1, 2)))
    return {"tokens": tokens, "w_query": w_query, "w_key": w_key, "w_value": w_value, "w_output": w_output, "w_gate": w_gate, "w_up": w_up, "w_down": w_down, "gain_query": gain_query, "gain_key": gain_key, "gain_attn": gain_attn, "gain_mlp": gain_mlp, "cotangent": cotangent}


@jax.custom_vjp
def low(v):
    return lax.optimization_barrier(v.astype(jnp.bfloat16)).astype(jnp.float32)

@jax.custom_vjp
def low_back(v):
    return v

def low_keep(v):
    return (low(v), None)

def low_pass(kept, grad):
    return (grad,)

def back_keep(v):
    return (v, None)

def back_low(kept, grad):
    return (low(grad),)
low.defvjp(low_keep, low_pass)
low_back.defvjp(back_keep, back_low)
exact_mode = lax.Precision.HIGHEST
norm_eps = 1e-06
rope_theta = 500000.0
masked_value = -1e+30

def matmul(left_matrix, right_matrix):
    return jnp.dot(left_matrix, right_matrix, precision=exact_mode)

def rms_scale(values, gain_vector):
    return values * lax.rsqrt(lax.optimization_barrier(jnp.mean(values * values, axis=-1, keepdims=True)) + norm_eps) * gain_vector

def rotate(values, positions):
    half_width = values.shape[-1] // 2
    frequency = rope_theta ** (-jnp.arange(half_width, dtype=jnp.float32) * 2.0 / values.shape[-1])
    angles = positions.astype(jnp.float32)[:, None] * frequency[None, :]
    cosine = jnp.cos(angles)[:, None, :]
    sine_table = jnp.sin(angles)[:, None, :]
    first_half = values[..., :half_width]
    second_half = values[..., half_width:]
    return jnp.concatenate([first_half * cosine - second_half * sine_table, second_half * cosine + first_half * sine_table], axis=-1)

def layer(tokens_f, w_query, w_key, w_value, w_output, w_gate, w_up, w_down, gain_query, gain_key, gain_attn, gain_mlp):
    length = tokens_f.shape[0]
    positions = jnp.arange(length, dtype=jnp.int32)
    queries = low_back(matmul(tokens_f, w_query))
    key_raw = low_back(matmul(tokens_f, w_key))
    value_low = low(low_back(matmul(tokens_f, w_value))).reshape(length, HEADS, HD)
    q_low = low(rotate(rms_scale(queries, gain_query).reshape(length, HEADS, HD), positions))
    k_low = low(rotate(rms_scale(key_raw, gain_key).reshape(length, HEADS, HD), positions))
    scores = low_back(jnp.einsum('qhd,khd->hqk', q_low, k_low, precision=exact_mode) * HD ** (-0.5))
    causal = positions[:, None] >= positions[None, :]
    scores = jnp.where(causal[None], scores, masked_value)
    row_top = lax.optimization_barrier(jnp.max(scores, axis=-1, keepdims=True))
    weights_exp = jnp.exp(scores - row_top)
    row_total = lax.optimization_barrier(jnp.sum(weights_exp, axis=-1))
    head_out = jnp.einsum('hqk,khd->qhd', low(weights_exp), value_low, precision=exact_mode) / jnp.transpose(row_total)[:, :, None]
    head_low = low(low_back(head_out.reshape(length, HEADS * HD)))
    attention = low_back(matmul(head_low, w_output))
    mixed_rows = tokens_f + rms_scale(attention, gain_attn)
    mlp_in = low(mixed_rows)
    gate_proj = low_back(matmul(mlp_in, w_gate))
    up_proj = low_back(matmul(mlp_in, w_up))
    hidden = low(jax.nn.silu(gate_proj) * up_proj)
    down_proj = low_back(matmul(hidden, w_down))
    return mixed_rows + rms_scale(down_proj, gain_mlp)

def reference(tokens, w_query, w_key, w_value, w_output, w_gate, w_up, w_down, gain_query, gain_key, gain_attn, gain_mlp, cotangent):
    params = tuple((item.astype(jnp.float32) for item in (w_query, w_key, w_value, w_output, w_gate, w_up, w_down, gain_query, gain_key, gain_attn, gain_mlp)))

    def one_sequence(running, pair):
        seq_tokens, seq_grad = pair
        result, pull = jax.vjp(layer, seq_tokens.astype(jnp.float32), *params)
        grads = pull(seq_grad.astype(jnp.float32))
        updated = tuple((prior + extra for prior, extra in zip(running, grads[1:])))
        return (updated, (result.astype(jnp.bfloat16), grads[0].astype(jnp.bfloat16)))
    start_sums = tuple((jnp.zeros(item.shape, jnp.float32) for item in params))
    totals, (outputs, input_grads) = lax.scan(one_sequence, start_sums, (tokens, cotangent))
    return (outputs, input_grads, totals[0], totals[1], totals[2], totals[3], totals[4], totals[5], totals[6], totals[7], totals[8], totals[9], totals[10])
```

```python
import functools

import jax
import jax.numpy as jnp
from jax import lax
from jax.experimental import pallas as pl
from jax.experimental.pallas import tpu as pltpu
from jax.sharding import PartitionSpec as P

HD = 128
norm_eps = 1e-06
rope_theta = 500000.0
masked_value = -1e30
f32 = jnp.float32
bf16 = jnp.bfloat16


def dot(a, b, dims, out=f32):
    return lax.dot_general(a, b, (dims, ((), ())), preferred_element_type=f32).astype(out)


PIECE = 16
LAG = 1
CHUNK = 256


class Line:
    def __init__(self, axis, n, groups, buf, total, send, recv):
        self.axis, self.n, self.groups = axis, n, groups
        self.buf, self.total, self.send, self.recv = buf, total, send, recv
        self.i = lax.axis_index(axis)
        self.stages = 2 * n - 1

    def rows(self, group, c, count=1):
        return pl.ds(pl.multiple_of((group * self.n + c) * PIECE, PIECE), count * PIECE)

    def copy(self, way, step, group, c, source):
        rows = self.rows(group, c)
        return pltpu.make_async_remote_copy(
            src_ref=self.buf.at[source, rows],
            dst_ref=self.buf.at[0 if way == 0 else 2, rows],
            send_sem=self.send.at[way, step, group],
            recv_sem=self.recv.at[way, step, group],
            device_id={self.axis: self.i + (1 if way == 0 else -1)},
            device_id_type=pl.DeviceIdType.MESH,
        )

    def add(self, c, group, source):
        rows = self.rows(group, c)
        both = self.buf[1, rows].astype(f32) + self.buf[source, rows].astype(f32)
        self.buf[1, rows] = both.astype(bf16)

    def reduce_step(self, s, group):
        i, n = self.i, self.n

        @pl.when(i <= min(s - 1, n - 2))
        def _():
            c = n - s + i
            if s >= 2:

                @pl.when(i >= 1)
                def _():
                    self.copy(0, s - 2, group, c, 1).wait_recv()
                    self.add(c, group, 0)

            self.copy(0, s - 1, group, c, 1).start()

        @pl.when(i >= max(n - s, 1))
        def _():
            c = s + i - n
            if s >= 2:

                @pl.when(i <= n - 2)
                def _():
                    self.copy(1, s - 2, group, c, 1).wait_recv()
                    self.add(c, group, 2)

            self.copy(1, s - 1, group, c, 1).start()

    def finish(self, group, then):
        i, n = self.i, self.n
        rows = self.rows(group, i)
        self.total[...] = self.buf[1, rows].astype(f32)

        @pl.when(i >= 1)
        def _():
            self.copy(0, n - 2, group, i, 1).wait_recv()
            self.total[...] += self.buf[0, rows].astype(f32)

        @pl.when(i <= n - 2)
        def _():
            self.copy(1, n - 2, group, i, 1).wait_recv()
            self.total[...] += self.buf[2, rows].astype(f32)

        self.buf[1, rows] = then(group, self.total[...]).astype(bf16)

        @pl.when(i <= n - 2)
        def _():
            self.copy(0, n - 1, group, i, 1).start()

        @pl.when(i >= 1)
        def _():
            self.copy(1, n - 1, group, i, 1).start()

    def gather_step(self, s, group):
        i, n = self.i, self.n

        @pl.when(i >= s - 1)
        def _():
            c = i - s + 1
            self.copy(0, n + s - 3, group, c, 0).wait_recv()
            if s <= n - 1:

                @pl.when(i <= n - 2)
                def _():
                    self.copy(0, n + s - 2, group, c, 0).start()

        @pl.when(i <= n - s)
        def _():
            c = i + s - 1
            self.copy(1, n + s - 3, group, c, 2).wait_recv()
            if s <= n - 1:

                @pl.when(i >= 1)
                def _():
                    self.copy(1, n + s - 2, group, c, 2).start()

    def sent(self, group):
        i, n = self.i, self.n
        for s in range(1, n):

            @pl.when(i <= min(s - 1, n - 2))
            def _():
                self.copy(0, s - 1, group, n - s + i, 1).wait_send()

            @pl.when(i >= max(n - s, 1))
            def _():
                self.copy(1, s - 1, group, s + i - n, 1).wait_send()

            @pl.when((i >= s - 1) & (i <= n - 2))
            def _():
                self.copy(0, n + s - 2, group, i - s + 1, 1 if s == 1 else 0).wait_send()

            @pl.when((i <= n - s) & (i >= 1))
            def _():
                self.copy(1, n + s - 2, group, i + s - 1, 1 if s == 1 else 2).wait_send()

    def piece(self, group, c):
        slot = jnp.where(c < self.i, 0, jnp.where(c > self.i, 2, 1))
        return self.buf[slot, self.rows(group, c)]

    def piece_ref(self, group, c):
        slot = jnp.where(c < self.i, 0, jnp.where(c > self.i, 2, 1))
        return self.buf.at[slot, self.rows(group, c)]

    def tick(self, t, then, done):
        n = self.n

        def stage(index, body):
            group = t - index * LAG

            @pl.when((group >= 0) & (group < self.groups))
            def _():
                body(group)

        for s in range(1, n):
            stage(s - 1, functools.partial(self.reduce_step, s))
        stage(n - 1, lambda group: self.finish(group, then))
        for s in range(2, n):
            stage(n + s - 2, functools.partial(self.gather_step, s))

        def last(group):
            self.gather_step(n, group)
            self.sent(group)
            done(group)

        stage(2 * n - 2, last)

    def ticks(self):
        return self.groups + (2 * self.n - 2) * LAG


def greet(axis, n):
    i = lax.axis_index(axis)
    barrier = pltpu.get_barrier_semaphore()

    @pl.when(i >= 1)
    def _():
        pl.semaphore_signal(barrier, inc=1, device_id={axis: i - 1}, device_id_type=pl.DeviceIdType.MESH)

    @pl.when(i <= n - 2)
    def _():
        pl.semaphore_signal(barrier, inc=1, device_id={axis: i + 1}, device_id_type=pl.DeviceIdType.MESH)

    pl.semaphore_wait(barrier, jnp.minimum(i, 1) + jnp.minimum(n - 1 - i, 1))


def line_scratch(n, rows, width):
    sems = pltpu.SemaphoreType.DMA((2, 2 * n - 2, rows // (n * PIECE)))
    return [pltpu.VMEM((3, rows, width), bf16), pltpu.VMEM((PIECE, width), f32), sems, sems]


def params(collective_id):
    return pltpu.CompilerParams(
        collective_id=collective_id, has_side_effects=True, vmem_limit_bytes=60 << 20
    )


def scale_of(a):
    return lax.rsqrt(jnp.mean(a * a, axis=-1, keepdims=True) + norm_eps)


def attn_out_kernel(n, head, w_out_t, x, gain, attention, mlp_in, buf, total, send, recv):
    rows, width = x.shape
    groups = rows // (n * PIECE)
    line = Line("tp", n, groups, buf, total, send, recv)
    greet("tp", n)
    per_chunk = CHUNK // (n * PIECE)
    tile = 512

    def done(group):
        for c in range(n):
            at = line.rows(group, c)
            low = line.piece(group, c)
            attention[at] = low
            a = low.astype(f32)
            mlp_in[at] = (x[at].astype(f32) + a * scale_of(a) * gain[...]).astype(bf16)

    @pl.loop(0, line.ticks())
    def _(t):
        @pl.when((t < groups) & (lax.rem(t, per_chunk) == 0))
        def _():
            at = pl.ds(pl.multiple_of(t * n * PIECE, CHUNK), CHUNK)

            @pl.loop(0, width // tile)
            def _(j):
                cols = pl.ds(pl.multiple_of(j * tile, tile), tile)
                buf[1, at, cols] = dot(head[at], w_out_t[cols], ((1,), (1,)), bf16)

        line.tick(t, lambda group, total: total, done)


def attn_out(head, w_out_t, x, gain, n):
    rows, width = x.shape
    vmem = pl.BlockSpec(memory_space=pltpu.VMEM)
    return pl.pallas_call(
        functools.partial(attn_out_kernel, n),
        out_shape=[jax.ShapeDtypeStruct(x.shape, bf16)] * 2,
        in_specs=[vmem] * 4,
        out_specs=[vmem] * 2,
        scratch_shapes=line_scratch(n, rows, width),
        compiler_params=params(1),
        cost_estimate=pl.CostEstimate(flops=100 * 10**9, bytes_accessed=20 << 20, transcendentals=0),
        name="attn_out",
    )(head, w_out_t, x, gain)


def local_copies(pairs, sems):
    copies = [pltpu.make_async_copy(a, b, sems.at[k]) for k, (a, b) in enumerate(pairs)]
    for copy in copies:
        copy.start()
    return copies


def mlp_kernel(
    n, mlp_in, grad, attn_own, gain_m, gain_a, w_g_hbm, w_u_hbm, w_d_hbm,
    down_out, down_low_out, hidden_out, gate_out, up_out, attn_low_out, mixed_own, gain_m_sum, gain_a_sum,
    buf, total, send, recv, w_g, w_u, w_d, mlp_rows, hidden, gate_low, up_low, down_low, gate_kept, up_kept,
    ready, w_sems, io_sems, piece_sems,
):
    rows, width = grad.shape
    units = w_g.shape[1]
    groups = rows // (n * PIECE)
    per_chunk = CHUNK // (n * PIECE)
    line = Line("tp", n, groups, buf, total, send, recv)
    i = line.i
    weights = local_copies([(w_g_hbm, w_g), (w_u_hbm, w_u), (w_d_hbm, w_d)], w_sems)
    gain_m_sum[...] = jnp.zeros_like(gain_m_sum)
    gain_a_sum[...] = jnp.zeros_like(gain_a_sum)
    greet("tp", n)
    offset = per_chunk + line.stages - 1
    tile = 512

    def chunk_rows(chunk):
        return pl.ds(pl.multiple_of(chunk * CHUNK, CHUNK), CHUNK)

    def hidden_copy(chunk):
        return pltpu.make_async_copy(hidden, hidden_out.at[chunk_rows(chunk)], io_sems.at[1])

    def back_copies(chunk):
        at = chunk_rows(chunk)
        return [
            pltpu.make_async_copy(gate_low, gate_out.at[at], io_sems.at[2]),
            pltpu.make_async_copy(up_low, up_out.at[at], io_sems.at[3]),
            pltpu.make_async_copy(down_low, down_low_out.at[at], io_sems.at[4]),
        ]

    def forward(chunk, first):
        at = chunk_rows(chunk)
        fetch = pltpu.make_async_copy(mlp_in.at[at], mlp_rows, io_sems.at[0])
        fetch.start()
        if first:
            weights[0].wait()
            weights[1].wait()
        else:
            hidden_copy(chunk - 1).wait()
        fetch.wait()

        @pl.loop(0, units // tile)
        def _(j):
            cols = pl.ds(pl.multiple_of(j * tile, tile), tile)
            gate = dot(mlp_rows[...], w_g[:, cols], ((1,), (0,)))
            up = dot(mlp_rows[...], w_u[:, cols], ((1,), (0,)))
            gate_kept[at, cols] = gate.astype(bf16)
            up_kept[at, cols] = up.astype(bf16)
            hidden[:, cols] = (gate / (1.0 + jnp.exp(-gate)) * up).astype(bf16)

        hidden_copy(chunk).start()
        if first:
            weights[2].wait()

        @pl.loop(0, width // tile)
        def _(j):
            cols = pl.ds(pl.multiple_of(j * tile, tile), tile)
            buf[1, at, cols] = dot(hidden[...], w_d[cols], ((1,), (1,)), bf16)

    def backward(chunk):
        at = chunk_rows(chunk)

        @pl.loop(0, units // tile)
        def _(j):
            cols = pl.ds(pl.multiple_of(j * tile, tile), tile)
            gate = gate_kept[at, cols].astype(f32)
            sig = 1.0 / (1.0 + jnp.exp(-gate))
            grad_hidden = dot(down_low[...], w_d[:, cols], ((1,), (0,)))
            up_low[:, cols] = (grad_hidden * gate * sig).astype(bf16)
            gate_low[:, cols] = (
                grad_hidden * up_kept[at, cols].astype(f32) * sig * (1.0 + gate * (1.0 - sig))
            ).astype(bf16)

        for copy in back_copies(chunk):
            copy.start()

        @pl.loop(0, width // tile)
        def _(j):
            cols = pl.ds(pl.multiple_of(j * tile, tile), tile)
            buf[1, at, cols] = (
                dot(gate_low[...], w_g[cols], ((1,), (1,))) + dot(up_low[...], w_u[cols], ((1,), (1,)))
            ).astype(bf16)

        for copy in back_copies(chunk):
            copy.wait()

    def pieces_out(group, out):
        return local_copies([(line.piece_ref(group, c), out.at[line.rows(group, c)]) for c in range(n)], piece_sems)

    def down_done(group):
        copies = pieces_out(group, down_out)
        for c in range(n):
            at = line.rows(group, c)
            branch = line.piece(group, c).astype(f32)
            r = scale_of(branch)
            g = grad[at].astype(f32)
            scaled = g * gain_m[...]
            inner = jnp.mean(scaled * branch, axis=-1, keepdims=True)
            gain_m_sum[...] += g * branch * r
            inside = pl.ds(pl.multiple_of((lax.rem(group, per_chunk) * n + c) * PIECE, PIECE), PIECE)
            down_low[inside] = (r * scaled - branch * (r * r * r) * inner).astype(bf16)
        for copy in copies:
            copy.wait()

    def attn_grad(group, total):
        at = pl.ds(pl.multiple_of(group * PIECE, PIECE), PIECE)
        mixed = grad[line.rows(group, i)].astype(f32) + total
        mixed_own[at] = mixed
        branch = attn_own[at].astype(f32)
        r = scale_of(branch)
        scaled = mixed * gain_a[...]
        inner = jnp.mean(scaled * branch, axis=-1, keepdims=True)
        gain_a_sum[...] += mixed * branch * r
        return r * scaled - branch * (r * r * r) * inner

    def attn_done(group):
        for copy in pieces_out(group, attn_low_out):
            copy.wait()

    forward(0, True)

    @pl.loop(0, offset + line.ticks())
    def _(t):
        back = t - offset

        @pl.when((back >= 0) & (back < groups) & (lax.rem(back + groups, per_chunk) == 0))
        def _():
            @pl.when(i >= 1)
            def _():
                pl.semaphore_wait(ready.at[0], 1)

            @pl.when(i <= n - 2)
            def _():
                pl.semaphore_wait(ready.at[1], 1)

        line.tick(back, attn_grad, attn_done)
        line.tick(t, lambda group, total: total, down_done)
        after = t + 1

        @pl.when((after < groups) & (lax.rem(after, per_chunk) == 0))
        def _():
            forward(lax.div(after, per_chunk), False)

        next_back = after - offset

        @pl.when((next_back >= 0) & (next_back < groups) & (lax.rem(next_back + groups, per_chunk) == 0))
        def _():
            @pl.when(i >= 1)
            def _():
                pl.semaphore_signal(
                    ready.at[1], inc=1, device_id={"tp": i - 1}, device_id_type=pl.DeviceIdType.MESH
                )

            @pl.when(i <= n - 2)
            def _():
                pl.semaphore_signal(
                    ready.at[0], inc=1, device_id={"tp": i + 1}, device_id_type=pl.DeviceIdType.MESH
                )

            backward(lax.div(next_back, per_chunk))

    hidden_copy(rows // CHUNK - 1).wait()


def mlp(mlp_in, grad, attn_own, gain_m, gain_a, w_g, w_u, w_d, n):
    rows, width = grad.shape
    units = w_g.shape[1]
    vmem, anywhere = pl.BlockSpec(memory_space=pltpu.VMEM), pl.BlockSpec(memory_space=pl.ANY)
    acts = jax.ShapeDtypeStruct((rows, width), bf16)
    inner = jax.ShapeDtypeStruct((rows, units), bf16)
    per_piece = jax.ShapeDtypeStruct((PIECE, width), f32)
    return pl.pallas_call(
        functools.partial(mlp_kernel, n),
        out_shape=[acts, acts, inner, inner, inner, acts, jax.ShapeDtypeStruct((rows // n, width), f32), per_piece, per_piece],
        in_specs=[anywhere] + [vmem] * 4 + [anywhere] * 3,
        out_specs=[anywhere] * 6 + [vmem] * 3,
        scratch_shapes=line_scratch(n, rows, width) + [
            pltpu.VMEM(w_g.shape, bf16), pltpu.VMEM(w_u.shape, bf16), pltpu.VMEM(w_d.shape, bf16),
            pltpu.VMEM((CHUNK, width), bf16),
            pltpu.VMEM((CHUNK, units), bf16), pltpu.VMEM((CHUNK, units), bf16), pltpu.VMEM((CHUNK, units), bf16),
            pltpu.VMEM((CHUNK, width), bf16),
            pltpu.VMEM((rows, units), bf16), pltpu.VMEM((rows, units), bf16),
            pltpu.SemaphoreType.REGULAR((2,)),
            pltpu.SemaphoreType.DMA((3,)), pltpu.SemaphoreType.DMA((5,)), pltpu.SemaphoreType.DMA((n,)),
        ],
        compiler_params=params(2),
        cost_estimate=pl.CostEstimate(flops=200 * 10**9, bytes_accessed=60 << 20, transcendentals=0),
        name="mlp",
    )(mlp_in, grad, attn_own, gain_m, gain_a, w_g, w_u, w_d)


def input_grad_kernel(n, grad_qkv, w_qkv_hbm, mixed_own, grad_out, buf, total, send, recv, w_qkv, w_sem, piece_sems):
    rows, width = buf.shape[1:]
    groups = rows // (n * PIECE)
    per_chunk = CHUNK // (n * PIECE)
    line = Line("tp", n, groups, buf, total, send, recv)
    fetch = pltpu.make_async_copy(w_qkv_hbm, w_qkv, w_sem)
    fetch.start()
    greet("tp", n)
    fetch.wait()
    tile = 512

    def own(group, total):
        return total + mixed_own[pl.ds(pl.multiple_of(group * PIECE, PIECE), PIECE)]

    def done(group):
        copies = local_copies(
            [(line.piece_ref(group, c), grad_out.at[line.rows(group, c)]) for c in range(n)], piece_sems
        )
        for copy in copies:
            copy.wait()

    @pl.loop(0, line.ticks())
    def _(t):
        @pl.when((t < groups) & (lax.rem(t, per_chunk) == 0))
        def _():
            at = pl.ds(pl.multiple_of(t * n * PIECE, CHUNK), CHUNK)

            @pl.loop(0, width // tile)
            def _(j):
                cols = pl.ds(pl.multiple_of(j * tile, tile), tile)
                buf[1, at, cols] = dot(grad_qkv[at], w_qkv[cols], ((1,), (1,)), bf16)

        line.tick(t, own, done)


def input_grad(grad_qkv, w_qkv, mixed_own, n):
    rows, width = grad_qkv.shape[0], w_qkv.shape[0]
    vmem, anywhere = pl.BlockSpec(memory_space=pltpu.VMEM), pl.BlockSpec(memory_space=pl.ANY)
    return pl.pallas_call(
        functools.partial(input_grad_kernel, n),
        out_shape=jax.ShapeDtypeStruct((rows, width), bf16),
        in_specs=[vmem, anywhere, vmem],
        out_specs=anywhere,
        scratch_shapes=line_scratch(n, rows, width) + [
            pltpu.VMEM(w_qkv.shape, bf16), pltpu.SemaphoreType.DMA, pltpu.SemaphoreType.DMA((n,)),
        ],
        compiler_params=params(3),
        cost_estimate=pl.CostEstimate(flops=100 * 10**9, bytes_accessed=20 << 20, transcendentals=0),
        name="input_grad",
    )(grad_qkv, w_qkv, mixed_own)


def small_sum(values, axis):
    n = lax.axis_size(axis)
    total = values
    for k in range(1, n):
        total = total + lax.ppermute(values, axis, [(a, (a + k) % n) for a in range(n)])
    return total


def rotation_tables(positions):
    half = HD // 2
    frequency = rope_theta ** (-jnp.arange(half, dtype=f32) * 2.0 / HD)
    angles = positions.astype(f32)[:, None] * frequency[None, :]
    return jnp.cos(angles)[:, None, :], jnp.sin(angles)[:, None, :]


def rotate(values, cosine, sine):
    half = HD // 2
    first, second = values[..., :half], values[..., half:]
    return jnp.concatenate([first * cosine - second * sine, second * cosine + first * sine], axis=-1)


def per_device(
    tokens, w_query, w_key, w_value, w_output, w_gate, w_up, w_down,
    gain_query, gain_key, gain_attn, gain_mlp, cotangent,
):
    micro_count, rows, width = tokens.shape
    local = w_query.shape[1]
    heads = local // HD
    ctx = lax.axis_size("ctx")
    ctx_rank = lax.axis_index("ctx")
    tp = lax.axis_size("tp")
    tp_rank = lax.axis_index("tp")
    positions = ctx_rank * rows + jnp.arange(rows, dtype=jnp.int32)
    cosine, sine = rotation_tables(positions)
    scale = HD ** (-0.5)
    gain_q = gain_query.astype(f32)
    gain_k = gain_key.astype(f32)
    gain_a = gain_attn.astype(f32)
    gain_m = gain_mlp.astype(f32)
    xy = ("fsdp", "ctx")

    def gather(w):
        return lax.all_gather(w, xy, axis=0, tiled=True)

    w_qkv = gather(jnp.concatenate([w_query, w_key, w_value], axis=1))
    w_out_t = gather(w_output.T)
    w_g = gather(w_gate)
    w_u = gather(w_up)
    w_down_t = gather(w_down.T)

    def rms(a):
        return lax.rsqrt(jnp.mean(a * a, axis=-1, keepdims=True) + norm_eps)

    blocks = range(ctx)
    key_pos = jnp.arange(rows, dtype=jnp.int32)
    causal = key_pos[None, :] <= key_pos[:, None]

    def allowed(j):
        return causal if j == 0 else jnp.broadcast_to(ctx_rank >= j, causal.shape)

    def split_heads(a):
        return a.reshape(rows, heads, HD)

    def attend(x):
        qkv = dot(x, w_qkv, ((1,), (0,)))
        queries, key_raw = qkv[:, :local], qkv[:, local : 2 * local]
        value_low = qkv[:, 2 * local :].astype(bf16)
        squares = jnp.stack([jnp.sum(queries * queries, axis=-1), jnp.sum(key_raw * key_raw, axis=-1)])
        squares = small_sum(squares, "tp")
        rq = lax.rsqrt(squares[0] / width + norm_eps)[:, None]
        rk = lax.rsqrt(squares[1] / width + norm_eps)[:, None]
        q_low = rotate(split_heads(queries * rq * gain_q), cosine, sine).astype(bf16)
        k_low = rotate(split_heads(key_raw * rk * gain_k), cosine, sine).astype(bf16)
        keys, values = [k_low], [split_heads(value_low)]
        for j in blocks[1:]:
            pairs = [(a, a + j) for a in range(ctx - j)]
            keys.append(lax.ppermute(k_low.reshape(rows, local), "ctx", pairs).reshape(k_low.shape))
            values.append(lax.ppermute(value_low, "ctx", pairs).reshape(k_low.shape))
        scores = [
            jnp.where(
                allowed(j)[None],
                jnp.einsum("qhd,khd->hqk", q_low, keys[j], preferred_element_type=f32) * scale,
                masked_value,
            )
            for j in blocks
        ]
        top = scores[0].max(-1, keepdims=True)
        for j in blocks[1:]:
            top = jnp.maximum(top, scores[j].max(-1, keepdims=True))
        exps = [jnp.exp(a - top) for a in scores]
        total = sum(a.sum(-1, keepdims=True) for a in exps)
        exps = [a.astype(bf16) for a in exps]
        weighted = sum(
            jnp.einsum("hqk,khd->qhd", exps[j], values[j], preferred_element_type=f32) for j in blocks
        )
        inverse = 1.0 / total
        head_out = weighted * jnp.transpose(inverse, (1, 0, 2))
        head_low = head_out.reshape(rows, local).astype(bf16)
        return head_low, (queries, key_raw, rq, rk, q_low, keys, values, exps, inverse, head_out)

    def attend_back(kept, grad_heads):
        queries, key_raw, rq, rk, q_low, keys, values, exps, inverse, head_out = kept
        delta = jnp.sum(split_heads(grad_heads.astype(f32)) * head_out, axis=-1)
        delta = jnp.transpose(delta)[:, :, None]
        heads_grad = split_heads(grad_heads)
        scaled_grad = (heads_grad.astype(f32) * jnp.transpose(inverse, (1, 0, 2))).astype(bf16)
        grad_q_rot = 0.0
        key_terms, value_terms = [], []
        for j in blocks:
            grad_probs = jnp.einsum("qhd,khd->hqk", heads_grad, values[j], preferred_element_type=f32)
            grad_scores = (exps[j].astype(f32) * inverse * (grad_probs - delta)).astype(bf16)
            grad_q_rot = grad_q_rot + jnp.einsum(
                "hqk,khd->qhd", grad_scores, keys[j], preferred_element_type=f32
            )
            key_terms.append(
                jnp.einsum("hqk,qhd->khd", grad_scores, q_low, preferred_element_type=f32) * scale
            )
            value_terms.append(
                jnp.einsum("hqk,qhd->khd", exps[j], scaled_grad, preferred_element_type=f32)
            )
        grad_q_rot = grad_q_rot * scale
        grad_k_rot, grad_values = key_terms[0], value_terms[0]
        for j in blocks[1:]:
            pairs = [(a, a - j) for a in range(j, ctx)]
            back_k = lax.ppermute(key_terms[j].reshape(rows, local).astype(bf16), "ctx", pairs)
            back_v = lax.ppermute(value_terms[j].reshape(rows, local).astype(bf16), "ctx", pairs)
            grad_k_rot = grad_k_rot + split_heads(back_k).astype(f32)
            grad_values = grad_values + split_heads(back_v).astype(f32)
        value_grad = grad_values.reshape(rows, local).astype(bf16)
        grad_qn = rotate(grad_q_rot, cosine, -sine).reshape(rows, local)
        grad_kn = rotate(grad_k_rot, cosine, -sine).reshape(rows, local)
        inner = jnp.stack(
            [
                jnp.sum(grad_qn * queries * gain_q, axis=-1),
                jnp.sum(grad_kn * key_raw * gain_k, axis=-1),
            ]
        )
        inner = small_sum(inner, "tp") / width
        grad_queries = (grad_qn * rq * gain_q - queries * rq**3 * inner[0][:, None]).astype(bf16)
        grad_keys = (grad_kn * rk * gain_k - key_raw * rk**3 * inner[1][:, None]).astype(bf16)
        gain_q_term = jnp.sum(grad_qn * queries * rq, axis=0)
        gain_k_term = jnp.sum(grad_kn * key_raw * rk, axis=0)
        return jnp.concatenate([grad_queries, grad_keys, value_grad], axis=1), gain_q_term, gain_k_term

    flat = (micro_count * rows, width)
    x_all, grad_all = tokens.reshape(flat), cotangent.reshape(flat)

    def own(a):
        a = a.reshape(flat[0] // (tp * PIECE), tp, PIECE, width)
        return lax.dynamic_index_in_dim(a, tp_rank, 1, keepdims=False).reshape(flat[0] // tp, width)

    attended = [attend(tokens[m]) for m in range(micro_count)]
    head_low = jnp.concatenate([a[0] for a in attended], axis=0)
    attention, mlp_in = attn_out(head_low, w_out_t, x_all, gain_a[None], tp)
    down, down_low, hidden, gate_low, up_low, attn_low, mixed_own, gain_m_sum, gain_a_sum = mlp(
        mlp_in, grad_all, own(attention), gain_m[None], gain_a[None], w_g, w_u, w_down_t, tp
    )
    att, down = attention.astype(f32), down.astype(f32)
    out = (x_all.astype(f32) + att * rms(att) * gain_a + down * rms(down) * gain_m).astype(bf16)

    def weight_grad(left, right):
        full = dot(left, right, ((0,), (0,)), bf16)
        return lax.psum_scatter(full, xy, scatter_dimension=0, tiled=True).astype(f32)

    d_down = weight_grad(down_low, hidden).T
    d_gate = weight_grad(mlp_in, gate_low)
    d_up = weight_grad(mlp_in, up_low)
    d_out = weight_grad(attn_low, head_low).T
    grad_heads = dot(attn_low, w_out_t, ((1,), (0,)), bf16)
    back = [
        attend_back(attended[m][1], grad_heads[m * rows : (m + 1) * rows]) for m in range(micro_count)
    ]
    grad_qkv = jnp.concatenate([b[0] for b in back], axis=0)
    d_qkv = weight_grad(x_all, grad_qkv)
    grad_tokens = input_grad(grad_qkv, w_qkv, mixed_own, tp)
    gain_a_total = lax.psum(jnp.sum(gain_a_sum, axis=0), xy + ("tp",))
    gain_q_total, gain_k_total, gain_m_total = lax.psum(
        (sum(b[1] for b in back), sum(b[2] for b in back), jnp.sum(gain_m_sum, axis=0)), xy
    )
    return (
        out.reshape(tokens.shape),
        grad_tokens.reshape(tokens.shape),
        d_qkv[:, :local], d_qkv[:, local : 2 * local], d_qkv[:, 2 * local :],
        d_out, d_gate, d_up, d_down,
        gain_q_total, gain_k_total, gain_a_total, gain_m_total,
    )


def solution(mesh):
    rows, cols = P(("fsdp", "ctx"), "tp"), P("tp", ("fsdp", "ctx"))
    acts = P("fsdp", "ctx", None)
    in_specs = (acts, rows, rows, rows, cols, rows, rows, cols, P("tp"), P("tp"), P(), P(), acts)
    out_specs = (acts, acts, rows, rows, rows, cols, rows, rows, cols, P("tp"), P("tp"), P(), P())
    return jax.shard_map(
        per_device, mesh=mesh, in_specs=in_specs, out_specs=out_specs, check_vma=False
    )
```

```python
import functools

import jax
import jax.numpy as jnp
from jax import lax
from jax.experimental import pallas as pl
from jax.experimental.pallas import tpu as pltpu
from jax.sharding import PartitionSpec as P

HD = 128
norm_eps = 1e-06
rope_theta = 500000.0
masked_value = -1e30
f32 = jnp.float32
bf16 = jnp.bfloat16


def dot(a, b, dims, out=f32):
    return lax.dot_general(a, b, (dims, ((), ())), preferred_element_type=f32).astype(out)


PIECE = 16
LAG = 1
CHUNK = 256
TILE_ROWS = 256
TILES_PER_TICK = 3


class Line:
    def __init__(self, axis, n, groups, buf, total, send, recv):
        self.axis, self.n, self.groups = axis, n, groups
        self.buf, self.total, self.send, self.recv = buf, total, send, recv
        self.i = lax.axis_index(axis)
        self.stages = 2 * n - 1

    def rows(self, group, c, count=1):
        return pl.ds(pl.multiple_of((group * self.n + c) * PIECE, PIECE), count * PIECE)

    def copy(self, way, step, group, c, source):
        rows = self.rows(group, c)
        return pltpu.make_async_remote_copy(
            src_ref=self.buf.at[source, rows],
            dst_ref=self.buf.at[0 if way == 0 else 2, rows],
            send_sem=self.send.at[way, step, group],
            recv_sem=self.recv.at[way, step, group],
            device_id={self.axis: self.i + (1 if way == 0 else -1)},
            device_id_type=pl.DeviceIdType.MESH,
        )

    def add(self, c, group, source):
        rows = self.rows(group, c)
        both = self.buf[1, rows].astype(f32) + self.buf[source, rows].astype(f32)
        self.buf[1, rows] = both.astype(bf16)

    def reduce_step(self, s, group):
        i, n = self.i, self.n

        @pl.when(i <= min(s - 1, n - 2))
        def _():
            c = n - s + i
            if s >= 2:

                @pl.when(i >= 1)
                def _():
                    self.copy(0, s - 2, group, c, 1).wait_recv()
                    self.add(c, group, 0)

            self.copy(0, s - 1, group, c, 1).start()

        @pl.when(i >= max(n - s, 1))
        def _():
            c = s + i - n
            if s >= 2:

                @pl.when(i <= n - 2)
                def _():
                    self.copy(1, s - 2, group, c, 1).wait_recv()
                    self.add(c, group, 2)

            self.copy(1, s - 1, group, c, 1).start()

    def finish(self, group, then):
        i, n = self.i, self.n
        rows = self.rows(group, i)
        self.total[...] = self.buf[1, rows].astype(f32)

        @pl.when(i >= 1)
        def _():
            self.copy(0, n - 2, group, i, 1).wait_recv()
            self.total[...] += self.buf[0, rows].astype(f32)

        @pl.when(i <= n - 2)
        def _():
            self.copy(1, n - 2, group, i, 1).wait_recv()
            self.total[...] += self.buf[2, rows].astype(f32)

        self.buf[1, rows] = then(group, self.total[...]).astype(bf16)

        @pl.when(i <= n - 2)
        def _():
            self.copy(0, n - 1, group, i, 1).start()

        @pl.when(i >= 1)
        def _():
            self.copy(1, n - 1, group, i, 1).start()

    def gather_step(self, s, group):
        i, n = self.i, self.n

        @pl.when(i >= s - 1)
        def _():
            c = i - s + 1
            self.copy(0, n + s - 3, group, c, 0).wait_recv()
            if s <= n - 1:

                @pl.when(i <= n - 2)
                def _():
                    self.copy(0, n + s - 2, group, c, 0).start()

        @pl.when(i <= n - s)
        def _():
            c = i + s - 1
            self.copy(1, n + s - 3, group, c, 2).wait_recv()
            if s <= n - 1:

                @pl.when(i >= 1)
                def _():
                    self.copy(1, n + s - 2, group, c, 2).start()

    def sent(self, group):
        i, n = self.i, self.n
        for s in range(1, n):

            @pl.when(i <= min(s - 1, n - 2))
            def _():
                self.copy(0, s - 1, group, n - s + i, 1).wait_send()

            @pl.when(i >= max(n - s, 1))
            def _():
                self.copy(1, s - 1, group, s + i - n, 1).wait_send()

            @pl.when((i >= s - 1) & (i <= n - 2))
            def _():
                self.copy(0, n + s - 2, group, i - s + 1, 1 if s == 1 else 0).wait_send()

            @pl.when((i <= n - s) & (i >= 1))
            def _():
                self.copy(1, n + s - 2, group, i + s - 1, 1 if s == 1 else 2).wait_send()

    def piece(self, group, c):
        slot = jnp.where(c < self.i, 0, jnp.where(c > self.i, 2, 1))
        return self.buf[slot, self.rows(group, c)]

    def piece_ref(self, group, c):
        slot = jnp.where(c < self.i, 0, jnp.where(c > self.i, 2, 1))
        return self.buf.at[slot, self.rows(group, c)]

    def tick(self, t, then, done):
        n = self.n

        def stage(index, body):
            group = t - index * LAG

            @pl.when((group >= 0) & (group < self.groups))
            def _():
                body(group)

        for s in range(1, n):
            stage(s - 1, functools.partial(self.reduce_step, s))
        stage(n - 1, lambda group: self.finish(group, then))
        for s in range(2, n):
            stage(n + s - 2, functools.partial(self.gather_step, s))

        def last(group):
            self.gather_step(n, group)
            self.sent(group)
            done(group)

        stage(2 * n - 2, last)

    def ticks(self):
        return self.groups + (2 * self.n - 2) * LAG


def greet(axis, n, others=()):
    i = lax.axis_index(axis)
    barrier = pltpu.get_barrier_semaphore()
    for peer in others:
        pl.semaphore_signal(barrier, inc=1, device_id=peer, device_id_type=pl.DeviceIdType.MESH)

    @pl.when(i >= 1)
    def _():
        pl.semaphore_signal(barrier, inc=1, device_id={axis: i - 1}, device_id_type=pl.DeviceIdType.MESH)

    @pl.when(i <= n - 2)
    def _():
        pl.semaphore_signal(barrier, inc=1, device_id={axis: i + 1}, device_id_type=pl.DeviceIdType.MESH)

    pl.semaphore_wait(barrier, len(others) + jnp.minimum(i, 1) + jnp.minimum(n - 1 - i, 1))


def line_scratch(n, rows, width):
    sems = pltpu.SemaphoreType.DMA((2, 2 * n - 2, rows // (n * PIECE)))
    return [pltpu.VMEM((3, rows, width), bf16), pltpu.VMEM((PIECE, width), f32), sems, sems]


def params(collective_id):
    return pltpu.CompilerParams(
        collective_id=collective_id, has_side_effects=True, vmem_limit_bytes=63 << 20
    )


def scale_of(a):
    return lax.rsqrt(jnp.mean(a * a, axis=-1, keepdims=True) + norm_eps)


def attn_out_kernel(n, head, w_out_t, x, gain, attention, mlp_in, buf, total, send, recv):
    rows, width = x.shape
    groups = rows // (n * PIECE)
    line = Line("tp", n, groups, buf, total, send, recv)
    greet("tp", n)
    per_chunk = CHUNK // (n * PIECE)
    tile = 512

    def done(group):
        for c in range(n):
            at = line.rows(group, c)
            low = line.piece(group, c)
            attention[at] = low
            a = low.astype(f32)
            mlp_in[at] = (x[at].astype(f32) + a * scale_of(a) * gain[...]).astype(bf16)

    @pl.loop(0, line.ticks())
    def _(t):
        @pl.when((t < groups) & (lax.rem(t, per_chunk) == 0))
        def _():
            at = pl.ds(pl.multiple_of(t * n * PIECE, CHUNK), CHUNK)

            @pl.loop(0, width // tile)
            def _(j):
                cols = pl.ds(pl.multiple_of(j * tile, tile), tile)
                buf[1, at, cols] = dot(head[at], w_out_t[cols], ((1,), (1,)), bf16)

        line.tick(t, lambda group, total: total, done)


def attn_out(head, w_out_t, x, gain, n):
    rows, width = x.shape
    vmem = pl.BlockSpec(memory_space=pltpu.VMEM)
    return pl.pallas_call(
        functools.partial(attn_out_kernel, n),
        out_shape=[jax.ShapeDtypeStruct(x.shape, bf16)] * 2,
        in_specs=[vmem] * 4,
        out_specs=[vmem] * 2,
        scratch_shapes=line_scratch(n, rows, width),
        compiler_params=params(1),
        cost_estimate=pl.CostEstimate(flops=100 * 10**9, bytes_accessed=20 << 20, transcendentals=0),
        name="attn_out",
    )(head, w_out_t, x, gain)


def local_copies(pairs, sems):
    copies = [pltpu.make_async_copy(a, b, sems.at[k]) for k, (a, b) in enumerate(pairs)]
    for copy in copies:
        copy.start()
    return copies


def mlp_kernel(
    n, mlp_in, grad, attn_own, gain_m, gain_a, w_g_hbm, w_u_hbm, w_d_hbm,
    down_out, hidden_out, attn_low_out, weights_out, mixed_own, gain_m_sum, gain_a_sum,
    buf, total, send, recv, w_g, w_u, w_d, mlp_rows, hidden, down_low, gate, up, tiles,
    ready, w_sems, io_sems, piece_sems, tile_sems,
):
    rows, width = grad.shape
    units = w_g.shape[1]
    groups = rows // (n * PIECE)
    per_chunk = CHUNK // (n * PIECE)
    line = Line("tp", n, groups, buf, total, send, recv)
    i = line.i
    weights = local_copies([(w_g_hbm, w_g), (w_u_hbm, w_u), (w_d_hbm, w_d)], w_sems)
    gain_m_sum[...] = jnp.zeros_like(gain_m_sum)
    gain_a_sum[...] = jnp.zeros_like(gain_a_sum)
    greet("tp", n)
    offset = per_chunk + line.stages - 1
    tile = 512

    def chunk_rows(chunk):
        return pl.ds(pl.multiple_of(chunk * CHUNK, CHUNK), CHUNK)

    def hidden_copy(chunk):
        return pltpu.make_async_copy(hidden, hidden_out.at[chunk_rows(chunk)], io_sems.at[1])

    def forward(chunk, first):
        at = chunk_rows(chunk)
        fetch = pltpu.make_async_copy(mlp_in.at[at], mlp_rows, io_sems.at[0])
        fetch.start()
        if first:
            weights[0].wait()
            weights[1].wait()
        else:
            hidden_copy(chunk - 1).wait()
        fetch.wait()

        @pl.loop(0, units // tile)
        def _(j):
            cols = pl.ds(pl.multiple_of(j * tile, tile), tile)
            gate_proj = dot(mlp_rows[...], w_g[:, cols], ((1,), (0,)))
            up_proj = dot(mlp_rows[...], w_u[:, cols], ((1,), (0,)))
            gate[at, cols] = gate_proj.astype(bf16)
            up[at, cols] = up_proj.astype(bf16)
            hidden[:, cols] = (gate_proj / (1.0 + jnp.exp(-gate_proj)) * up_proj).astype(bf16)

        hidden_copy(chunk).start()
        if first:
            weights[2].wait()

        @pl.loop(0, width // tile)
        def _(j):
            cols = pl.ds(pl.multiple_of(j * tile, tile), tile)
            buf[1, at, cols] = dot(hidden[...], w_d[cols], ((1,), (1,)), bf16)

    def backward(chunk):
        at = chunk_rows(chunk)

        @pl.loop(0, units // tile)
        def _(j):
            cols = pl.ds(pl.multiple_of(j * tile, tile), tile)
            gate_proj, up_proj = gate[at, cols].astype(f32), up[at, cols].astype(f32)
            sig = 1.0 / (1.0 + jnp.exp(-gate_proj))
            grad_hidden = dot(down_low[at], w_d[:, cols], ((1,), (0,)))
            up[at, cols] = (grad_hidden * gate_proj * sig).astype(bf16)
            gate[at, cols] = (grad_hidden * up_proj * sig * (1.0 + gate_proj * (1.0 - sig))).astype(bf16)

        @pl.loop(0, width // tile)
        def _(j):
            cols = pl.ds(pl.multiple_of(j * tile, tile), tile)
            buf[1, at, cols] = (
                dot(gate[at], w_g[cols], ((1,), (1,))) + dot(up[at], w_u[cols], ((1,), (1,)))
            ).astype(bf16)

    whole = pl.ds(0, rows)
    late_in = [(hidden_out, w_g.at[whole]), (mlp_in, w_u.at[whole])]
    per_part = width // TILE_ROWS

    def tile_copy(k, slot):
        part, block = lax.div(k, per_part), lax.rem(k, per_part)
        return pltpu.make_async_copy(
            tiles.at[slot],
            weights_out.at[
                pl.ds(pl.multiple_of(block * TILE_ROWS, TILE_ROWS), TILE_ROWS),
                pl.ds(pl.multiple_of(part * units, units), units),
            ],
            tile_sems.at[slot],
        )

    def weight_tile(k):
        slot = lax.rem(k, 2)
        block = pl.ds(pl.multiple_of(lax.rem(k, per_part) * TILE_ROWS, TILE_ROWS), TILE_ROWS)

        @pl.when(k >= 2)
        def _():
            tile_copy(k - 2, slot).wait()

        def fill(left, right):
            @pl.loop(0, units // tile)
            def _(j):
                cols = pl.ds(pl.multiple_of(j * tile, tile), tile)
                tiles[slot, :, cols] = dot(left[whole, block], right[whole, cols], ((0,), (0,)), bf16)

        @pl.when(k < per_part)
        def _():
            fill(down_low, w_g)

        @pl.when((k >= per_part) & (k < 2 * per_part))
        def _():
            fill(w_u, gate)

        @pl.when(k >= 2 * per_part)
        def _():
            fill(w_u, up)

        tile_copy(k, slot).start()

    def pieces_out(group, out):
        return local_copies([(line.piece_ref(group, c), out.at[line.rows(group, c)]) for c in range(n)], piece_sems)

    def down_done(group):
        copies = pieces_out(group, down_out)
        for c in range(n):
            at = line.rows(group, c)
            branch = line.piece(group, c).astype(f32)
            r = scale_of(branch)
            g = grad[at].astype(f32)
            scaled = g * gain_m[...]
            inner = jnp.mean(scaled * branch, axis=-1, keepdims=True)
            gain_m_sum[...] += g * branch * r
            down_low[at] = (r * scaled - branch * (r * r * r) * inner).astype(bf16)
        for copy in copies:
            copy.wait()

    def attn_grad(group, total):
        at = pl.ds(pl.multiple_of(group * PIECE, PIECE), PIECE)
        mixed = grad[line.rows(group, i)].astype(f32) + total
        mixed_own[at] = mixed
        branch = attn_own[at].astype(f32)
        r = scale_of(branch)
        scaled = mixed * gain_a[...]
        inner = jnp.mean(scaled * branch, axis=-1, keepdims=True)
        gain_a_sum[...] += mixed * branch * r
        return r * scaled - branch * (r * r * r) * inner

    def attn_done(group):
        for copy in pieces_out(group, attn_low_out):
            copy.wait()

    forward(0, True)

    @pl.loop(0, offset + line.ticks())
    def _(t):
        back = t - offset

        @pl.when((back >= 0) & (back < groups) & (lax.rem(back + groups, per_chunk) == 0))
        def _():
            @pl.when(i >= 1)
            def _():
                pl.semaphore_wait(ready.at[0], 1)

            @pl.when(i <= n - 2)
            def _():
                pl.semaphore_wait(ready.at[1], 1)

        line.tick(back, attn_grad, attn_done)
        line.tick(t, lambda group, total: total, down_done)
        after = t + 1

        @pl.when((after < groups) & (lax.rem(after, per_chunk) == 0))
        def _():
            forward(lax.div(after, per_chunk), False)

        next_back = after - offset

        @pl.when((next_back >= 0) & (next_back < groups) & (lax.rem(next_back + groups, per_chunk) == 0))
        def _():
            @pl.when(i >= 1)
            def _():
                pl.semaphore_signal(
                    ready.at[1], inc=1, device_id={"tp": i - 1}, device_id_type=pl.DeviceIdType.MESH
                )

            @pl.when(i <= n - 2)
            def _():
                pl.semaphore_signal(
                    ready.at[0], inc=1, device_id={"tp": i + 1}, device_id_type=pl.DeviceIdType.MESH
                )

            backward(lax.div(next_back, per_chunk))

        first_tick = offset + groups - per_chunk

        @pl.when(after == first_tick)
        def _():
            hidden_copy(rows // CHUNK - 1).wait()
            local_copies(late_in, w_sems)

        @pl.when(t == first_tick)
        def _():
            for k, (source, target) in enumerate(late_in):
                pltpu.make_async_copy(source, target, w_sems.at[k]).wait()

        for m in range(TILES_PER_TICK):
            k = (t - first_tick) * TILES_PER_TICK + m

            @pl.when((k >= 0) & (k < 3 * per_part))
            def _():
                weight_tile(k)

    for k in (3 * per_part - 2, 3 * per_part - 1):
        tile_copy(k, k % 2).wait()


def mlp(mlp_in, grad, attn_own, gain_m, gain_a, w_g, w_u, w_d, n):
    rows, width = grad.shape
    units = w_g.shape[1]
    vmem, anywhere = pl.BlockSpec(memory_space=pltpu.VMEM), pl.BlockSpec(memory_space=pl.ANY)
    acts = jax.ShapeDtypeStruct((rows, width), bf16)
    inner = jax.ShapeDtypeStruct((rows, units), bf16)
    per_piece = jax.ShapeDtypeStruct((PIECE, width), f32)
    return pl.pallas_call(
        functools.partial(mlp_kernel, n),
        out_shape=[
            acts, inner, acts, jax.ShapeDtypeStruct((width, 3 * units), bf16),
            jax.ShapeDtypeStruct((rows // n, width), f32), per_piece, per_piece,
        ],
        in_specs=[anywhere] + [vmem] * 4 + [anywhere] * 3,
        out_specs=[anywhere] * 4 + [vmem] * 3,
        scratch_shapes=line_scratch(n, rows, width) + [
            pltpu.VMEM(w_g.shape, bf16), pltpu.VMEM(w_u.shape, bf16), pltpu.VMEM(w_d.shape, bf16),
            pltpu.VMEM((CHUNK, width), bf16), pltpu.VMEM((CHUNK, units), bf16), pltpu.VMEM((rows, width), bf16),
            pltpu.VMEM((rows, units), bf16), pltpu.VMEM((rows, units), bf16),
            pltpu.VMEM((2, TILE_ROWS, units), bf16),
            pltpu.SemaphoreType.REGULAR((2,)),
            pltpu.SemaphoreType.DMA((3,)), pltpu.SemaphoreType.DMA((2,)), pltpu.SemaphoreType.DMA((n,)),
            pltpu.SemaphoreType.DMA((2,)),
        ],
        compiler_params=params(2),
        cost_estimate=pl.CostEstimate(flops=200 * 10**9, bytes_accessed=60 << 20, transcendentals=0),
        name="mlp",
    )(mlp_in, grad, attn_own, gain_m, gain_a, w_g, w_u, w_d)


class Owners:
    def __init__(self, n_xy, full, pair_in, peer_in, result, pair_sems, peer_sems):
        n_fsdp, self.n_ctx = n_xy
        self.chips = n_fsdp // 2
        self.full, self.pair_in, self.peer_in, self.result = full, pair_in, peer_in, result
        self.pair_sems, self.peer_sems = pair_sems, peer_sems
        fsdp = lax.axis_index("fsdp")
        self.core = lax.rem(fsdp, 2)
        self.ctx = lax.axis_index("ctx")
        self.place = lax.div(fsdp, 2) * self.n_ctx + self.ctx
        self.block = full.shape[0] // (n_fsdp * self.n_ctx)

    def pair_copy(self, chip):
        there = 1 - self.core
        span = self.n_ctx * self.block
        rows = pl.ds(pl.multiple_of((2 * chip + there) * span, span), span)
        return pltpu.make_async_remote_copy(
            src_ref=self.full.at[rows], dst_ref=self.pair_in.at[pl.ds(chip * span, span)],
            send_sem=self.pair_sems.at[0, chip], recv_sem=self.pair_sems.at[1, chip],
            device_id={"fsdp": 2 * lax.div(lax.axis_index("fsdp"), 2) + there}, device_id_type=pl.DeviceIdType.MESH,
        )

    def peer_copy(self, k):
        place = lax.rem(self.place + k, self.chips * self.n_ctx)
        return pltpu.make_async_remote_copy(
            src_ref=self.pair_in.at[self.block_rows(place)], dst_ref=self.peer_in.at[k - 1],
            send_sem=self.peer_sems.at[0, k - 1], recv_sem=self.peer_sems.at[1, k - 1],
            device_id={"fsdp": 2 * lax.div(place, self.n_ctx) + self.core, "ctx": lax.rem(place, self.n_ctx)},
            device_id_type=pl.DeviceIdType.MESH,
        )

    def block_rows(self, place):
        return pl.ds(pl.multiple_of(place * self.block, self.block), self.block)

    def start(self):
        for chip in range(self.chips):
            self.pair_copy(chip).start()

    def pass_on(self):
        span = self.n_ctx * self.block
        for chip in range(self.chips):
            self.pair_copy(chip).wait_recv()
            rows = pl.ds(chip * span, span)
            mine = pl.ds(pl.multiple_of((2 * chip + self.core) * span, span), span)
            self.pair_in[rows] = (self.pair_in[rows].astype(f32) + self.full[mine].astype(f32)).astype(bf16)
        for k in range(1, self.chips * self.n_ctx):
            self.peer_copy(k).start()

    def end(self):
        self.result[...] = self.pair_in[self.block_rows(self.place)].astype(f32)
        for k in range(1, self.chips * self.n_ctx):
            self.peer_copy(k).wait()
            self.result[...] += self.peer_in[k - 1].astype(f32)
        for chip in range(self.chips):
            self.pair_copy(chip).wait_send()


def owners_scratch(n_xy, shape):
    n_fsdp, n_ctx = n_xy
    peers = n_fsdp // 2 * n_ctx - 1
    block = shape[0] // (n_fsdp * n_ctx)
    return [
        pltpu.VMEM((shape[0] // 2, shape[1]), bf16), pltpu.VMEM((peers, block, shape[1]), bf16),
        pltpu.SemaphoreType.DMA((2, n_fsdp // 2)), pltpu.SemaphoreType.DMA((2, peers)),
    ]


def input_grad_kernel(
    n, n_xy, grad_qkv, w_qkv_hbm, mixed_own, gains, weights, grad_out, gains_sum, weights_own,
    buf, total, send, recv, w_qkv, w_sem, piece_sems, gains_theirs, gain_send, gain_recv,
    pair_in, peer_in, pair_sems, peer_sems,
):
    rows, width = buf.shape[1:]
    groups = rows // (n * PIECE)
    per_chunk = CHUNK // (n * PIECE)
    line = Line("tp", n, groups, buf, total, send, recv)
    fetch = pltpu.make_async_copy(w_qkv_hbm, w_qkv, w_sem)
    fetch.start()
    n_fsdp, n_ctx = n_xy
    place = lax.axis_index("fsdp") * n_ctx + lax.axis_index("ctx")
    others = []
    for k in range(1, n_fsdp * n_ctx):
        peer = lax.rem(place + k, n_fsdp * n_ctx)
        others.append({"fsdp": lax.div(peer, n_ctx), "ctx": lax.rem(peer, n_ctx)})
    greet("tp", n, others)
    gain_copies = [
        pltpu.make_async_remote_copy(
            src_ref=gains, dst_ref=gains_theirs.at[k], send_sem=gain_send.at[k], recv_sem=gain_recv.at[k],
            device_id=peer, device_id_type=pl.DeviceIdType.MESH,
        )
        for k, peer in enumerate(others)
    ]
    for copy in gain_copies:
        copy.start()
    owners = Owners(n_xy, weights, pair_in, peer_in, weights_own, pair_sems, peer_sems)
    owners.start()
    fetch.wait()
    tile = 512

    def own(group, total):
        return total + mixed_own[pl.ds(pl.multiple_of(group * PIECE, PIECE), PIECE)]

    def done(group):
        copies = local_copies(
            [(line.piece_ref(group, c), grad_out.at[line.rows(group, c)]) for c in range(n)], piece_sems
        )
        for copy in copies:
            copy.wait()

    @pl.loop(0, line.ticks())
    def _(t):
        @pl.when((t < groups) & (lax.rem(t, per_chunk) == 0))
        def _():
            at = pl.ds(pl.multiple_of(t * n * PIECE, CHUNK), CHUNK)

            @pl.loop(0, width // tile)
            def _(j):
                cols = pl.ds(pl.multiple_of(j * tile, tile), tile)
                buf[1, at, cols] = dot(grad_qkv[at], w_qkv[cols], ((1,), (1,)), bf16)

        line.tick(t, own, done)

        @pl.when(t == 2)
        def _():
            owners.pass_on()

    owners.end()
    gains_sum[...] = gains[...]
    for k, copy in enumerate(gain_copies):
        copy.wait()
        gains_sum[...] += gains_theirs[k]


def input_grad(grad_qkv, w_qkv, mixed_own, gains, weights, n, n_xy):
    rows, width = grad_qkv.shape[0], w_qkv.shape[0]
    peers = n_xy[0] * n_xy[1] - 1
    vmem, anywhere = pl.BlockSpec(memory_space=pltpu.VMEM), pl.BlockSpec(memory_space=pl.ANY)
    return pl.pallas_call(
        functools.partial(input_grad_kernel, n, n_xy),
        out_shape=[
            jax.ShapeDtypeStruct((rows, width), bf16), jax.ShapeDtypeStruct(gains.shape, f32),
            jax.ShapeDtypeStruct((weights.shape[0] // (n_xy[0] * n_xy[1]), weights.shape[1]), f32),
        ],
        in_specs=[vmem, anywhere, vmem, vmem, vmem],
        out_specs=[anywhere, vmem, vmem],
        scratch_shapes=line_scratch(n, rows, width) + [
            pltpu.VMEM(w_qkv.shape, bf16), pltpu.SemaphoreType.DMA, pltpu.SemaphoreType.DMA((n,)),
            pltpu.VMEM((peers,) + gains.shape, f32), pltpu.SemaphoreType.DMA((peers,)), pltpu.SemaphoreType.DMA((peers,)),
        ] + owners_scratch(n_xy, weights.shape),
        compiler_params=params(3),
        cost_estimate=pl.CostEstimate(flops=100 * 10**9, bytes_accessed=20 << 20, transcendentals=0),
        name="input_grad",
    )(grad_qkv, w_qkv, mixed_own, gains, weights)


def peers_of(axis, n):
    i = lax.axis_index(axis)
    return [(k - 1, lax.rem(i + k, n)) for k in range(1, n)]


def meet(axes):
    barrier = pltpu.get_barrier_semaphore()
    count = 0
    for axis, n in axes:
        for _, peer in peers_of(axis, n):
            pl.semaphore_signal(barrier, inc=1, device_id={axis: peer}, device_id_type=pl.DeviceIdType.MESH)
            count += 1
    pl.semaphore_wait(barrier, count)


def swap(axis, n, pairs, send, recv):
    copies = []
    for k, (mine, theirs) in enumerate(pairs):
        for slot, peer in peers_of(axis, n):
            copy = pltpu.make_async_remote_copy(
                src_ref=mine, dst_ref=theirs.at[slot],
                send_sem=send.at[k, slot], recv_sem=recv.at[k, slot],
                device_id={axis: peer}, device_id_type=pl.DeviceIdType.MESH,
            )
            copy.start()
            copies.append(copy)
    for copy in copies:
        copy.wait()


def lanes_to_rows(columns):
    return jnp.transpose(columns)[:8]


def rows_to_lanes(packed):
    rows = packed.shape[1]
    return jnp.transpose(jnp.concatenate([packed, jnp.zeros((120, rows), f32)], axis=0))


def two_lanes(first, second):
    lane = lax.broadcasted_iota(jnp.int32, (first.shape[0], 128), 1)
    return jnp.where(lane == 0, first, jnp.where(lane == 1, second, 0.0))


def turn(values, cosine, sine):
    return values * cosine + pltpu.roll(values, HD // 2, 1) * sine


def heads_loop(heads, body):
    @pl.loop(0, heads)
    def _(h):
        body(h, lambda part, width: pl.ds(pl.multiple_of(part * width + h * HD, HD), HD))


def attend_kernel(
    n_tp, n_ctx, seqs, x, w_qkv, gain_q, gain_k, cosine, sine,
    raw, low, prev, head_low, head_out, stats,
    sums, theirs, kv_send, kv_recv, sum_send, sum_recv,
):
    rows_all, width = x.shape
    rows = rows_all // seqs
    local = w_qkv.shape[1] // 3
    heads = local // HD
    me = lax.axis_index("ctx")
    scale = HD ** (-0.5)
    meet([("tp", n_tp), ("ctx", n_ctx)])
    step = min(256, rows)

    def chunks(body):
        @pl.loop(0, rows_all // step)
        def _(k):
            body(pl.ds(pl.multiple_of(k * step, step), step), pl.ds(pl.multiple_of(lax.rem(k, rows // step) * step, step), step))

    for j in range(1, n_ctx):

        @pl.when(me < j)
        def _():
            prev[j - 1] = jnp.zeros(prev.shape[1:], bf16)

    def kv_copy(j, part, seq):
        at = pl.ds(seq * rows, rows)
        return pltpu.make_async_remote_copy(
            src_ref=low.at[at, pl.ds((1 + part) * local, local)],
            dst_ref=prev.at[j - 1, at, pl.ds(part * local, local)],
            send_sem=kv_send.at[j - 1, part, seq], recv_sem=kv_recv.at[j - 1, part, seq],
            device_id={"ctx": lax.rem(me + j, n_ctx)}, device_id_type=pl.DeviceIdType.MESH,
        )

    def kv_each(method, part, seq, here):
        for j in range(1, n_ctx):

            @pl.when((me >= j) if here else (me + j < n_ctx))
            def _():
                getattr(kv_copy(j, part, seq), method)()

    def value_chunk(at, _):
        low[at, 2 * local :] = dot(x[at], w_qkv[:, 2 * local :], ((1,), (0,)), bf16)

    chunks(value_chunk)
    for seq in range(seqs):
        kv_each("start", 1, seq, False)

    def raw_chunk(at, _):
        q = dot(x[at], w_qkv[:, :local], ((1,), (0,)))
        raw[at, :local] = q
        k = dot(x[at], w_qkv[:, local : 2 * local], ((1,), (0,)))
        raw[at, local:] = k
        both = two_lanes(jnp.sum(q * q, axis=-1, keepdims=True), jnp.sum(k * k, axis=-1, keepdims=True))
        sums[:, at] = lanes_to_rows(both)

    chunks(raw_chunk)
    swap("tp", n_tp, [(sums, theirs)], sum_send, sum_recv)
    total = sums[...]
    for slot in range(n_tp - 1):
        total = total + theirs[slot]
    stats[...] = rows_to_lanes(lax.rsqrt(total / width + norm_eps))

    def turned(part, gain):
        def chunk(at, pos):
            r = stats[at, part : part + 1]
            for h in range(heads):
                cols = pl.ds(part * local + h * HD, HD)
                v = raw[at, cols] * r * gain[:, h * HD : (h + 1) * HD]
                low[at, cols] = turn(v, cosine[pos], sine[pos]).astype(bf16)

        chunks(chunk)

    turned(1, gain_k)
    for seq in range(seqs):
        kv_each("start", 0, seq, False)
    turned(0, gain_q)
    lane = lax.broadcasted_iota(jnp.int32, (step, 128), 1)

    for seq in range(seqs):
        for part in range(2):
            kv_each("wait_recv", part, seq, True)
        seq_rows = pl.ds(seq * rows, rows)

        def one_head(h, cols, seq=seq, seq_rows=seq_rows):
            for tile in range(rows // step):
                at = pl.ds(seq * rows + tile * step, step)
                q = low[at, cols(0, local)]
                seen = (tile + 1) * step
                own = pl.ds(seq * rows, seen)
                s = dot(q, low[own, cols(1, local)], ((1,), (1,))) * scale
                i_pos = lax.broadcasted_iota(jnp.int32, (step, seen), 0) + tile * step
                j_pos = lax.broadcasted_iota(jnp.int32, (step, seen), 1)
                scores = [jnp.where(j_pos <= i_pos, s, masked_value)]
                values = [low[own, cols(2, local)]]
                for j in range(1, n_ctx):
                    s = dot(q, prev[j - 1, seq_rows, cols(0, local)], ((1,), (1,))) * scale
                    scores.append(jnp.where(me >= j, s, masked_value))
                    values.append(prev[j - 1, seq_rows, cols(1, local)])
                top = scores[0].max(-1, keepdims=True)
                for s in scores[1:]:
                    top = jnp.maximum(top, s.max(-1, keepdims=True))
                total, weighted = 0.0, 0.0
                for s, v in zip(scores, values):
                    e = jnp.exp(s - top)
                    total = total + e.sum(-1, keepdims=True)
                    weighted = weighted + dot(e.astype(bf16), v, ((1,), (0,)))
                out = weighted / total
                head_out[at, cols(0, local)] = out
                head_low[at, cols(0, local)] = out.astype(bf16)
                stats[at] = jnp.where(lane == h + 2, top + jnp.log(total), stats[at])

        heads_loop(heads, one_head)

    for seq in range(seqs):
        for part in range(2):
            kv_each("wait_send", part, seq, False)


def attend(x, w_qkv, gain_q, gain_k, cosine, sine, seqs, n_tp, n_ctx):
    rows, width = x.shape
    local = w_qkv.shape[1] // 3
    vmem = pl.BlockSpec(memory_space=pltpu.VMEM)
    shape = jax.ShapeDtypeStruct
    kv_sems = pltpu.SemaphoreType.DMA((max(n_ctx - 1, 1), 2, seqs))
    sum_sems = pltpu.SemaphoreType.DMA((1, n_tp - 1))
    return pl.pallas_call(
        functools.partial(attend_kernel, n_tp, n_ctx, seqs),
        out_shape=[
            shape((rows, 2 * local), f32), shape((rows, 3 * local), bf16),
            shape((max(n_ctx - 1, 1), rows, 2 * local), bf16),
            shape((rows, local), bf16), shape((rows, local), f32), shape((rows, 128), f32),
        ],
        in_specs=[vmem] * 6,
        out_specs=[vmem] * 6,
        scratch_shapes=[
            pltpu.VMEM((8, rows), f32), pltpu.VMEM((n_tp - 1, 8, rows), f32),
            kv_sems, kv_sems, sum_sems, sum_sems,
        ],
        compiler_params=params(4),
        cost_estimate=pl.CostEstimate(flops=50 * 10**9, bytes_accessed=30 << 20, transcendentals=0),
        name="attend",
    )(x, w_qkv, gain_q, gain_k, cosine, sine)


def attend_back_kernel(
    n_tp, n_ctx, seqs, attn_low, w_out_t, raw, low, prev, head_out, stats, x, head_low, gain_q, gain_k, cosine, sine, gain_a,
    grad_qkv, gain_qk_sum, gain_a_sum, weights_out,
    grad_heads, grad_q, grad_kv, out_kv, in_kv, sums, theirs, gain_theirs, kv_send, kv_recv, sum_send, sum_recv,
):
    rows_all, width = attn_low.shape
    rows = rows_all // seqs
    local = w_out_t.shape[1]
    heads = local // HD
    me = lax.axis_index("ctx")
    scale = HD ** (-0.5)
    meet([("tp", n_tp), ("ctx", n_ctx)])
    step = min(256, rows)

    def chunks(body):
        @pl.loop(0, rows_all // step)
        def _(k):
            body(pl.ds(pl.multiple_of(k * step, step), step), pl.ds(pl.multiple_of(lax.rem(k, rows // step) * step, step), step))

    def heads_chunk(at, _):
        grad_heads[at] = dot(attn_low[at], w_out_t[...], ((1,), (0,)), bf16)

    chunks(heads_chunk)
    grad_q[...] = jnp.zeros_like(grad_q)
    grad_kv[...] = jnp.zeros_like(grad_kv)

    def kv_copy(j, seq):
        at = pl.ds(seq * rows, rows)
        return pltpu.make_async_remote_copy(
            src_ref=out_kv.at[j - 1, at], dst_ref=in_kv.at[j - 1, at],
            send_sem=kv_send.at[j - 1, seq], recv_sem=kv_recv.at[j - 1, seq],
            device_id={"ctx": lax.rem(me + n_ctx - j, n_ctx)}, device_id_type=pl.DeviceIdType.MESH,
        )

    def lane_of(at, index):
        lane = lax.broadcasted_iota(jnp.int32, (step, 128), 1)
        return jnp.sum(jnp.where(lane == index, stats[at], 0.0), axis=-1, keepdims=True)

    def block(h, cols, at, keys, values, mask):
        q, g = low[at, cols(0, local)], grad_heads[at, cols(0, local)]
        delta = jnp.sum(g.astype(f32) * head_out[at, cols(0, local)], axis=-1, keepdims=True)
        s = dot(q, keys, ((1,), (1,))) * scale
        p = jnp.exp(s - lane_of(at, h + 2))
        if mask is not None:
            p = jnp.where(mask, p, 0.0)
        dp = dot(g, values, ((1,), (1,)))
        ds = (p * (dp - delta)).astype(bf16)
        grad_q[at, cols(0, local)] += dot(ds, keys, ((1,), (0,))) * scale
        return dot(ds, q, ((0,), (0,))) * scale, dot(p.astype(bf16), g, ((0,), (0,)))

    for j in range(1, n_ctx):

        @pl.when(me >= j)
        def _():
            for seq in range(seqs):
                seq_rows = pl.ds(seq * rows, rows)

                def one_head(h, cols):
                    keys, values = prev[j - 1, seq_rows, cols(0, local)], prev[j - 1, seq_rows, cols(1, local)]
                    dk, dv = 0.0, 0.0
                    for tile in range(rows // step):
                        at = pl.ds(seq * rows + tile * step, step)
                        k_term, v_term = block(h, cols, at, keys, values, None)
                        dk, dv = dk + k_term, dv + v_term
                    out_kv[j - 1, seq_rows, cols(0, local)] = dk.astype(bf16)
                    out_kv[j - 1, seq_rows, cols(1, local)] = dv.astype(bf16)

                heads_loop(heads, one_head)
                kv_copy(j, seq).start()

    for seq in range(seqs):

        def one_head(h, cols):
            for tile in range(rows // step):
                at = pl.ds(seq * rows + tile * step, step)
                seen = (tile + 1) * step
                own = pl.ds(seq * rows, seen)
                i_pos = lax.broadcasted_iota(jnp.int32, (step, seen), 0) + tile * step
                j_pos = lax.broadcasted_iota(jnp.int32, (step, seen), 1)
                k_term, v_term = block(
                    h, cols, at, low[own, cols(1, local)], low[own, cols(2, local)], j_pos <= i_pos
                )
                grad_kv[own, cols(0, local)] += k_term
                grad_kv[own, cols(1, local)] += v_term

        heads_loop(heads, one_head)

    def weight_rows(left, right, cols):
        @pl.loop(0, width // step)
        def _(k):
            at = pl.ds(pl.multiple_of(k * step, step), step)
            weights_out[at, cols] = dot(left[:, at], right[...], ((0,), (0,)), bf16)

    weight_rows(attn_low, head_low, pl.ds(3 * local, local))

    for j in range(1, n_ctx):
        for seq in range(seqs):

            @pl.when(me + j < n_ctx)
            def _():
                kv_copy(j, seq).wait_recv()
                at = pl.ds(seq * rows, rows)
                grad_kv[at] += in_kv[j - 1, at].astype(f32)

    def turned(at, pos, part, ref, gain):
        inner = 0.0
        for h in range(heads):
            cols = pl.ds(h * HD, HD)
            d = turn(ref[at, cols], cosine[pos], -sine[pos])
            ref[at, cols] = d
            weighted = d * raw[at, pl.ds(part * local + h * HD, HD)] * gain[:, h * HD : (h + 1) * HD]
            inner = inner + jnp.sum(weighted, axis=-1, keepdims=True)
        return inner

    def inner_chunk(at, pos):
        both = two_lanes(
            turned(at, pos, 0, grad_q, gain_q), turned(at, pos, 1, grad_kv, gain_k)
        )
        sums[:, at] = lanes_to_rows(both)

    chunks(inner_chunk)
    swap("tp", n_tp, [(sums, theirs), (gain_a, gain_theirs)], sum_send, sum_recv)
    total, gain_total = sums[...], gain_a[...]
    for slot in range(n_tp - 1):
        total = total + theirs[slot]
        gain_total = gain_total + gain_theirs[slot]
    gain_a_sum[...] = gain_total
    sums[...] = total / width
    gain_qk_sum[...] = jnp.zeros_like(gain_qk_sum)

    def out_chunk(at, _):
        inner = rows_to_lanes(sums[:, at])
        for part, ref, gain in ((0, grad_q, gain_q), (1, grad_kv, gain_k)):
            cols = pl.ds(part * local, local)
            r = stats[at, part : part + 1]
            d, v = ref[at, :local], raw[at, cols]
            grad_qkv[at, cols] = (d * r * gain[...] - v * (r * r * r) * inner[:, part : part + 1]).astype(bf16)
            gain_qk_sum[part : part + 1] += jnp.sum(d * v * r, axis=0, keepdims=True)
        grad_qkv[at, 2 * local :] = grad_kv[at, local:].astype(bf16)

    chunks(out_chunk)
    weight_rows(x, grad_qkv, pl.ds(0, 3 * local))

    for j in range(1, n_ctx):
        for seq in range(seqs):

            @pl.when(me >= j)
            def _():
                kv_copy(j, seq).wait_send()


def attend_back(
    attn_low, w_out_t, raw, low, prev, head_out, stats, x, head_low, gain_q, gain_k, cosine, sine, gain_a, seqs, n_tp, n_ctx
):
    rows, width = attn_low.shape
    local = w_out_t.shape[1]
    vmem = pl.BlockSpec(memory_space=pltpu.VMEM)
    shape = jax.ShapeDtypeStruct
    blocks = max(n_ctx - 1, 1)
    kv_sems = pltpu.SemaphoreType.DMA((blocks, seqs))
    sum_sems = pltpu.SemaphoreType.DMA((2, n_tp - 1))
    return pl.pallas_call(
        functools.partial(attend_back_kernel, n_tp, n_ctx, seqs),
        out_shape=[
            shape((rows, 3 * local), bf16), shape((8, local), f32), shape(gain_a.shape, f32),
            shape((width, 4 * local), bf16),
        ],
        in_specs=[vmem] * 14,
        out_specs=[vmem] * 4,
        scratch_shapes=[
            pltpu.VMEM((rows, local), bf16), pltpu.VMEM((rows, local), f32), pltpu.VMEM((rows, 2 * local), f32),
            pltpu.VMEM((blocks, rows, 2 * local), bf16), pltpu.VMEM((blocks, rows, 2 * local), bf16),
            pltpu.VMEM((8, rows), f32), pltpu.VMEM((n_tp - 1, 8, rows), f32),
            pltpu.VMEM((n_tp - 1,) + gain_a.shape, f32),
            kv_sems, kv_sems, sum_sems, sum_sems,
        ],
        compiler_params=params(5),
        cost_estimate=pl.CostEstimate(flops=60 * 10**9, bytes_accessed=30 << 20, transcendentals=0),
        name="attend_back",
    )(attn_low, w_out_t, raw, low, prev, head_out, stats, x, head_low, gain_q, gain_k, cosine, sine, gain_a)


def rotation_tables(positions):
    half = HD // 2
    frequency = rope_theta ** (-jnp.arange(half, dtype=f32) * 2.0 / HD)
    angles = positions.astype(f32)[:, None] * frequency[None, :]
    cosine, sine = jnp.cos(angles), jnp.sin(angles)
    return jnp.concatenate([cosine, cosine], axis=1), jnp.concatenate([-sine, sine], axis=1)


def per_device(
    tokens, w_query, w_key, w_value, w_output, w_gate, w_up, w_down,
    gain_query, gain_key, gain_attn, gain_mlp, cotangent,
):
    micro_count, rows, width = tokens.shape
    local = w_query.shape[1]
    ctx = lax.axis_size("ctx")
    ctx_rank = lax.axis_index("ctx")
    tp = lax.axis_size("tp")
    tp_rank = lax.axis_index("tp")
    positions = ctx_rank * rows + jnp.arange(rows, dtype=jnp.int32)
    cosine, sine = rotation_tables(positions)
    gain_q = gain_query.astype(f32)
    gain_k = gain_key.astype(f32)
    gain_a = gain_attn.astype(f32)
    gain_m = gain_mlp.astype(f32)
    xy = ("fsdp", "ctx")

    def gather(w):
        return lax.all_gather(w, xy, axis=0, tiled=True)

    w_qkv = gather(jnp.concatenate([w_query, w_key, w_value], axis=1))
    w_out_t = gather(w_output.T)
    w_g = gather(w_gate)
    w_u = gather(w_up)
    w_down_t = gather(w_down.T)

    def rms(a):
        return lax.rsqrt(jnp.mean(a * a, axis=-1, keepdims=True) + norm_eps)

    flat = (micro_count * rows, width)
    x_all, grad_all = tokens.reshape(flat), cotangent.reshape(flat)

    def own(a):
        a = a.reshape(flat[0] // (tp * PIECE), tp, PIECE, width)
        return lax.dynamic_index_in_dim(a, tp_rank, 1, keepdims=False).reshape(flat[0] // tp, width)

    tables = (gain_q[None], gain_k[None], cosine, sine)
    raw, low, prev, head_low, head_out, stats = attend(x_all, w_qkv, *tables, micro_count, tp, ctx)
    attention, mlp_in = attn_out(head_low, w_out_t, x_all, gain_a[None], tp)
    down, _, attn_low, mlp_weights, mixed_own, gain_m_sum, gain_a_sum = mlp(
        mlp_in, grad_all, own(attention), gain_m[None], gain_a[None], w_g, w_u, w_down_t, tp
    )
    att, down = attention.astype(f32), down.astype(f32)
    out = (x_all.astype(f32) + att * rms(att) * gain_a + down * rms(down) * gain_m).astype(bf16)

    def scatter(full):
        return lax.psum_scatter(full, xy, scatter_dimension=0, tiled=True).astype(f32)

    units = w_gate.shape[1]
    d_mlp = scatter(mlp_weights)
    d_down, d_gate, d_up = d_mlp[:, :units].T, d_mlp[:, units : 2 * units], d_mlp[:, 2 * units :]
    gain_a_own = jnp.sum(gain_a_sum, axis=0).reshape(8, width // 8)
    grad_qkv, gain_qk_sum, gain_a_tp, attn_weights = attend_back(
        attn_low, w_out_t, raw, low, prev, head_out, stats, x_all, head_low, *tables, gain_a_own, micro_count, tp, ctx
    )
    gains = jnp.concatenate(
        [gain_qk_sum[0], gain_qk_sum[1], gain_a_tp.reshape(width), jnp.sum(gain_m_sum, axis=0)]
    ).reshape(8, (local + width) // 4)
    grad_tokens, gains, d_attn = input_grad(
        grad_qkv, w_qkv, mixed_own, gains, attn_weights, tp, (lax.axis_size("fsdp"), lax.axis_size("ctx"))
    )
    gains = gains.reshape(2 * (local + width))
    return (
        out.reshape(tokens.shape),
        grad_tokens.reshape(tokens.shape),
        d_attn[:, :local], d_attn[:, local : 2 * local], d_attn[:, 2 * local : 3 * local],
        d_attn[:, 3 * local :].T, d_gate, d_up, d_down,
        gains[:local], gains[local : 2 * local],
        gains[2 * local : 2 * local + width], gains[2 * local + width :],
    )


def solution(mesh):
    rows, cols = P(("fsdp", "ctx"), "tp"), P("tp", ("fsdp", "ctx"))
    acts = P("fsdp", "ctx", None)
    in_specs = (acts, rows, rows, rows, cols, rows, rows, cols, P("tp"), P("tp"), P(), P(), acts)
    out_specs = (acts, acts, rows, rows, rows, cols, rows, rows, cols, P("tp"), P("tp"), P(), P())
    return jax.shard_map(
        per_device, mesh=mesh, in_specs=in_specs, out_specs=out_specs, check_vma=False
    )
```

```python
import functools

import jax
import jax.numpy as jnp
import numpy as np
from jax import lax
from jax.experimental import pallas as pl
from jax.experimental.pallas import tpu as pltpu
from jax.sharding import PartitionSpec as P

HD = 128
norm_eps = 1e-06
rope_theta = 500000.0
masked_value = -1e30
f32 = jnp.float32
bf16 = jnp.bfloat16


def dot(a, b, dims, out=f32):
    return lax.dot_general(a, b, (dims, ((), ())), preferred_element_type=f32).astype(out)


PIECE = 16
LAG = 1
CHUNK = 256
TILE_ROWS = 256
TILE_COLUMNS = 2048
MLP_TILE = 1024
TILES_PER_TICK = 3


class Line:
    def __init__(self, axis, n, groups, buf, total, send, recv):
        self.axis, self.n, self.groups = axis, n, groups
        self.buf, self.total, self.send, self.recv = buf, total, send, recv
        self.i = lax.axis_index(axis)
        self.stages = 2 * n - 1

    def rows(self, group, c, count=1):
        return pl.ds(pl.multiple_of((group * self.n + c) * PIECE, PIECE), count * PIECE)

    def copy(self, way, step, group, c, source):
        rows = self.rows(group, c)
        return pltpu.make_async_remote_copy(
            src_ref=self.buf.at[source, rows],
            dst_ref=self.buf.at[0 if way == 0 else 2, rows],
            send_sem=self.send.at[way, step, group],
            recv_sem=self.recv.at[way, step, group],
            device_id={self.axis: self.i + (1 if way == 0 else -1)},
            device_id_type=pl.DeviceIdType.MESH,
        )

    def add(self, c, group, source):
        rows = self.rows(group, c)
        both = self.buf[1, rows].astype(f32) + self.buf[source, rows].astype(f32)
        self.buf[1, rows] = both.astype(bf16)

    def reduce_step(self, s, group):
        i, n = self.i, self.n

        @pl.when(i <= min(s - 1, n - 2))
        def _():
            c = n - s + i
            if s >= 2:

                @pl.when(i >= 1)
                def _():
                    self.copy(0, s - 2, group, c, 1).wait_recv()
                    self.add(c, group, 0)

            self.copy(0, s - 1, group, c, 1).start()

        @pl.when(i >= max(n - s, 1))
        def _():
            c = s + i - n
            if s >= 2:

                @pl.when(i <= n - 2)
                def _():
                    self.copy(1, s - 2, group, c, 1).wait_recv()
                    self.add(c, group, 2)

            self.copy(1, s - 1, group, c, 1).start()

    def finish(self, group, then):
        i, n = self.i, self.n
        rows = self.rows(group, i)
        self.total[...] = self.buf[1, rows].astype(f32)

        @pl.when(i >= 1)
        def _():
            self.copy(0, n - 2, group, i, 1).wait_recv()
            self.total[...] += self.buf[0, rows].astype(f32)

        @pl.when(i <= n - 2)
        def _():
            self.copy(1, n - 2, group, i, 1).wait_recv()
            self.total[...] += self.buf[2, rows].astype(f32)

        self.buf[1, rows] = then(group, self.total[...]).astype(bf16)

        @pl.when(i <= n - 2)
        def _():
            self.copy(0, n - 1, group, i, 1).start()

        @pl.when(i >= 1)
        def _():
            self.copy(1, n - 1, group, i, 1).start()

    def gather_step(self, s, group):
        i, n = self.i, self.n

        @pl.when(i >= s - 1)
        def _():
            c = i - s + 1
            self.copy(0, n + s - 3, group, c, 0).wait_recv()
            if s <= n - 1:

                @pl.when(i <= n - 2)
                def _():
                    self.copy(0, n + s - 2, group, c, 0).start()

        @pl.when(i <= n - s)
        def _():
            c = i + s - 1
            self.copy(1, n + s - 3, group, c, 2).wait_recv()
            if s <= n - 1:

                @pl.when(i >= 1)
                def _():
                    self.copy(1, n + s - 2, group, c, 2).start()

    def sent(self, group):
        i, n = self.i, self.n
        for s in range(1, n):

            @pl.when(i <= min(s - 1, n - 2))
            def _():
                self.copy(0, s - 1, group, n - s + i, 1).wait_send()

            @pl.when(i >= max(n - s, 1))
            def _():
                self.copy(1, s - 1, group, s + i - n, 1).wait_send()

            @pl.when((i >= s - 1) & (i <= n - 2))
            def _():
                self.copy(0, n + s - 2, group, i - s + 1, 1 if s == 1 else 0).wait_send()

            @pl.when((i <= n - s) & (i >= 1))
            def _():
                self.copy(1, n + s - 2, group, i + s - 1, 1 if s == 1 else 2).wait_send()

    def piece(self, group, c):
        slot = jnp.where(c < self.i, 0, jnp.where(c > self.i, 2, 1))
        return self.buf[slot, self.rows(group, c)]

    def piece_ref(self, group, c):
        slot = jnp.where(c < self.i, 0, jnp.where(c > self.i, 2, 1))
        return self.buf.at[slot, self.rows(group, c)]

    def tick(self, t, then, done):
        n = self.n

        def stage(index, body):
            group = t - index * LAG

            @pl.when((group >= 0) & (group < self.groups))
            def _():
                body(group)

        for s in range(1, n):
            stage(s - 1, functools.partial(self.reduce_step, s))
        stage(n - 1, lambda group: self.finish(group, then))
        for s in range(2, n):
            stage(n + s - 2, functools.partial(self.gather_step, s))

        def last(group):
            self.gather_step(n, group)
            self.sent(group)
            done(group)

        stage(2 * n - 2, last)

    def ticks(self):
        return self.groups + (2 * self.n - 2) * LAG


def greet(axis, n, others=()):
    i = lax.axis_index(axis)
    barrier = pltpu.get_barrier_semaphore()
    for peer in others:
        pl.semaphore_signal(barrier, inc=1, device_id=peer, device_id_type=pl.DeviceIdType.MESH)

    @pl.when(i >= 1)
    def _():
        pl.semaphore_signal(barrier, inc=1, device_id={axis: i - 1}, device_id_type=pl.DeviceIdType.MESH)

    @pl.when(i <= n - 2)
    def _():
        pl.semaphore_signal(barrier, inc=1, device_id={axis: i + 1}, device_id_type=pl.DeviceIdType.MESH)

    pl.semaphore_wait(barrier, len(others) + jnp.minimum(i, 1) + jnp.minimum(n - 1 - i, 1))


def line_scratch(n, rows, width):
    sems = pltpu.SemaphoreType.DMA((2, 2 * n - 2, rows // (n * PIECE)))
    return [pltpu.VMEM((3, rows, width), bf16), pltpu.VMEM((PIECE, width), f32), sems, sems]


def params(collective_id):
    return pltpu.CompilerParams(
        collective_id=collective_id, has_side_effects=True, vmem_limit_bytes=63 << 20
    )


def scale_of(a):
    return lax.rsqrt(jnp.mean(a * a, axis=-1, keepdims=True) + norm_eps)


def local_copies(pairs, sems):
    copies = [pltpu.make_async_copy(a, b, sems.at[k]) for k, (a, b) in enumerate(pairs)]
    for copy in copies:
        copy.start()
    return copies


def mlp_kernel(
    n, mlp_in, grad, attn_own, gain_m, gain_a, w_g_hbm, w_u_hbm, w_d_hbm,
    down_out, hidden_out, attn_low_out, weights_out, mixed_own, gain_m_sum, gain_a_sum,
    buf, total, send, recv, w_g, w_u, w_d, mlp_rows, hidden, down_low, gate, up,
    ready, w_sems, io_sems, piece_sems, tile_sems, gain_m_acc, gain_a_acc,
):
    rows, width = grad.shape
    units = w_g.shape[1]
    groups = rows // (n * PIECE)
    per_chunk = CHUNK // (n * PIECE)
    line = Line("tp", n, groups, buf, total, send, recv)
    i = line.i
    tile = MLP_TILE

    def weight_copies(j):
        cols = pl.ds(pl.multiple_of(j * tile, tile), tile)
        return [
            pltpu.make_async_copy(w_g_hbm.at[:, cols], w_g.at[:, cols], w_sems.at[0, j]),
            pltpu.make_async_copy(w_u_hbm.at[:, cols], w_u.at[:, cols], w_sems.at[1, j]),
        ]

    for j in range(units // tile):
        for copy in weight_copies(j):
            copy.start()
    down_weights = pltpu.make_async_copy(w_d_hbm, w_d, w_sems.at[2, 0])
    down_weights.start()
    gain_m_acc[...] = jnp.zeros_like(gain_m_acc)
    gain_a_acc[...] = jnp.zeros_like(gain_a_acc)
    greet("tp", n)
    offset = per_chunk + line.stages

    def chunk_rows(chunk):
        return pl.ds(pl.multiple_of(chunk * CHUNK, CHUNK), CHUNK)

    def hidden_copy(chunk):
        return pltpu.make_async_copy(hidden, hidden_out.at[chunk_rows(chunk)], io_sems.at[1])

    def forward(chunk, first=False):
        at = chunk_rows(chunk)
        fetch = pltpu.make_async_copy(mlp_in.at[at], mlp_rows, io_sems.at[0])
        fetch.start()
        if not first:
            hidden_copy(chunk - 1).wait()
        fetch.wait()

        @pl.loop(0, units // tile)
        def _(j):
            if first:
                for copy in weight_copies(j):
                    copy.wait()
            cols = pl.ds(pl.multiple_of(j * tile, tile), tile)
            gate_proj = dot(mlp_rows[...], w_g[:, cols], ((1,), (0,)))
            up_proj = dot(mlp_rows[...], w_u[:, cols], ((1,), (0,)))
            gate[at, cols] = gate_proj.astype(bf16)
            up[at, cols] = up_proj.astype(bf16)
            hidden[:, cols] = (gate_proj / (1.0 + jnp.exp(-gate_proj)) * up_proj).astype(bf16)

        hidden_copy(chunk).start()

    def forward_down(chunk):
        at = chunk_rows(chunk)

        @pl.loop(0, width // tile)
        def _(j):
            cols = pl.ds(pl.multiple_of(j * tile, tile), tile)
            buf[1, at, cols] = dot(hidden[...], w_d[cols], ((1,), (1,)), bf16)

    def backward(chunk):
        at = chunk_rows(chunk)

        @pl.loop(0, units // tile)
        def _(j):
            cols = pl.ds(pl.multiple_of(j * tile, tile), tile)
            gate_proj, up_proj = gate[at, cols].astype(f32), up[at, cols].astype(f32)
            sig = 1.0 / (1.0 + jnp.exp(-gate_proj))
            grad_hidden = dot(down_low[at], w_d[:, cols], ((1,), (0,)))
            up[at, cols] = (grad_hidden * gate_proj * sig).astype(bf16)
            gate[at, cols] = (grad_hidden * up_proj * sig * (1.0 + gate_proj * (1.0 - sig))).astype(bf16)

    def backward_in(chunk):
        at = chunk_rows(chunk)

        @pl.loop(0, width // tile)
        def _(j):
            cols = pl.ds(pl.multiple_of(j * tile, tile), tile)
            buf[1, at, cols] = (
                dot(gate[at], w_g[cols], ((1,), (1,))) + dot(up[at], w_u[cols], ((1,), (1,)))
            ).astype(bf16)

    whole = pl.ds(0, rows)
    late_in = [(hidden_out, w_g.at[whole]), (mlp_in, w_u.at[whole])]
    per_part = width // TILE_ROWS

    def tile_copy(k, slot):
        part, block = lax.div(k, per_part), lax.rem(k, per_part)
        return pltpu.make_async_copy(
            w_d.at[pl.ds(pl.multiple_of(slot * TILE_ROWS, TILE_ROWS), TILE_ROWS)],
            weights_out.at[
                pl.ds(pl.multiple_of(block * TILE_ROWS, TILE_ROWS), TILE_ROWS),
                pl.ds(pl.multiple_of(part * units, units), units),
            ],
            tile_sems.at[slot],
        )

    def weight_tile(k):
        slot = lax.rem(k, 2)
        block = pl.ds(pl.multiple_of(lax.rem(k, per_part) * TILE_ROWS, TILE_ROWS), TILE_ROWS)

        @pl.when(k >= 2)
        def _():
            tile_copy(k - 2, slot).wait()

        def fill(left, right):
            @pl.loop(0, units // TILE_COLUMNS)
            def _(j):
                cols = pl.ds(pl.multiple_of(j * TILE_COLUMNS, TILE_COLUMNS), TILE_COLUMNS)
                w_d[pl.ds(pl.multiple_of(slot * TILE_ROWS, TILE_ROWS), TILE_ROWS), cols] = dot(
                    left[whole, block], right[whole, cols], ((0,), (0,)), bf16
                )

        @pl.when(k < per_part)
        def _():
            fill(down_low, w_g)

        @pl.when((k >= per_part) & (k < 2 * per_part))
        def _():
            fill(w_u, gate)

        @pl.when(k >= 2 * per_part)
        def _():
            fill(w_u, up)

        tile_copy(k, slot).start()

    def let_in():
        @pl.when(i >= 1)
        def _():
            pl.semaphore_signal(
                ready.at[1], inc=1, device_id={"tp": i - 1}, device_id_type=pl.DeviceIdType.MESH
            )

        @pl.when(i <= n - 2)
        def _():
            pl.semaphore_signal(
                ready.at[0], inc=1, device_id={"tp": i + 1}, device_id_type=pl.DeviceIdType.MESH
            )

    def pieces_out(group, out):
        return local_copies([(line.piece_ref(group, c), out.at[line.rows(group, c)]) for c in range(n)], piece_sems)

    def down_done(group):
        copies = pieces_out(group, down_out)
        for c in range(n):
            at = line.rows(group, c)
            branch = line.piece(group, c).astype(f32)
            r = scale_of(branch)
            g = grad[at].astype(f32)
            scaled = g * gain_m[...]
            inner = jnp.mean(scaled * branch, axis=-1, keepdims=True)
            gain_m_acc[...] += g * branch * r
            down_low[at] = (r * scaled - branch * (r * r * r) * inner).astype(bf16)
        for copy in copies:
            copy.wait()

    def attn_grad(group, total):
        at = pl.ds(pl.multiple_of(group * PIECE, PIECE), PIECE)
        mixed = grad[line.rows(group, i)].astype(f32) + total
        mixed_own[at] = mixed
        branch = attn_own[at].astype(f32)
        r = scale_of(branch)
        scaled = mixed * gain_a[...]
        inner = jnp.mean(scaled * branch, axis=-1, keepdims=True)
        gain_a_acc[...] += mixed * branch * r
        return r * scaled - branch * (r * r * r) * inner

    def attn_done(group):
        for copy in pieces_out(group, attn_low_out):
            copy.wait()

    forward(0, True)
    down_weights.wait()
    forward_down(0)

    @pl.loop(0, offset + line.ticks())
    def _(t):
        back = t - offset

        @pl.when((back >= 0) & (back < groups) & (lax.rem(back + groups, per_chunk) == 0))
        def _():
            @pl.when(i >= 1)
            def _():
                pl.semaphore_wait(ready.at[0], 1)

            @pl.when(i <= n - 2)
            def _():
                pl.semaphore_wait(ready.at[1], 1)

        line.tick(back, attn_grad, attn_done)
        line.tick(t, lambda group, total: total, down_done)
        for ahead, work in ((2, forward), (1, forward_down)):
            due = t + ahead

            @pl.when((due >= per_chunk) & (due < groups) & (lax.rem(due, per_chunk) == 0))
            def _():
                work(lax.div(due, per_chunk))

        for ahead, work in ((2, backward), (1, backward_in)):
            due = t + ahead - offset

            @pl.when((due >= 0) & (due < groups) & (lax.rem(due + groups, per_chunk) == 0))
            def _():
                if ahead == 1:
                    let_in()
                work(lax.div(due, per_chunk))

        first_tick = offset + groups - per_chunk

        def late_copies():
            return [pltpu.make_async_copy(a, b, io_sems.at[k]) for k, (a, b) in enumerate(late_in)]

        @pl.when(t == first_tick - 1)
        def _():
            hidden_copy(rows // CHUNK - 1).wait()
            for copy in late_copies():
                copy.start()

        @pl.when(t == first_tick)
        def _():
            for copy in late_copies():
                copy.wait()

        for m in range(TILES_PER_TICK):
            k = (t - first_tick) * TILES_PER_TICK + m

            @pl.when((k >= 0) & (k < 3 * per_part))
            def _():
                weight_tile(k)

    for k in (3 * per_part - 2, 3 * per_part - 1):
        tile_copy(k, k % 2).wait()
    gain_m_sum[...] = jnp.sum(gain_m_acc[...], axis=0, keepdims=True)
    gain_a_sum[...] = jnp.sum(gain_a_acc[...], axis=0, keepdims=True)


def mlp(mlp_in, grad, attn_own, gain_m, gain_a, w_g, w_u, w_d, n):
    rows, width = grad.shape
    units = w_g.shape[1]
    vmem, anywhere = pl.BlockSpec(memory_space=pltpu.VMEM), pl.BlockSpec(memory_space=pl.ANY)
    acts = jax.ShapeDtypeStruct((rows, width), bf16)
    inner = jax.ShapeDtypeStruct((rows, units), bf16)
    gain_shape = jax.ShapeDtypeStruct((1, width), f32)
    return pl.pallas_call(
        functools.partial(mlp_kernel, n),
        out_shape=[
            acts, inner, acts, jax.ShapeDtypeStruct((width, 3 * units), bf16),
            jax.ShapeDtypeStruct((rows // n, width), f32), gain_shape, gain_shape,
        ],
        in_specs=[anywhere] + [vmem] * 4 + [anywhere] * 3,
        out_specs=[anywhere] * 4 + [vmem] * 3,
        scratch_shapes=line_scratch(n, rows, width) + [
            pltpu.VMEM(w_g.shape, bf16), pltpu.VMEM(w_u.shape, bf16), pltpu.VMEM(w_d.shape, bf16),
            pltpu.VMEM((CHUNK, width), bf16), pltpu.VMEM((CHUNK, units), bf16), pltpu.VMEM((rows, width), bf16),
            pltpu.VMEM((rows, units), bf16), pltpu.VMEM((rows, units), bf16),
            pltpu.SemaphoreType.REGULAR((2,)),
            pltpu.SemaphoreType.DMA((3, units // 512)), pltpu.SemaphoreType.DMA((2,)), pltpu.SemaphoreType.DMA((n,)),
            pltpu.SemaphoreType.DMA((2,)),
            pltpu.VMEM((PIECE, width), f32), pltpu.VMEM((PIECE, width), f32),
        ],
        compiler_params=params(2),
        cost_estimate=pl.CostEstimate(flops=200 * 10**9, bytes_accessed=60 << 20, transcendentals=0),
        name="mlp",
    )(mlp_in, grad, attn_own, gain_m, gain_a, w_g, w_u, w_d)


class Owners:
    def __init__(self, n_xy, full, pair_in, peer_in, result, pair_sems, peer_sems):
        n_fsdp, self.n_ctx = n_xy
        self.chips = n_fsdp // 2
        self.full, self.pair_in, self.peer_in, self.result = full, pair_in, peer_in, result
        self.pair_sems, self.peer_sems = pair_sems, peer_sems
        fsdp = lax.axis_index("fsdp")
        self.core = lax.rem(fsdp, 2)
        self.ctx = lax.axis_index("ctx")
        self.place = lax.div(fsdp, 2) * self.n_ctx + self.ctx
        self.block = full.shape[0] // (n_fsdp * self.n_ctx)

    def pair_copy(self, chip):
        there = 1 - self.core
        span = self.n_ctx * self.block
        rows = pl.ds(pl.multiple_of((2 * chip + there) * span, span), span)
        return pltpu.make_async_remote_copy(
            src_ref=self.full.at[rows], dst_ref=self.pair_in.at[pl.ds(chip * span, span)],
            send_sem=self.pair_sems.at[0, chip], recv_sem=self.pair_sems.at[1, chip],
            device_id={"fsdp": 2 * lax.div(lax.axis_index("fsdp"), 2) + there}, device_id_type=pl.DeviceIdType.MESH,
        )

    def peer_copy(self, k):
        place = lax.rem(self.place + k, self.chips * self.n_ctx)
        return pltpu.make_async_remote_copy(
            src_ref=self.pair_in.at[self.block_rows(place)], dst_ref=self.peer_in.at[k - 1],
            send_sem=self.peer_sems.at[0, k - 1], recv_sem=self.peer_sems.at[1, k - 1],
            device_id={"fsdp": 2 * lax.div(place, self.n_ctx) + self.core, "ctx": lax.rem(place, self.n_ctx)},
            device_id_type=pl.DeviceIdType.MESH,
        )

    def block_rows(self, place):
        return pl.ds(pl.multiple_of(place * self.block, self.block), self.block)

    def start(self):
        for chip in range(self.chips):
            self.pair_copy(chip).start()

    def pass_on(self):
        span = self.n_ctx * self.block
        for chip in range(self.chips):
            self.pair_copy(chip).wait_recv()
            rows = pl.ds(chip * span, span)
            mine = pl.ds(pl.multiple_of((2 * chip + self.core) * span, span), span)
            self.pair_in[rows] = (self.pair_in[rows].astype(f32) + self.full[mine].astype(f32)).astype(bf16)
        for k in range(1, self.chips * self.n_ctx):
            self.peer_copy(k).start()

    def end(self):
        self.result[...] = self.pair_in[self.block_rows(self.place)].astype(f32)
        for k in range(1, self.chips * self.n_ctx):
            self.peer_copy(k).wait()
            self.result[...] += self.peer_in[k - 1].astype(f32)
        for chip in range(self.chips):
            self.pair_copy(chip).wait_send()


def owners_scratch(n_xy, shape):
    n_fsdp, n_ctx = n_xy
    peers = n_fsdp // 2 * n_ctx - 1
    block = shape[0] // (n_fsdp * n_ctx)
    return [
        pltpu.VMEM((shape[0] // 2, shape[1]), bf16), pltpu.VMEM((peers, block, shape[1]), bf16),
        pltpu.SemaphoreType.DMA((2, n_fsdp // 2)), pltpu.SemaphoreType.DMA((2, peers)),
    ]


def input_grad_kernel(
    n, n_xy, grad_qkv, w_full_hbm, mixed_own, gains, weights, grad_out, gains_sum, weights_own,
    buf, total, send, recv, w_qkv, w_sem, piece_sems, gains_theirs, gain_send, gain_recv,
    pair_in, peer_in, pair_sems, peer_sems,
):
    rows, width = buf.shape[1:]
    groups = rows // (n * PIECE)
    per_chunk = CHUNK // (n * PIECE)
    line = Line("tp", n, groups, buf, total, send, recv)
    fetch = pltpu.make_async_copy(w_full_hbm.at[:, pl.ds(0, w_qkv.shape[1])], w_qkv, w_sem)
    fetch.start()
    n_fsdp, n_ctx = n_xy
    place = lax.axis_index("fsdp") * n_ctx + lax.axis_index("ctx")
    others = []
    for k in range(1, n_fsdp * n_ctx):
        peer = lax.rem(place + k, n_fsdp * n_ctx)
        others.append({"fsdp": lax.div(peer, n_ctx), "ctx": lax.rem(peer, n_ctx)})
    greet("tp", n, others)
    gain_copies = [
        pltpu.make_async_remote_copy(
            src_ref=gains, dst_ref=gains_theirs.at[k], send_sem=gain_send.at[k], recv_sem=gain_recv.at[k],
            device_id=peer, device_id_type=pl.DeviceIdType.MESH,
        )
        for k, peer in enumerate(others)
    ]
    for copy in gain_copies:
        copy.start()
    owners = Owners(n_xy, weights, pair_in, peer_in, weights_own, pair_sems, peer_sems)
    owners.start()
    fetch.wait()
    tile = 512

    def own(group, total):
        return total + mixed_own[pl.ds(pl.multiple_of(group * PIECE, PIECE), PIECE)]

    def done(group):
        copies = local_copies(
            [(line.piece_ref(group, c), grad_out.at[line.rows(group, c)]) for c in range(n)], piece_sems
        )
        for copy in copies:
            copy.wait()

    @pl.loop(0, line.ticks())
    def _(t):
        @pl.when((t < groups) & (lax.rem(t, per_chunk) == 0))
        def _():
            at = pl.ds(pl.multiple_of(t * n * PIECE, CHUNK), CHUNK)

            @pl.loop(0, width // tile)
            def _(j):
                cols = pl.ds(pl.multiple_of(j * tile, tile), tile)
                buf[1, at, cols] = dot(grad_qkv[at], w_qkv[cols], ((1,), (1,)), bf16)

        line.tick(t, own, done)

        @pl.when(t == 2)
        def _():
            owners.pass_on()

    owners.end()
    gains_sum[...] = gains[...]
    for k, copy in enumerate(gain_copies):
        copy.wait()
        gains_sum[...] += gains_theirs[k]


def input_grad(grad_qkv, w_full, mixed_own, gains, weights, n, n_xy):
    rows, width = grad_qkv.shape[0], w_full.shape[0]
    peers = n_xy[0] * n_xy[1] - 1
    vmem, anywhere = pl.BlockSpec(memory_space=pltpu.VMEM), pl.BlockSpec(memory_space=pl.ANY)
    return pl.pallas_call(
        functools.partial(input_grad_kernel, n, n_xy),
        out_shape=[
            jax.ShapeDtypeStruct((rows, width), bf16), jax.ShapeDtypeStruct(gains.shape, f32),
            jax.ShapeDtypeStruct((weights.shape[0] // (n_xy[0] * n_xy[1]), weights.shape[1]), f32),
        ],
        in_specs=[vmem, anywhere, vmem, vmem, vmem],
        out_specs=[anywhere, vmem, vmem],
        scratch_shapes=line_scratch(n, rows, width) + [
            pltpu.VMEM((width, grad_qkv.shape[1]), bf16), pltpu.SemaphoreType.DMA, pltpu.SemaphoreType.DMA((n,)),
            pltpu.VMEM((peers,) + gains.shape, f32), pltpu.SemaphoreType.DMA((peers,)), pltpu.SemaphoreType.DMA((peers,)),
        ] + owners_scratch(n_xy, weights.shape),
        compiler_params=params(3),
        cost_estimate=pl.CostEstimate(flops=100 * 10**9, bytes_accessed=20 << 20, transcendentals=0),
        name="input_grad",
    )(grad_qkv, w_full, mixed_own, gains, weights)


def peers_of(axis, n):
    i = lax.axis_index(axis)
    return [(k - 1, lax.rem(i + k, n)) for k in range(1, n)]


def meet(axes, others=()):
    barrier = pltpu.get_barrier_semaphore()
    count = len(others)
    for peer in others:
        pl.semaphore_signal(barrier, inc=1, device_id=peer, device_id_type=pl.DeviceIdType.MESH)
    for axis, n in axes:
        for _, peer in peers_of(axis, n):
            pl.semaphore_signal(barrier, inc=1, device_id={axis: peer}, device_id_type=pl.DeviceIdType.MESH)
            count += 1
    pl.semaphore_wait(barrier, count)


def swap(axis, n, pairs, send, recv):
    copies = []
    for k, (mine, theirs) in enumerate(pairs):
        for slot, peer in peers_of(axis, n):
            copy = pltpu.make_async_remote_copy(
                src_ref=mine, dst_ref=theirs.at[slot],
                send_sem=send.at[k, slot], recv_sem=recv.at[k, slot],
                device_id={axis: peer}, device_id_type=pl.DeviceIdType.MESH,
            )
            copy.start()
            copies.append(copy)
    for copy in copies:
        copy.wait()


def lanes_to_rows(columns):
    return jnp.transpose(columns)[:8]


def rows_to_lanes(packed):
    rows = packed.shape[1]
    return jnp.transpose(jnp.concatenate([packed, jnp.zeros((120, rows), f32)], axis=0))


def two_lanes(first, second):
    lane = lax.broadcasted_iota(jnp.int32, (first.shape[0], 128), 1)
    return jnp.where(lane == 0, first, jnp.where(lane == 1, second, 0.0))


def turn(values, cosine, sine):
    return values * cosine + pltpu.roll(values, HD // 2, 1) * sine


def heads_loop(heads, body):
    @pl.loop(0, heads)
    def _(h):
        body(h, lambda part, width: pl.ds(pl.multiple_of(part * width + h * HD, HD), HD))


class Gather:
    def __init__(self, n_xy, parts, full, local_sems, sems):
        n_fsdp, self.n_ctx = n_xy
        self.chips = n_fsdp // 2
        self.parts, self.full, self.local_sems, self.sems = parts, full, local_sems, sems
        fsdp = lax.axis_index("fsdp")
        self.chip, self.core = lax.div(fsdp, 2), lax.rem(fsdp, 2)
        self.ctx = lax.axis_index("ctx")
        self.block = parts[0].shape[0]

    def place(self, part, chip, core, ctx):
        columns = self.parts[part].shape[1]
        first = sum(p.shape[1] for p in self.parts[:part])
        row = ((2 * chip + core) * self.n_ctx + ctx) * self.block
        return self.full.at[pl.ds(pl.multiple_of(row, self.block), self.block), pl.ds(first, columns)]

    def send(self, part, slot, source, target, device):
        return pltpu.make_async_remote_copy(
            src_ref=source, dst_ref=target,
            send_sem=self.sems.at[0, part, slot], recv_sem=self.sems.at[1, part, slot],
            device_id=device, device_id_type=pl.DeviceIdType.MESH,
        )

    def keep(self, part):
        return pltpu.make_async_copy(
            self.parts[part], self.place(part, self.chip, self.core, self.ctx), self.local_sems.at[part]
        )

    def to_ctx(self, part, k):
        target = self.place(part, self.chip, self.core, self.ctx)
        return self.send(part, k - 1, self.parts[part], target, {"ctx": lax.rem(self.ctx + k, self.n_ctx)})

    def to_chip(self, part, c, k):
        ctx = lax.rem(self.ctx + self.n_ctx - c, self.n_ctx)
        target = self.place(part, self.chip, self.core, ctx)
        source = self.parts[part] if c == 0 else target
        slot = self.n_ctx - 1 + c * (self.chips - 1) + k - 1
        chip = lax.rem(self.chip + k, self.chips)
        return self.send(part, slot, source, target, {"fsdp": 2 * chip + self.core})

    def to_core(self, part, c, k):
        ctx = lax.rem(self.ctx + self.n_ctx - c, self.n_ctx)
        chip = lax.rem(self.chip + self.chips - k, self.chips)
        target = self.place(part, chip, self.core, ctx)
        source = self.parts[part] if c == 0 and k == 0 else target
        slot = self.n_ctx - 1 + self.n_ctx * (self.chips - 1) + c * self.chips + k
        return self.send(part, slot, source, target, {"fsdp": 2 * self.chip + 1 - self.core})

    def slots(self):
        return self.n_ctx - 1 + self.n_ctx * (self.chips - 1) + self.n_ctx * self.chips

    def start(self, part):
        self.keep(part).start()
        for k in range(1, self.n_ctx):
            self.to_ctx(part, k).start()
        for k in range(1, self.chips):
            self.to_chip(part, 0, k).start()
        self.to_core(part, 0, 0).start()

    def pass_on(self, part):
        for c in range(1, self.n_ctx):
            self.to_ctx(part, c).wait_recv()
            for k in range(1, self.chips):
                self.to_chip(part, c, k).start()
            self.to_core(part, c, 0).start()
        for c in range(self.n_ctx):
            for k in range(1, self.chips):
                self.to_chip(part, c, k).wait_recv()
                self.to_core(part, c, k).start()

    def end(self, part):
        for c in range(self.n_ctx):
            for k in range(self.chips):
                self.to_core(part, c, k).wait_recv()
        self.keep(part).wait()

    def sent(self, part):
        for k in range(1, self.n_ctx):
            self.to_ctx(part, k).wait_send()
        for c in range(self.n_ctx):
            for k in range(1, self.chips):
                self.to_chip(part, c, k).wait_send()
            for k in range(self.chips):
                self.to_core(part, c, k).wait_send()


def front_kernel(
    n_tp, n_xy, seqs, x_hbm, w_q, w_k, w_v, w_o, gain_q, gain_k, gain_a, cosine, sine,
    raw_out, low_out, prev_out, head_low_out, stats_out, attention_out, mlp_in_out, w_out, attn_own_out,
    buf, total, send, recv, x, w, raw, low, prev, head_low, stats, mlp_in, attn_own,
    sums, theirs, kv_send, kv_recv, sum_send, sum_recv, w_local_sems, w_sems, io_sems, piece_sems, group_sems,
):
    n_ctx = n_xy[1]
    rows_all, width = x.shape
    rows = rows_all // seqs
    local = w_q.shape[1]
    heads = local // HD
    me = lax.axis_index("ctx")
    scale = HD ** (-0.5)
    step = min(256, rows)
    fetch_x = pltpu.make_async_copy(x_hbm, x, io_sems.at[0])
    fetch_x.start()
    gather = Gather(n_xy, [w_v, w_k, w_q, w_o], w, w_local_sems, w_sems)
    value_at, key_at, query_at, out_at = 0, local, 2 * local, 3 * local
    fsdp = lax.axis_index("fsdp")
    meet(
        [("tp", n_tp), ("ctx", n_ctx)],
        [{"fsdp": 2 * lax.div(fsdp, 2) + 1 - lax.rem(fsdp, 2)}]
        + [{"fsdp": lax.rem(fsdp + 2 * k, n_xy[0])} for k in range(1, n_xy[0] // 2)],
    )
    for part in range(4):
        gather.start(part)

    def chunks(body):
        @pl.loop(0, rows_all // step)
        def _(k):
            at = pl.ds(pl.multiple_of(k * step, step), step)
            body(at, pl.ds(pl.multiple_of(me * rows + lax.rem(k, rows // step) * step, step), step))

    for j in range(1, n_ctx):

        @pl.when(me < j)
        def _():
            prev[j - 1] = jnp.zeros(prev.shape[1:], bf16)

    def kv_copy(j, part, seq):
        at = pl.ds(seq * rows, rows)
        return pltpu.make_async_remote_copy(
            src_ref=low.at[at, pl.ds((1 + part) * local, local)],
            dst_ref=prev.at[j - 1, at, pl.ds(part * local, local)],
            send_sem=kv_send.at[j - 1, part, seq], recv_sem=kv_recv.at[j - 1, part, seq],
            device_id={"ctx": lax.rem(me + j, n_ctx)}, device_id_type=pl.DeviceIdType.MESH,
        )

    def kv_each(method, part, seq, here):
        for j in range(1, n_ctx):

            @pl.when((me >= j) if here else (me + j < n_ctx))
            def _():
                getattr(kv_copy(j, part, seq), method)()

    gather.pass_on(0)
    gather.pass_on(1)
    gather.end(0)
    fetch_x.wait()

    def value_chunk(at, _):
        low[at, 2 * local :] = dot(x[at], w[:, value_at : value_at + local], ((1,), (0,)), bf16)

    chunks(value_chunk)
    for seq in range(seqs):
        kv_each("start", 1, seq, False)
    gather.pass_on(2)
    gather.end(1)

    def raw_chunk(part, first):
        def chunk(at, _):
            v = dot(x[at], w[:, first : first + local], ((1,), (0,)))
            raw[at, part * local : (part + 1) * local] = v
            square = jnp.sum(v * v, axis=-1, keepdims=True)
            lane = lax.broadcasted_iota(jnp.int32, (step, 128), 1)
            stats[at] = jnp.where(lane == part, square, stats[at] if part == 0 else 0.0)

        chunks(chunk)

    raw_chunk(1, key_at)
    gather.pass_on(3)
    gather.end(2)
    raw_chunk(0, query_at)

    def sums_chunk(at, _):
        sums[:, at] = lanes_to_rows(stats[at])

    chunks(sums_chunk)
    swap("tp", n_tp, [(sums, theirs)], sum_send, sum_recv)
    square_sums = sums[...]
    for slot in range(n_tp - 1):
        square_sums = square_sums + theirs[slot]
    stats[...] = rows_to_lanes(lax.rsqrt(square_sums / width + norm_eps))

    def turned(part, gain):
        def chunk(at, pos):
            r = stats[at, part : part + 1]
            for h in range(heads):
                cols = pl.ds(part * local + h * HD, HD)
                v = raw[at, cols] * r * gain[:, h * HD : (h + 1) * HD]
                low[at, cols] = turn(v, cosine[pos], sine[pos]).astype(bf16)

        chunks(chunk)

    turned(1, gain_k)
    for seq in range(seqs):
        kv_each("start", 0, seq, False)
    turned(0, gain_q)
    lane = lax.broadcasted_iota(jnp.int32, (step, 128), 1)

    def attention(seq):
        for part in range(2):
            kv_each("wait_recv", part, seq, True)
        seq_rows = pl.ds(seq * rows, rows)

        def one_head(h, cols):
            for tile in range(rows // step):
                at = pl.ds(seq * rows + tile * step, step)
                q = low[at, cols(0, local)]
                seen = (tile + 1) * step
                own = pl.ds(seq * rows, seen)
                s = dot(q, low[own, cols(1, local)], ((1,), (1,))) * scale
                i_pos = lax.broadcasted_iota(jnp.int32, (step, seen), 0) + tile * step
                j_pos = lax.broadcasted_iota(jnp.int32, (step, seen), 1)
                scores = [jnp.where(j_pos <= i_pos, s, masked_value)]
                values = [low[own, cols(2, local)]]
                for j in range(1, n_ctx):
                    s = dot(q, prev[j - 1, seq_rows, cols(0, local)], ((1,), (1,))) * scale
                    scores.append(jnp.where(me >= j, s, masked_value))
                    values.append(prev[j - 1, seq_rows, cols(1, local)])
                top = scores[0].max(-1, keepdims=True)
                for s in scores[1:]:
                    top = jnp.maximum(top, s.max(-1, keepdims=True))
                total, weighted = 0.0, 0.0
                for s, v in zip(scores, values):
                    e = jnp.exp(s - top)
                    total = total + e.sum(-1, keepdims=True)
                    weighted = weighted + dot(e.astype(bf16), v, ((1,), (0,)))
                head_low[at, cols(0, local)] = (weighted / total).astype(bf16)
                stats[at] = jnp.where(lane == h + 2, top + jnp.log(total), stats[at])

        heads_loop(heads, one_head)

    attention(0)
    gather.end(3)

    groups = rows_all // (n_tp * PIECE)
    line = Line("tp", n_tp, groups, buf, total, send, recv)
    per_chunk, per_seq = step // (n_tp * PIECE), rows // (n_tp * PIECE)
    tile = 512

    def group_rows(group):
        return pl.ds(pl.multiple_of(group * n_tp * PIECE, n_tp * PIECE), n_tp * PIECE)

    def mlp_copy(group):
        at = group_rows(group)
        return pltpu.make_async_copy(mlp_in.at[at], mlp_in_out.at[at], group_sems.at[group])

    def own(group, total):
        attn_own[pl.ds(pl.multiple_of(group * PIECE, PIECE), PIECE)] = total.astype(bf16)
        return total

    def done(group):
        copies = local_copies(
            [(line.piece_ref(group, c), attention_out.at[line.rows(group, c)]) for c in range(n_tp)], piece_sems
        )
        for c in range(n_tp):
            at = line.rows(group, c)
            a = line.piece(group, c).astype(f32)
            mlp_in[at] = (x[at].astype(f32) + a * scale_of(a) * gain_a[...]).astype(bf16)
        mlp_copy(group).start()
        for copy in copies:
            copy.wait()

    saves = [
        (raw, raw_out), (low, low_out), (prev, prev_out), (head_low, head_low_out), (stats, stats_out), (w, w_out),
    ]

    @pl.loop(0, line.ticks())
    def _(t):
        @pl.when((t < groups) & (lax.rem(t, per_chunk) == 0))
        def _():
            at = pl.ds(pl.multiple_of(t * n_tp * PIECE, step), step)

            @pl.loop(0, width // tile)
            def _(j):
                cols = pl.ds(pl.multiple_of(j * tile, tile), tile)
                buf[1, at, cols] = dot(head_low[at], w[cols, out_at : out_at + local], ((1,), (1,)), bf16)

        line.tick(t, own, done)
        for seq in range(1, seqs):

            @pl.when(t == seq * per_seq - 1)
            def _():
                attention(seq)

        @pl.when(t == (seqs - 1) * per_seq)
        def _():
            for k, (source, target) in enumerate(saves):
                pltpu.make_async_copy(source, target, io_sems.at[k]).start()

    own_out = pltpu.make_async_copy(attn_own, attn_own_out, piece_sems.at[0])
    own_out.start()
    for k, (source, target) in enumerate(saves):
        pltpu.make_async_copy(source, target, io_sems.at[k]).wait()
    own_out.wait()

    @pl.loop(0, groups)
    def _(group):
        mlp_copy(group).wait()

    for part in range(4):
        gather.sent(part)
    for seq in range(seqs):
        for part in range(2):
            kv_each("wait_send", part, seq, False)


def front(x, w_q, w_k, w_v, w_o, gain_q, gain_k, gain_a, cosine, sine, seqs, n_tp, n_xy):
    rows, width = x.shape
    local = w_q.shape[1]
    n_fsdp, n_ctx = n_xy
    chips = n_fsdp // 2
    vmem, anywhere = pl.BlockSpec(memory_space=pltpu.VMEM), pl.BlockSpec(memory_space=pl.ANY)
    shape = jax.ShapeDtypeStruct
    dma = pltpu.SemaphoreType.DMA
    saved = [
        shape((rows, 2 * local), f32), shape((rows, 3 * local), bf16),
        shape((max(n_ctx - 1, 1), rows, 2 * local), bf16),
        shape((rows, local), bf16), shape((rows, 128), f32),
    ]
    acts, full = shape(x.shape, bf16), shape((width, 4 * local), bf16)
    vmem_of = [pltpu.VMEM(a.shape, a.dtype) for a in saved]
    slots = n_ctx - 1 + n_ctx * (chips - 1) + n_ctx * chips
    kv_sems, sum_sems = dma((max(n_ctx - 1, 1), 2, seqs)), dma((1, n_tp - 1))
    return pl.pallas_call(
        functools.partial(front_kernel, n_tp, n_xy, seqs),
        out_shape=saved + [acts, acts, full, shape((rows // n_tp, width), bf16)],
        in_specs=[anywhere] + [vmem] * 9,
        out_specs=[anywhere] * 9,
        scratch_shapes=line_scratch(n_tp, rows, width) + [
            pltpu.VMEM(x.shape, bf16), pltpu.VMEM(full.shape, bf16), *vmem_of, pltpu.VMEM(x.shape, bf16),
            pltpu.VMEM((rows // n_tp, width), bf16),
            pltpu.VMEM((8, rows), f32), pltpu.VMEM((n_tp - 1, 8, rows), f32),
            kv_sems, kv_sems, sum_sems, sum_sems, dma((4,)), dma((2, 4, slots)), dma((7,)), dma((n_tp,)),
            dma((rows // (n_tp * PIECE),)),
        ],
        compiler_params=params(1),
        cost_estimate=pl.CostEstimate(flops=150 * 10**9, bytes_accessed=30 << 20, transcendentals=0),
        name="front",
    )(x, w_q, w_k, w_v, w_o, gain_q, gain_k, gain_a, cosine, sine)


def attend_back_kernel(
    n_tp, n_ctx, seqs, attn_low, w_full, raw, low, prev, stats, x, head_low, gain_q, gain_k, cosine, sine, gain_a,
    grad_qkv, gain_qk_sum, gain_a_sum, weights_out,
    grad_heads, grad_q, grad_kv, out_kv, in_kv, sums, theirs, gain_theirs, kv_send, kv_recv, sum_send, sum_recv,
):
    rows_all, width = attn_low.shape
    rows = rows_all // seqs
    local = head_low.shape[1]
    heads = local // HD
    me = lax.axis_index("ctx")
    scale = HD ** (-0.5)
    meet([("tp", n_tp), ("ctx", n_ctx)])
    step = min(256, rows)

    def chunks(body):
        @pl.loop(0, rows_all // step)
        def _(k):
            at = pl.ds(pl.multiple_of(k * step, step), step)
            body(at, pl.ds(pl.multiple_of(me * rows + lax.rem(k, rows // step) * step, step), step))

    def heads_chunk(at, _):
        grad_heads[at] = dot(attn_low[at], w_full[:, 3 * local :], ((1,), (0,)), bf16)

    chunks(heads_chunk)
    grad_q[...] = jnp.zeros_like(grad_q)
    grad_kv[...] = jnp.zeros_like(grad_kv)

    def kv_copy(j, seq):
        at = pl.ds(seq * rows, rows)
        return pltpu.make_async_remote_copy(
            src_ref=out_kv.at[j - 1, at], dst_ref=in_kv.at[j - 1, at],
            send_sem=kv_send.at[j - 1, seq], recv_sem=kv_recv.at[j - 1, seq],
            device_id={"ctx": lax.rem(me + n_ctx - j, n_ctx)}, device_id_type=pl.DeviceIdType.MESH,
        )

    def lane_of(at, index):
        lane = lax.broadcasted_iota(jnp.int32, (step, 128), 1)
        return jnp.sum(jnp.where(lane == index, stats[at], 0.0), axis=-1, keepdims=True)

    def block(h, cols, at, keys, values, mask):
        q, g = low[at, cols(0, local)], grad_heads[at, cols(0, local)]
        delta = jnp.sum(g.astype(f32) * head_low[at, cols(0, local)].astype(f32), axis=-1, keepdims=True)
        s = dot(q, keys, ((1,), (1,))) * scale
        p = jnp.exp(s - lane_of(at, h + 2))
        if mask is not None:
            p = jnp.where(mask, p, 0.0)
        dp = dot(g, values, ((1,), (1,)))
        ds = (p * (dp - delta)).astype(bf16)
        grad_q[at, cols(0, local)] += dot(ds, keys, ((1,), (0,))) * scale
        return dot(ds, q, ((0,), (0,))) * scale, dot(p.astype(bf16), g, ((0,), (0,)))

    for j in range(1, n_ctx):

        @pl.when(me >= j)
        def _():
            for seq in range(seqs):
                seq_rows = pl.ds(seq * rows, rows)

                def one_head(h, cols):
                    keys, values = prev[j - 1, seq_rows, cols(0, local)], prev[j - 1, seq_rows, cols(1, local)]
                    dk, dv = 0.0, 0.0
                    for tile in range(rows // step):
                        at = pl.ds(seq * rows + tile * step, step)
                        k_term, v_term = block(h, cols, at, keys, values, None)
                        dk, dv = dk + k_term, dv + v_term
                    out_kv[j - 1, seq_rows, cols(0, local)] = dk.astype(bf16)
                    out_kv[j - 1, seq_rows, cols(1, local)] = dv.astype(bf16)

                heads_loop(heads, one_head)
                kv_copy(j, seq).start()

    for seq in range(seqs):

        def one_head(h, cols):
            for tile in range(rows // step):
                at = pl.ds(seq * rows + tile * step, step)
                seen = (tile + 1) * step
                own = pl.ds(seq * rows, seen)
                i_pos = lax.broadcasted_iota(jnp.int32, (step, seen), 0) + tile * step
                j_pos = lax.broadcasted_iota(jnp.int32, (step, seen), 1)
                k_term, v_term = block(
                    h, cols, at, low[own, cols(1, local)], low[own, cols(2, local)], j_pos <= i_pos
                )
                grad_kv[own, cols(0, local)] += k_term
                grad_kv[own, cols(1, local)] += v_term

        heads_loop(heads, one_head)

    def weight_rows(left, right, cols):
        @pl.loop(0, width // step)
        def _(k):
            at = pl.ds(pl.multiple_of(k * step, step), step)
            weights_out[at, cols] = dot(left[:, at], right[...], ((0,), (0,)), bf16)

    weight_rows(attn_low, head_low, pl.ds(3 * local, local))

    for j in range(1, n_ctx):
        for seq in range(seqs):

            @pl.when(me + j < n_ctx)
            def _():
                kv_copy(j, seq).wait_recv()
                at = pl.ds(seq * rows, rows)
                grad_kv[at] += in_kv[j - 1, at].astype(f32)

    def turned(at, pos, part, ref, gain):
        inner = 0.0
        for h in range(heads):
            cols = pl.ds(h * HD, HD)
            d = turn(ref[at, cols], cosine[pos], -sine[pos])
            ref[at, cols] = d
            weighted = d * raw[at, pl.ds(part * local + h * HD, HD)] * gain[:, h * HD : (h + 1) * HD]
            inner = inner + jnp.sum(weighted, axis=-1, keepdims=True)
        return inner

    def inner_chunk(at, pos):
        both = two_lanes(
            turned(at, pos, 0, grad_q, gain_q), turned(at, pos, 1, grad_kv, gain_k)
        )
        sums[:, at] = lanes_to_rows(both)

    chunks(inner_chunk)
    swap("tp", n_tp, [(sums, theirs), (gain_a, gain_theirs)], sum_send, sum_recv)
    total, gain_total = sums[...], gain_a[...]
    for slot in range(n_tp - 1):
        total = total + theirs[slot]
        gain_total = gain_total + gain_theirs[slot]
    gain_a_sum[...] = gain_total
    sums[...] = total / width
    gain_qk_sum[...] = jnp.zeros_like(gain_qk_sum)

    def out_chunk(at, _):
        inner = rows_to_lanes(sums[:, at])
        for part, ref, gain in ((0, grad_q, gain_q), (1, grad_kv, gain_k)):
            r = stats[at, part : part + 1]
            d, v = ref[at, :local], raw[at, pl.ds(part * local, local)]
            grad_qkv[at, pl.ds((2 - part) * local, local)] = (
                d * r * gain[...] - v * (r * r * r) * inner[:, part : part + 1]
            ).astype(bf16)
            gain_qk_sum[part : part + 1] += jnp.sum(d * v * r, axis=0, keepdims=True)
        grad_qkv[at, :local] = grad_kv[at, local:].astype(bf16)

    chunks(out_chunk)
    weight_rows(x, grad_qkv, pl.ds(0, 3 * local))

    for j in range(1, n_ctx):
        for seq in range(seqs):

            @pl.when(me >= j)
            def _():
                kv_copy(j, seq).wait_send()


def attend_back(
    attn_low, w_full, raw, low, prev, stats, x, head_low, gain_q, gain_k, cosine, sine, gain_a, seqs, n_tp, n_ctx
):
    rows, width = attn_low.shape
    local = head_low.shape[1]
    vmem = pl.BlockSpec(memory_space=pltpu.VMEM)
    shape = jax.ShapeDtypeStruct
    blocks = max(n_ctx - 1, 1)
    kv_sems = pltpu.SemaphoreType.DMA((blocks, seqs))
    sum_sems = pltpu.SemaphoreType.DMA((2, n_tp - 1))
    return pl.pallas_call(
        functools.partial(attend_back_kernel, n_tp, n_ctx, seqs),
        out_shape=[
            shape((rows, 3 * local), bf16), shape((8, local), f32), shape(gain_a.shape, f32),
            shape((width, 4 * local), bf16),
        ],
        in_specs=[vmem] * 13,
        out_specs=[vmem] * 4,
        scratch_shapes=[
            pltpu.VMEM((rows, local), bf16), pltpu.VMEM((rows, local), f32), pltpu.VMEM((rows, 2 * local), f32),
            pltpu.VMEM((blocks, rows, 2 * local), bf16), pltpu.VMEM((blocks, rows, 2 * local), bf16),
            pltpu.VMEM((8, rows), f32), pltpu.VMEM((n_tp - 1, 8, rows), f32),
            pltpu.VMEM((n_tp - 1,) + gain_a.shape, f32),
            kv_sems, kv_sems, sum_sems, sum_sems,
        ],
        compiler_params=params(5),
        cost_estimate=pl.CostEstimate(flops=60 * 10**9, bytes_accessed=30 << 20, transcendentals=0),
        name="attend_back",
    )(attn_low, w_full, raw, low, prev, stats, x, head_low, gain_q, gain_k, cosine, sine, gain_a)


def rotation_tables(length):
    half = HD // 2
    frequency = rope_theta ** (-np.arange(half) * 2.0 / HD)
    angles = np.arange(length)[:, None] * frequency[None, :]
    cosine, sine = np.cos(angles), np.sin(angles)
    return (
        jnp.asarray(np.concatenate([cosine, cosine], axis=1), f32),
        jnp.asarray(np.concatenate([-sine, sine], axis=1), f32),
    )


def per_device(
    tokens, w_query, w_key, w_value, w_output, w_gate, w_up, w_down,
    gain_query, gain_key, gain_attn, gain_mlp, cotangent,
):
    micro_count, rows, width = tokens.shape
    local = w_query.shape[1]
    ctx = lax.axis_size("ctx")
    tp = lax.axis_size("tp")
    cosine, sine = rotation_tables(rows * ctx)
    gain_q = gain_query.astype(f32)
    gain_k = gain_key.astype(f32)
    gain_a = gain_attn.astype(f32)
    gain_m = gain_mlp.astype(f32)
    xy = ("fsdp", "ctx")

    def gather(w):
        return lax.all_gather(w, xy, axis=0, tiled=True)

    w_g = gather(w_gate)
    w_u = gather(w_up)
    w_down_t = gather(w_down.T)

    def rms(a):
        return lax.rsqrt(jnp.mean(a * a, axis=-1, keepdims=True) + norm_eps)

    flat = (micro_count * rows, width)
    x_all, grad_all = tokens.reshape(flat), cotangent.reshape(flat)

    tables = (gain_q[None], gain_k[None], cosine, sine)
    n_xy = (lax.axis_size("fsdp"), ctx)
    raw, low, prev, head_low, stats, attention, mlp_in, w_full, attn_own = front(
        x_all, w_query, w_key, w_value, w_output.T, gain_q[None], gain_k[None], gain_a[None], cosine, sine,
        micro_count, tp, n_xy
    )
    down, _, attn_low, mlp_weights, mixed_own, gain_m_sum, gain_a_sum = mlp(
        mlp_in, grad_all, attn_own, gain_m[None], gain_a[None], w_g, w_u, w_down_t, tp
    )
    att, down = attention.astype(f32), down.astype(f32)
    out = (x_all.astype(f32) + att * rms(att) * gain_a + down * rms(down) * gain_m).astype(bf16)

    def scatter(full):
        return lax.psum_scatter(full, xy, scatter_dimension=0, tiled=True).astype(f32)

    units = w_gate.shape[1]
    d_mlp = scatter(mlp_weights)
    d_down, d_gate, d_up = d_mlp[:, :units].T, d_mlp[:, units : 2 * units], d_mlp[:, 2 * units :]
    grad_qkv, gain_qk_sum, gain_a_tp, attn_weights = attend_back(
        attn_low, w_full, raw, low, prev, stats, x_all, head_low, *tables, gain_a_sum, micro_count, tp, ctx
    )
    gains = jnp.concatenate(
        [gain_qk_sum[0], gain_qk_sum[1], gain_a_tp[0], gain_m_sum[0]]
    ).reshape(8, (local + width) // 4)
    grad_tokens, gains, d_attn = input_grad(
        grad_qkv, w_full, mixed_own, gains, attn_weights, tp, n_xy
    )
    gains = gains.reshape(2 * (local + width))
    return (
        out.reshape(tokens.shape),
        grad_tokens.reshape(tokens.shape),
        d_attn[:, 2 * local : 3 * local], d_attn[:, local : 2 * local], d_attn[:, :local],
        d_attn[:, 3 * local :].T, d_gate, d_up, d_down,
        gains[:local], gains[local : 2 * local],
        gains[2 * local : 2 * local + width], gains[2 * local + width :],
    )


def solution(mesh):
    rows, cols = P(("fsdp", "ctx"), "tp"), P("tp", ("fsdp", "ctx"))
    acts = P("fsdp", "ctx", None)
    in_specs = (acts, rows, rows, rows, cols, rows, rows, cols, P("tp"), P("tp"), P(), P(), acts)
    out_specs = (acts, acts, rows, rows, rows, cols, rows, rows, cols, P("tp"), P("tp"), P(), P())
    return jax.shard_map(
        per_device, mesh=mesh, in_specs=in_specs, out_specs=out_specs, check_vma=False
    )
```

```python
import functools

import jax
import jax.numpy as jnp
import numpy as np
from jax import lax
from jax.experimental import pallas as pl
from jax.experimental.pallas import tpu as pltpu
from jax.sharding import PartitionSpec as P

HD = 128
norm_eps = 1e-06
rope_theta = 500000.0
masked_value = -1e30
f32 = jnp.float32
bf16 = jnp.bfloat16


def dot(a, b, dims, out=f32):
    return lax.dot_general(a, b, (dims, ((), ())), preferred_element_type=f32).astype(out)


PIECE = 16
LAG = 1
CHUNK = 256
TILE_ROWS = 256
EXTRA = 4
TILE_COLUMNS = 2048
WEIGHT_ROWS = 256
WEIGHT_TILES = 2
MLP_TILE = 1024
TILES_PER_TICK = 3


class Line:
    def __init__(self, axis, n, groups, buf, total, send, recv):
        self.axis, self.n, self.groups = axis, n, groups
        self.buf, self.total, self.send, self.recv = buf, total, send, recv
        self.i = lax.axis_index(axis)
        self.stages = 2 * n - 1

    def rows(self, group, c, count=1):
        return pl.ds(pl.multiple_of((group * self.n + c) * PIECE, PIECE), count * PIECE)

    def copy(self, way, step, group, c, source):
        rows = self.rows(group, c)
        return pltpu.make_async_remote_copy(
            src_ref=self.buf.at[source, rows],
            dst_ref=self.buf.at[0 if way == 0 else 2, rows],
            send_sem=self.send.at[way, step, group],
            recv_sem=self.recv.at[way, step, group],
            device_id={self.axis: self.i + (1 if way == 0 else -1)},
            device_id_type=pl.DeviceIdType.MESH,
        )

    def add(self, c, group, source):
        rows = self.rows(group, c)
        both = self.buf[1, rows].astype(f32) + self.buf[source, rows].astype(f32)
        self.buf[1, rows] = both.astype(bf16)

    def reduce_step(self, s, group):
        i, n = self.i, self.n

        @pl.when(i <= min(s - 1, n - 2))
        def _():
            c = n - s + i
            if s >= 2:

                @pl.when(i >= 1)
                def _():
                    self.copy(0, s - 2, group, c, 1).wait_recv()
                    self.add(c, group, 0)

            self.copy(0, s - 1, group, c, 1).start()

        @pl.when(i >= max(n - s, 1))
        def _():
            c = s + i - n
            if s >= 2:

                @pl.when(i <= n - 2)
                def _():
                    self.copy(1, s - 2, group, c, 1).wait_recv()
                    self.add(c, group, 2)

            self.copy(1, s - 1, group, c, 1).start()

    def finish(self, group, then):
        i, n = self.i, self.n
        rows = self.rows(group, i)
        self.total[...] = self.buf[1, rows].astype(f32)

        @pl.when(i >= 1)
        def _():
            self.copy(0, n - 2, group, i, 1).wait_recv()
            self.total[...] += self.buf[0, rows].astype(f32)

        @pl.when(i <= n - 2)
        def _():
            self.copy(1, n - 2, group, i, 1).wait_recv()
            self.total[...] += self.buf[2, rows].astype(f32)

        self.buf[1, rows] = then(group, self.total[...]).astype(bf16)

        @pl.when(i <= n - 2)
        def _():
            self.copy(0, n - 1, group, i, 1).start()

        @pl.when(i >= 1)
        def _():
            self.copy(1, n - 1, group, i, 1).start()

    def gather_step(self, s, group):
        i, n = self.i, self.n

        @pl.when(i >= s - 1)
        def _():
            c = i - s + 1
            self.copy(0, n + s - 3, group, c, 0).wait_recv()
            if s <= n - 1:

                @pl.when(i <= n - 2)
                def _():
                    self.copy(0, n + s - 2, group, c, 0).start()

        @pl.when(i <= n - s)
        def _():
            c = i + s - 1
            self.copy(1, n + s - 3, group, c, 2).wait_recv()
            if s <= n - 1:

                @pl.when(i >= 1)
                def _():
                    self.copy(1, n + s - 2, group, c, 2).start()

    def sent(self, group):
        i, n = self.i, self.n
        for s in range(1, n):

            @pl.when(i <= min(s - 1, n - 2))
            def _():
                self.copy(0, s - 1, group, n - s + i, 1).wait_send()

            @pl.when(i >= max(n - s, 1))
            def _():
                self.copy(1, s - 1, group, s + i - n, 1).wait_send()

            @pl.when((i >= s - 1) & (i <= n - 2))
            def _():
                self.copy(0, n + s - 2, group, i - s + 1, 1 if s == 1 else 0).wait_send()

            @pl.when((i <= n - s) & (i >= 1))
            def _():
                self.copy(1, n + s - 2, group, i + s - 1, 1 if s == 1 else 2).wait_send()

    def piece(self, group, c):
        slot = jnp.where(c < self.i, 0, jnp.where(c > self.i, 2, 1))
        return self.buf[slot, self.rows(group, c)]

    def piece_ref(self, group, c):
        slot = jnp.where(c < self.i, 0, jnp.where(c > self.i, 2, 1))
        return self.buf.at[slot, self.rows(group, c)]

    def tick(self, t, then, done):
        n = self.n

        def stage(index, body):
            group = t - index * LAG

            @pl.when((group >= 0) & (group < self.groups))
            def _():
                body(group)

        for s in range(1, n):
            stage(s - 1, functools.partial(self.reduce_step, s))
        stage(n - 1, lambda group: self.finish(group, then))
        for s in range(2, n):
            stage(n + s - 2, functools.partial(self.gather_step, s))

        def last(group):
            self.gather_step(n, group)
            self.sent(group)
            done(group)

        stage(2 * n - 2, last)

    def ticks(self):
        return self.groups + (2 * self.n - 2) * LAG


def greet(axis, n, others=()):
    i = lax.axis_index(axis)
    barrier = pltpu.get_barrier_semaphore()
    for peer in others:
        pl.semaphore_signal(barrier, inc=1, device_id=peer, device_id_type=pl.DeviceIdType.MESH)

    @pl.when(i >= 1)
    def _():
        pl.semaphore_signal(barrier, inc=1, device_id={axis: i - 1}, device_id_type=pl.DeviceIdType.MESH)

    @pl.when(i <= n - 2)
    def _():
        pl.semaphore_signal(barrier, inc=1, device_id={axis: i + 1}, device_id_type=pl.DeviceIdType.MESH)

    pl.semaphore_wait(barrier, len(others) + jnp.minimum(i, 1) + jnp.minimum(n - 1 - i, 1))


def line_scratch(n, rows, width):
    sems = pltpu.SemaphoreType.DMA((2, 2 * n - 2, rows // (n * PIECE)))
    return [pltpu.VMEM((3, rows, width), bf16), pltpu.VMEM((PIECE, width), f32), sems, sems]


def params(collective_id):
    return pltpu.CompilerParams(
        collective_id=collective_id, has_side_effects=True, vmem_limit_bytes=63 << 20
    )


def scale_of(a):
    return lax.rsqrt(jnp.mean(a * a, axis=-1, keepdims=True) + norm_eps)


def local_copies(pairs, sems):
    copies = [pltpu.make_async_copy(a, b, sems.at[k]) for k, (a, b) in enumerate(pairs)]
    for copy in copies:
        copy.start()
    return copies


def mlp_kernel(
    n, mlp_in, grad, attn_own, gain_m, gain_a, w_g_hbm, w_u_hbm, w_d_hbm,
    down_out, hidden_out, attn_low_out, weights_out, mixed_own, gain_m_sum, gain_a_sum,
    buf, total, send, recv, w_g, w_u, w_d, mlp_rows, hidden, down_low, gate, up,
    ready, w_sems, io_sems, piece_sems, tile_sems, gain_m_acc, gain_a_acc,
):
    rows, width = grad.shape
    units = w_g.shape[1]
    groups = rows // (n * PIECE)
    per_chunk = CHUNK // (n * PIECE)
    line = Line("tp", n, groups, buf, total, send, recv)
    i = line.i
    tile = MLP_TILE

    def weight_copies(j):
        cols = pl.ds(pl.multiple_of(j * tile, tile), tile)
        return [
            pltpu.make_async_copy(w_g_hbm.at[:, cols], w_g.at[:, cols], w_sems.at[0, j]),
            pltpu.make_async_copy(w_u_hbm.at[:, cols], w_u.at[:, cols], w_sems.at[1, j]),
        ]

    for j in range(units // tile):
        for copy in weight_copies(j):
            copy.start()
    down_weights = pltpu.make_async_copy(w_d_hbm, w_d, w_sems.at[2, 0])
    down_weights.start()
    gain_m_acc[...] = jnp.zeros_like(gain_m_acc)
    gain_a_acc[...] = jnp.zeros_like(gain_a_acc)
    greet("tp", n)
    offset = per_chunk + line.stages + EXTRA

    def chunk_rows(chunk):
        return pl.ds(pl.multiple_of(chunk * CHUNK, CHUNK), CHUNK)

    def hidden_copy(chunk):
        return pltpu.make_async_copy(hidden, hidden_out.at[chunk_rows(chunk)], io_sems.at[1])

    def forward(chunk, first=False):
        at = chunk_rows(chunk)
        fetch = pltpu.make_async_copy(mlp_in.at[at], mlp_rows, io_sems.at[0])
        fetch.start()
        if not first:
            hidden_copy(chunk - 1).wait()
        fetch.wait()

        @pl.loop(0, units // tile)
        def _(j):
            if first:
                for copy in weight_copies(j):
                    copy.wait()
            cols = pl.ds(pl.multiple_of(j * tile, tile), tile)
            gate_proj = dot(mlp_rows[...], w_g[:, cols], ((1,), (0,)))
            up_proj = dot(mlp_rows[...], w_u[:, cols], ((1,), (0,)))
            gate[at, cols] = gate_proj.astype(bf16)
            up[at, cols] = up_proj.astype(bf16)
            hidden[:, cols] = (gate_proj / (1.0 + jnp.exp(-gate_proj)) * up_proj).astype(bf16)

        hidden_copy(chunk).start()

    def forward_down(chunk):
        at = chunk_rows(chunk)

        @pl.loop(0, width // tile)
        def _(j):
            cols = pl.ds(pl.multiple_of(j * tile, tile), tile)
            buf[1, at, cols] = dot(hidden[...], w_d[cols], ((1,), (1,)), bf16)

    def backward(chunk):
        at = chunk_rows(chunk)

        @pl.loop(0, units // tile)
        def _(j):
            cols = pl.ds(pl.multiple_of(j * tile, tile), tile)
            gate_proj, up_proj = gate[at, cols].astype(f32), up[at, cols].astype(f32)
            sig = 1.0 / (1.0 + jnp.exp(-gate_proj))
            grad_hidden = dot(down_low[at], w_d[:, cols], ((1,), (0,)))
            up[at, cols] = (grad_hidden * gate_proj * sig).astype(bf16)
            gate[at, cols] = (grad_hidden * up_proj * sig * (1.0 + gate_proj * (1.0 - sig))).astype(bf16)

    def backward_in(chunk):
        at = chunk_rows(chunk)

        @pl.loop(0, width // tile)
        def _(j):
            cols = pl.ds(pl.multiple_of(j * tile, tile), tile)
            buf[1, at, cols] = (
                dot(gate[at], w_g[cols], ((1,), (1,))) + dot(up[at], w_u[cols], ((1,), (1,)))
            ).astype(bf16)

    whole = pl.ds(0, rows)
    late_in = [(hidden_out, w_g.at[whole]), (mlp_in, w_u.at[whole])]
    per_part = width // TILE_ROWS

    def tile_copy(k, slot):
        part, block = lax.div(k, per_part), lax.rem(k, per_part)
        return pltpu.make_async_copy(
            w_d.at[pl.ds(pl.multiple_of(slot * TILE_ROWS, TILE_ROWS), TILE_ROWS)],
            weights_out.at[
                pl.ds(pl.multiple_of(block * TILE_ROWS, TILE_ROWS), TILE_ROWS),
                pl.ds(pl.multiple_of(part * units, units), units),
            ],
            tile_sems.at[slot],
        )

    def weight_tile(k):
        slot = lax.rem(k, 2)
        block = pl.ds(pl.multiple_of(lax.rem(k, per_part) * TILE_ROWS, TILE_ROWS), TILE_ROWS)

        @pl.when(k >= 2)
        def _():
            tile_copy(k - 2, slot).wait()

        def fill(left, right):
            @pl.loop(0, units // TILE_COLUMNS)
            def _(j):
                cols = pl.ds(pl.multiple_of(j * TILE_COLUMNS, TILE_COLUMNS), TILE_COLUMNS)
                w_d[pl.ds(pl.multiple_of(slot * TILE_ROWS, TILE_ROWS), TILE_ROWS), cols] = dot(
                    left[whole, block], right[whole, cols], ((0,), (0,)), bf16
                )

        @pl.when(k < per_part)
        def _():
            fill(down_low, w_g)

        @pl.when((k >= per_part) & (k < 2 * per_part))
        def _():
            fill(w_u, gate)

        @pl.when(k >= 2 * per_part)
        def _():
            fill(w_u, up)

        tile_copy(k, slot).start()

    def let_in():
        @pl.when(i >= 1)
        def _():
            pl.semaphore_signal(
                ready.at[1], inc=1, device_id={"tp": i - 1}, device_id_type=pl.DeviceIdType.MESH
            )

        @pl.when(i <= n - 2)
        def _():
            pl.semaphore_signal(
                ready.at[0], inc=1, device_id={"tp": i + 1}, device_id_type=pl.DeviceIdType.MESH
            )

    def pieces_out(group, out):
        return local_copies([(line.piece_ref(group, c), out.at[line.rows(group, c)]) for c in range(n)], piece_sems)

    def down_done(group):
        copies = pieces_out(group, down_out)
        for c in range(n):
            at = line.rows(group, c)
            branch = line.piece(group, c).astype(f32)
            r = scale_of(branch)
            g = grad[at].astype(f32)
            scaled = g * gain_m[...]
            inner = jnp.mean(scaled * branch, axis=-1, keepdims=True)
            gain_m_acc[...] += g * branch * r
            down_low[at] = (r * scaled - branch * (r * r * r) * inner).astype(bf16)
        for copy in copies:
            copy.wait()

    def attn_grad(group, total):
        at = pl.ds(pl.multiple_of(group * PIECE, PIECE), PIECE)
        mixed = grad[line.rows(group, i)].astype(f32) + total
        mixed_own[at] = mixed
        branch = attn_own[at].astype(f32)
        r = scale_of(branch)
        scaled = mixed * gain_a[...]
        inner = jnp.mean(scaled * branch, axis=-1, keepdims=True)
        gain_a_acc[...] += mixed * branch * r
        return r * scaled - branch * (r * r * r) * inner

    def attn_done(group):
        for copy in pieces_out(group, attn_low_out):
            copy.wait()

    forward(0, True)
    down_weights.wait()
    forward_down(0)

    @pl.loop(0, offset + line.ticks())
    def _(t):
        back = t - offset

        @pl.when((back >= 0) & (back < groups) & (lax.rem(back + groups, per_chunk) == 0))
        def _():
            @pl.when(i >= 1)
            def _():
                pl.semaphore_wait(ready.at[0], 1)

            @pl.when(i <= n - 2)
            def _():
                pl.semaphore_wait(ready.at[1], 1)

        line.tick(back, attn_grad, attn_done)
        line.tick(t, lambda group, total: total, down_done)
        for ahead, work in ((2, forward), (1, forward_down)):
            due = t + ahead

            @pl.when((due >= per_chunk) & (due < groups) & (lax.rem(due, per_chunk) == 0))
            def _():
                work(lax.div(due, per_chunk))

        for ahead, work in ((2, backward), (1, backward_in)):
            due = t + ahead - offset

            @pl.when((due >= 0) & (due < groups) & (lax.rem(due + groups, per_chunk) == 0))
            def _():
                if ahead == 1:
                    let_in()
                work(lax.div(due, per_chunk))

        first_tick = offset + groups - per_chunk

        def late_copies():
            return [pltpu.make_async_copy(a, b, io_sems.at[k]) for k, (a, b) in enumerate(late_in)]

        @pl.when(t == first_tick - 1)
        def _():
            hidden_copy(rows // CHUNK - 1).wait()
            for copy in late_copies():
                copy.start()

        @pl.when(t == first_tick)
        def _():
            for copy in late_copies():
                copy.wait()

        for m in range(TILES_PER_TICK):
            k = (t - first_tick) * TILES_PER_TICK + m

            @pl.when((k >= 0) & (k < 3 * per_part))
            def _():
                weight_tile(k)

    for k in (3 * per_part - 2, 3 * per_part - 1):
        tile_copy(k, k % 2).wait()
    gain_m_sum[...] = jnp.sum(gain_m_acc[...], axis=0, keepdims=True)
    gain_a_sum[...] = jnp.sum(gain_a_acc[...], axis=0, keepdims=True)


def mlp(mlp_in, grad, attn_own, gain_m, gain_a, w_g, w_u, w_d, n):
    rows, width = grad.shape
    units = w_g.shape[1]
    vmem, anywhere = pl.BlockSpec(memory_space=pltpu.VMEM), pl.BlockSpec(memory_space=pl.ANY)
    acts = jax.ShapeDtypeStruct((rows, width), bf16)
    inner = jax.ShapeDtypeStruct((rows, units), bf16)
    gain_shape = jax.ShapeDtypeStruct((1, width), f32)
    return pl.pallas_call(
        functools.partial(mlp_kernel, n),
        out_shape=[
            acts, inner, acts, jax.ShapeDtypeStruct((width, 3 * units), bf16),
            jax.ShapeDtypeStruct((rows // n, width), f32), gain_shape, gain_shape,
        ],
        in_specs=[anywhere] + [vmem] * 4 + [anywhere] * 3,
        out_specs=[anywhere] * 4 + [vmem] * 3,
        scratch_shapes=line_scratch(n, rows, width) + [
            pltpu.VMEM(w_g.shape, bf16), pltpu.VMEM(w_u.shape, bf16), pltpu.VMEM(w_d.shape, bf16),
            pltpu.VMEM((CHUNK, width), bf16), pltpu.VMEM((CHUNK, units), bf16), pltpu.VMEM((rows, width), bf16),
            pltpu.VMEM((rows, units), bf16), pltpu.VMEM((rows, units), bf16),
            pltpu.SemaphoreType.REGULAR((2,)),
            pltpu.SemaphoreType.DMA((3, units // 512)), pltpu.SemaphoreType.DMA((2,)), pltpu.SemaphoreType.DMA((n,)),
            pltpu.SemaphoreType.DMA((2,)),
            pltpu.VMEM((PIECE, width), f32), pltpu.VMEM((PIECE, width), f32),
        ],
        compiler_params=params(2),
        cost_estimate=pl.CostEstimate(flops=200 * 10**9, bytes_accessed=60 << 20, transcendentals=0),
        name="mlp",
    )(mlp_in, grad, attn_own, gain_m, gain_a, w_g, w_u, w_d)


def peers_of(axis, n):
    i = lax.axis_index(axis)
    return [(k - 1, lax.rem(i + k, n)) for k in range(1, n)]


def meet(axes, others=()):
    barrier = pltpu.get_barrier_semaphore()
    count = len(others)
    for peer in others:
        pl.semaphore_signal(barrier, inc=1, device_id=peer, device_id_type=pl.DeviceIdType.MESH)
    for axis, n in axes:
        for _, peer in peers_of(axis, n):
            pl.semaphore_signal(barrier, inc=1, device_id={axis: peer}, device_id_type=pl.DeviceIdType.MESH)
            count += 1
    pl.semaphore_wait(barrier, count)


def swap(axis, n, pairs, send, recv):
    copies = []
    for k, (mine, theirs) in enumerate(pairs):
        for slot, peer in peers_of(axis, n):
            copy = pltpu.make_async_remote_copy(
                src_ref=mine, dst_ref=theirs.at[slot],
                send_sem=send.at[k, slot], recv_sem=recv.at[k, slot],
                device_id={axis: peer}, device_id_type=pl.DeviceIdType.MESH,
            )
            copy.start()
            copies.append(copy)
    for copy in copies:
        copy.wait()


def lanes_to_rows(columns):
    return jnp.transpose(columns)[:8]


def rows_to_lanes(packed):
    rows = packed.shape[1]
    return jnp.transpose(jnp.concatenate([packed, jnp.zeros((120, rows), f32)], axis=0))


def two_lanes(first, second):
    lane = lax.broadcasted_iota(jnp.int32, (first.shape[0], 128), 1)
    return jnp.where(lane == 0, first, jnp.where(lane == 1, second, 0.0))


def turn(values, cosine, sine):
    return values * cosine + pltpu.roll(values, HD // 2, 1) * sine


def heads_loop(heads, body):
    @pl.loop(0, heads)
    def _(h):
        body(h, lambda part, width: pl.ds(pl.multiple_of(part * width + h * HD, HD), HD))


class Gather:
    def __init__(self, n_xy, parts, full, local_sems, sems):
        n_fsdp, self.n_ctx = n_xy
        self.chips = n_fsdp // 2
        self.parts, self.full, self.local_sems, self.sems = parts, full, local_sems, sems
        fsdp = lax.axis_index("fsdp")
        self.chip, self.core = lax.div(fsdp, 2), lax.rem(fsdp, 2)
        self.ctx = lax.axis_index("ctx")
        self.block = parts[0].shape[0]

    def place(self, part, chip, core, ctx):
        columns = self.parts[part].shape[1]
        first = sum(p.shape[1] for p in self.parts[:part])
        row = ((2 * chip + core) * self.n_ctx + ctx) * self.block
        return self.full.at[pl.ds(pl.multiple_of(row, self.block), self.block), pl.ds(first, columns)]

    def send(self, part, slot, source, target, device):
        return pltpu.make_async_remote_copy(
            src_ref=source, dst_ref=target,
            send_sem=self.sems.at[0, part, slot], recv_sem=self.sems.at[1, part, slot],
            device_id=device, device_id_type=pl.DeviceIdType.MESH,
        )

    def keep(self, part):
        return pltpu.make_async_copy(
            self.parts[part], self.place(part, self.chip, self.core, self.ctx), self.local_sems.at[part]
        )

    def to_ctx(self, part, k):
        target = self.place(part, self.chip, self.core, self.ctx)
        return self.send(part, k - 1, self.parts[part], target, {"ctx": lax.rem(self.ctx + k, self.n_ctx)})

    def to_chip(self, part, c, k):
        ctx = lax.rem(self.ctx + self.n_ctx - c, self.n_ctx)
        target = self.place(part, self.chip, self.core, ctx)
        source = self.parts[part] if c == 0 else target
        slot = self.n_ctx - 1 + c * (self.chips - 1) + k - 1
        chip = lax.rem(self.chip + k, self.chips)
        return self.send(part, slot, source, target, {"fsdp": 2 * chip + self.core})

    def to_core(self, part, c, k):
        ctx = lax.rem(self.ctx + self.n_ctx - c, self.n_ctx)
        chip = lax.rem(self.chip + self.chips - k, self.chips)
        target = self.place(part, chip, self.core, ctx)
        source = self.parts[part] if c == 0 and k == 0 else target
        slot = self.n_ctx - 1 + self.n_ctx * (self.chips - 1) + c * self.chips + k
        return self.send(part, slot, source, target, {"fsdp": 2 * self.chip + 1 - self.core})

    def slots(self):
        return self.n_ctx - 1 + self.n_ctx * (self.chips - 1) + self.n_ctx * self.chips

    def start(self, part):
        self.keep(part).start()
        for k in range(1, self.n_ctx):
            self.to_ctx(part, k).start()
        for k in range(1, self.chips):
            self.to_chip(part, 0, k).start()
        self.to_core(part, 0, 0).start()

    def pass_on(self, part):
        for c in range(1, self.n_ctx):
            self.to_ctx(part, c).wait_recv()
            for k in range(1, self.chips):
                self.to_chip(part, c, k).start()
            self.to_core(part, c, 0).start()
        for c in range(self.n_ctx):
            for k in range(1, self.chips):
                self.to_chip(part, c, k).wait_recv()
                self.to_core(part, c, k).start()

    def end(self, part):
        for c in range(self.n_ctx):
            for k in range(self.chips):
                self.to_core(part, c, k).wait_recv()
        self.keep(part).wait()

    def sent(self, part):
        for k in range(1, self.n_ctx):
            self.to_ctx(part, k).wait_send()
        for c in range(self.n_ctx):
            for k in range(1, self.chips):
                self.to_chip(part, c, k).wait_send()
            for k in range(self.chips):
                self.to_core(part, c, k).wait_send()


def front_kernel(
    n_tp, n_xy, seqs, x_hbm, w_q, w_k, w_v, w_o, gain_q, gain_k, gain_a, cosine, sine,
    raw_out, low_out, prev_out, head_low_out, stats_out, attention_out, mlp_in_out, w_out, attn_own_out,
    buf, total, send, recv, x, w, raw, low, prev, head_low, stats, mlp_in, attn_own,
    sums, theirs, kv_send, kv_recv, sum_send, sum_recv, w_local_sems, w_sems, io_sems, piece_sems, group_sems,
):
    n_ctx = n_xy[1]
    rows_all, width = x.shape
    rows = rows_all // seqs
    local = w_q.shape[1]
    heads = local // HD
    me = lax.axis_index("ctx")
    scale = HD ** (-0.5)
    step = min(256, rows)
    fetch_x = pltpu.make_async_copy(x_hbm, x, io_sems.at[0])
    fetch_x.start()
    gather = Gather(n_xy, [w_v, w_k, w_q, w_o], w, w_local_sems, w_sems)
    value_at, key_at, query_at, out_at = 0, local, 2 * local, 3 * local
    fsdp = lax.axis_index("fsdp")
    meet(
        [("tp", n_tp), ("ctx", n_ctx)],
        [{"fsdp": 2 * lax.div(fsdp, 2) + 1 - lax.rem(fsdp, 2)}]
        + [{"fsdp": lax.rem(fsdp + 2 * k, n_xy[0])} for k in range(1, n_xy[0] // 2)],
    )
    for part in range(4):
        gather.start(part)

    def chunks(body):
        @pl.loop(0, rows_all // step)
        def _(k):
            at = pl.ds(pl.multiple_of(k * step, step), step)
            body(at, pl.ds(pl.multiple_of(me * rows + lax.rem(k, rows // step) * step, step), step))

    for j in range(1, n_ctx):

        @pl.when(me < j)
        def _():
            prev[j - 1] = jnp.zeros(prev.shape[1:], bf16)

    def kv_copy(j, part, seq):
        at = pl.ds(seq * rows, rows)
        return pltpu.make_async_remote_copy(
            src_ref=low.at[at, pl.ds((1 + part) * local, local)],
            dst_ref=prev.at[j - 1, at, pl.ds(part * local, local)],
            send_sem=kv_send.at[j - 1, part, seq], recv_sem=kv_recv.at[j - 1, part, seq],
            device_id={"ctx": lax.rem(me + j, n_ctx)}, device_id_type=pl.DeviceIdType.MESH,
        )

    def kv_each(method, part, seq, here):
        for j in range(1, n_ctx):

            @pl.when((me >= j) if here else (me + j < n_ctx))
            def _():
                getattr(kv_copy(j, part, seq), method)()

    gather.pass_on(0)
    gather.pass_on(1)
    gather.end(0)
    fetch_x.wait()

    def value_chunk(at, _):
        low[at, 2 * local :] = dot(x[at], w[:, value_at : value_at + local], ((1,), (0,)), bf16)

    chunks(value_chunk)
    for seq in range(seqs):
        kv_each("start", 1, seq, False)
    gather.pass_on(2)
    gather.end(1)

    def raw_chunk(part, first):
        def chunk(at, _):
            v = dot(x[at], w[:, first : first + local], ((1,), (0,)))
            raw[at, part * local : (part + 1) * local] = v
            square = jnp.sum(v * v, axis=-1, keepdims=True)
            lane = lax.broadcasted_iota(jnp.int32, (step, 128), 1)
            stats[at] = jnp.where(lane == part, square, stats[at] if part == 0 else 0.0)

        chunks(chunk)

    raw_chunk(1, key_at)
    gather.pass_on(3)
    gather.end(2)
    raw_chunk(0, query_at)

    def sums_chunk(at, _):
        sums[:, at] = lanes_to_rows(stats[at])

    chunks(sums_chunk)
    swap("tp", n_tp, [(sums, theirs)], sum_send, sum_recv)
    square_sums = sums[...]
    for slot in range(n_tp - 1):
        square_sums = square_sums + theirs[slot]
    stats[...] = rows_to_lanes(lax.rsqrt(square_sums / width + norm_eps))

    def turned(part, gain):
        def chunk(at, pos):
            r = stats[at, part : part + 1]
            for h in range(heads):
                cols = pl.ds(part * local + h * HD, HD)
                v = raw[at, cols] * r * gain[:, h * HD : (h + 1) * HD]
                low[at, cols] = turn(v, cosine[pos], sine[pos]).astype(bf16)

        chunks(chunk)

    turned(1, gain_k)
    for seq in range(seqs):
        kv_each("start", 0, seq, False)
    turned(0, gain_q)
    lane = lax.broadcasted_iota(jnp.int32, (step, 128), 1)

    def attention(seq):
        for part in range(2):
            kv_each("wait_recv", part, seq, True)
        seq_rows = pl.ds(seq * rows, rows)

        def one_head(h, cols):
            for tile in range(rows // step):
                at = pl.ds(seq * rows + tile * step, step)
                q = low[at, cols(0, local)]
                seen = (tile + 1) * step
                own = pl.ds(seq * rows, seen)
                s = dot(q, low[own, cols(1, local)], ((1,), (1,))) * scale
                i_pos = lax.broadcasted_iota(jnp.int32, (step, seen), 0) + tile * step
                j_pos = lax.broadcasted_iota(jnp.int32, (step, seen), 1)
                scores = [jnp.where(j_pos <= i_pos, s, masked_value)]
                values = [low[own, cols(2, local)]]
                for j in range(1, n_ctx):
                    s = dot(q, prev[j - 1, seq_rows, cols(0, local)], ((1,), (1,))) * scale
                    scores.append(jnp.where(me >= j, s, masked_value))
                    values.append(prev[j - 1, seq_rows, cols(1, local)])
                top = scores[0].max(-1, keepdims=True)
                for s in scores[1:]:
                    top = jnp.maximum(top, s.max(-1, keepdims=True))
                total, weighted = 0.0, 0.0
                for s, v in zip(scores, values):
                    e = jnp.exp(s - top)
                    total = total + e.sum(-1, keepdims=True)
                    weighted = weighted + dot(e.astype(bf16), v, ((1,), (0,)))
                head_low[at, cols(0, local)] = (weighted / total).astype(bf16)
                stats[at] = jnp.where(lane == h + 2, top + jnp.log(total), stats[at])

        heads_loop(heads, one_head)

    attention(0)
    gather.end(3)

    groups = rows_all // (n_tp * PIECE)
    line = Line("tp", n_tp, groups, buf, total, send, recv)
    per_chunk, per_seq = step // (n_tp * PIECE), rows // (n_tp * PIECE)
    tile = 512

    def group_rows(group):
        return pl.ds(pl.multiple_of(group * n_tp * PIECE, n_tp * PIECE), n_tp * PIECE)

    def mlp_copy(group):
        at = group_rows(group)
        return pltpu.make_async_copy(mlp_in.at[at], mlp_in_out.at[at], group_sems.at[group])

    def own(group, total):
        attn_own[pl.ds(pl.multiple_of(group * PIECE, PIECE), PIECE)] = total.astype(bf16)
        return total

    def done(group):
        copies = local_copies(
            [(line.piece_ref(group, c), attention_out.at[line.rows(group, c)]) for c in range(n_tp)], piece_sems
        )
        for c in range(n_tp):
            at = line.rows(group, c)
            a = line.piece(group, c).astype(f32)
            mlp_in[at] = (x[at].astype(f32) + a * scale_of(a) * gain_a[...]).astype(bf16)
        mlp_copy(group).start()
        for copy in copies:
            copy.wait()

    saves = [
        (raw, raw_out), (low, low_out), (prev, prev_out), (head_low, head_low_out), (stats, stats_out), (w, w_out),
    ]

    @pl.loop(0, line.ticks())
    def _(t):
        @pl.when((t < groups) & (lax.rem(t, per_chunk) == 0))
        def _():
            at = pl.ds(pl.multiple_of(t * n_tp * PIECE, step), step)

            @pl.loop(0, width // tile)
            def _(j):
                cols = pl.ds(pl.multiple_of(j * tile, tile), tile)
                buf[1, at, cols] = dot(head_low[at], w[cols, out_at : out_at + local], ((1,), (1,)), bf16)

        line.tick(t, own, done)
        for seq in range(1, seqs):

            @pl.when(t == seq * per_seq - 1)
            def _():
                attention(seq)

        @pl.when(t == (seqs - 1) * per_seq)
        def _():
            for k, (source, target) in enumerate(saves):
                pltpu.make_async_copy(source, target, io_sems.at[k]).start()

    own_out = pltpu.make_async_copy(attn_own, attn_own_out, piece_sems.at[0])
    own_out.start()
    for k, (source, target) in enumerate(saves):
        pltpu.make_async_copy(source, target, io_sems.at[k]).wait()
    own_out.wait()

    @pl.loop(0, groups)
    def _(group):
        mlp_copy(group).wait()

    for part in range(4):
        gather.sent(part)
    for seq in range(seqs):
        for part in range(2):
            kv_each("wait_send", part, seq, False)


def front(x, w_q, w_k, w_v, w_o, gain_q, gain_k, gain_a, cosine, sine, seqs, n_tp, n_xy):
    rows, width = x.shape
    local = w_q.shape[1]
    n_fsdp, n_ctx = n_xy
    chips = n_fsdp // 2
    vmem, anywhere = pl.BlockSpec(memory_space=pltpu.VMEM), pl.BlockSpec(memory_space=pl.ANY)
    shape = jax.ShapeDtypeStruct
    dma = pltpu.SemaphoreType.DMA
    saved = [
        shape((rows, 2 * local), f32), shape((rows, 3 * local), bf16),
        shape((max(n_ctx - 1, 1), rows, 2 * local), bf16),
        shape((rows, local), bf16), shape((rows, 128), f32),
    ]
    acts, full = shape(x.shape, bf16), shape((width, 4 * local), bf16)
    vmem_of = [pltpu.VMEM(a.shape, a.dtype) for a in saved]
    slots = n_ctx - 1 + n_ctx * (chips - 1) + n_ctx * chips
    kv_sems, sum_sems = dma((max(n_ctx - 1, 1), 2, seqs)), dma((1, n_tp - 1))
    return pl.pallas_call(
        functools.partial(front_kernel, n_tp, n_xy, seqs),
        out_shape=saved + [acts, acts, full, shape((rows // n_tp, width), bf16)],
        in_specs=[anywhere] + [vmem] * 9,
        out_specs=[anywhere] * 9,
        scratch_shapes=line_scratch(n_tp, rows, width) + [
            pltpu.VMEM(x.shape, bf16), pltpu.VMEM(full.shape, bf16), *vmem_of, pltpu.VMEM(x.shape, bf16),
            pltpu.VMEM((rows // n_tp, width), bf16),
            pltpu.VMEM((8, rows), f32), pltpu.VMEM((n_tp - 1, 8, rows), f32),
            kv_sems, kv_sems, sum_sems, sum_sems, dma((4,)), dma((2, 4, slots)), dma((7,)), dma((n_tp,)),
            dma((rows // (n_tp * PIECE),)),
        ],
        compiler_params=params(1),
        cost_estimate=pl.CostEstimate(flops=150 * 10**9, bytes_accessed=30 << 20, transcendentals=0),
        name="front",
    )(x, w_q, w_k, w_v, w_o, gain_q, gain_k, gain_a, cosine, sine)


class Owners:
    def __init__(self, n_xy, full, first, columns, pair_in, peer_in, stage, stage_sem, pair_sems, peer_sems):
        n_fsdp, self.n_ctx = n_xy
        self.chips = n_fsdp // 2
        self.first, self.columns = first, columns
        self.full, self.pair_in, self.peer_in = full, pair_in, peer_in
        self.stage, self.stage_sem = stage, stage_sem
        self.pair_sems, self.peer_sems = pair_sems, peer_sems
        fsdp = lax.axis_index("fsdp")
        self.chip, self.core = lax.div(fsdp, 2), lax.rem(fsdp, 2)
        self.place = self.chip * self.n_ctx + lax.axis_index("ctx")
        self.block = full.shape[0] // (n_fsdp * self.n_ctx)
        self.span = self.n_ctx * self.block

    def cols(self):
        return pl.ds(self.first, self.columns)

    def pair_copy(self, chip):
        there = 1 - self.core
        rows = pl.ds(pl.multiple_of((2 * chip + there) * self.span, self.span), self.span)
        return pltpu.make_async_remote_copy(
            src_ref=self.full.at[rows, self.cols()],
            dst_ref=self.pair_in.at[pl.ds(chip * self.span, self.span), self.cols()],
            send_sem=self.pair_sems.at[0, chip], recv_sem=self.pair_sems.at[1, chip],
            device_id={"fsdp": 2 * self.chip + there}, device_id_type=pl.DeviceIdType.MESH,
        )

    def peer_copy(self, k):
        place = lax.rem(self.place + k, self.chips * self.n_ctx)
        return pltpu.make_async_remote_copy(
            src_ref=self.pair_in.at[self.block_rows(place), self.cols()],
            dst_ref=self.peer_in.at[k - 1, :, self.cols()],
            send_sem=self.peer_sems.at[0, k - 1], recv_sem=self.peer_sems.at[1, k - 1],
            device_id={"fsdp": 2 * lax.div(place, self.n_ctx) + self.core, "ctx": lax.rem(place, self.n_ctx)},
            device_id_type=pl.DeviceIdType.MESH,
        )

    def block_rows(self, place):
        return pl.ds(pl.multiple_of(place * self.block, self.block), self.block)

    def start(self):
        for chip in range(self.chips):
            self.pair_copy(chip).start()

    def pass_on(self):
        unit = min(self.span, self.stage.shape[0])
        for chip in range(self.chips):
            for u in range(self.span // unit):
                mine = pl.multiple_of((2 * chip + self.core) * self.span + u * unit, unit)
                fetch = pltpu.make_async_copy(
                    self.full.at[pl.ds(mine, unit), self.cols()],
                    self.stage.at[pl.ds(0, unit), pl.ds(0, self.columns)], self.stage_sem,
                )
                fetch.start()
                if u == 0:
                    self.pair_copy(chip).wait_recv()
                fetch.wait()
                rows = pl.ds(chip * self.span + u * unit, unit)
                both = self.pair_in[rows, self.cols()].astype(f32) + self.stage[:unit, : self.columns].astype(f32)
                self.pair_in[rows, self.cols()] = both.astype(bf16)
        for k in range(1, self.chips * self.n_ctx):
            self.peer_copy(k).start()

    def end(self, result, width):
        for k in range(1, self.chips * self.n_ctx):
            self.peer_copy(k).wait()
        for part in range(self.first // width, (self.first + self.columns) // width):
            cols = pl.ds(part * width, width)
            sums = self.pair_in[self.block_rows(self.place), cols].astype(f32)
            for k in range(1, self.chips * self.n_ctx):
                sums = sums + self.peer_in[k - 1, :, cols].astype(f32)
            result[part * self.block : (part + 1) * self.block] = sums
        for chip in range(self.chips):
            self.pair_copy(chip).wait_send()


def back_kernel(
    n_tp, n_xy, seqs,
    attn_low_hbm, w_hbm, raw_hbm, low_hbm, prev_hbm, head_low_hbm, stats_hbm, x_hbm, mixed_own_hbm,
    attention_hbm, down_hbm, gain_q, gain_k, gain_a, gain_m, gain_a_own, gain_m_own, cosine, sine,
    grad_out, out_out, gains_sum, weights_own, weights_out,
    buf, total, send, recv, w, raw, low, kv, in_kv, head_low, stats, x, mixed_own, grad_heads, grad_q, grad_kv,
    grad_qkv, tiles, pair_in, peer_in, branches, outs, gains, gains_theirs, gain_qk,
    sums, theirs, gain_theirs, load_sems, kv_send, kv_recv, sum_send, sum_recv, tile_sems, stage_sem,
    pair_sems, peer_sems, gain_send, gain_recv, piece_sems, branch_sems, out_sems,
):
    n_fsdp, n_ctx = n_xy
    rows_all, width = x.shape
    rows = rows_all // seqs
    local = head_low.shape[1]
    heads = local // HD
    me = lax.axis_index("ctx")
    scale = HD ** (-0.5)
    step = min(256, rows)
    out_at = 3 * local
    groups = rows_all // (n_tp * PIECE)
    line = Line("tp", n_tp, groups, buf, total, send, recv)
    per_chunk, per_seq = step // (n_tp * PIECE), rows // (n_tp * PIECE)
    attn_low = buf.at[1]
    qkv_cols, out_cols = pl.ds(0, out_at), pl.ds(out_at, local)
    loads = local_copies(
        [
            (attn_low_hbm, attn_low), (w_hbm.at[:, out_cols], w.at[:, out_cols]), (prev_hbm, kv), (low_hbm, low),
            (head_low_hbm, head_low), (stats_hbm, stats), (raw_hbm, raw), (x_hbm, x),
            (w_hbm.at[:, qkv_cols], w.at[:, qkv_cols]), (mixed_own_hbm, mixed_own),
        ],
        load_sems,
    )
    place = lax.axis_index("fsdp") * n_ctx + me
    others = []
    for k in range(1, n_fsdp * n_ctx):
        peer = lax.rem(place + k, n_fsdp * n_ctx)
        others.append({"fsdp": lax.div(peer, n_ctx), "ctx": lax.rem(peer, n_ctx)})
    meet([("tp", n_tp)], others)

    def chunks(body, seq=None):
        count = rows_all if seq is None else rows
        first = 0 if seq is None else seq * rows

        @pl.loop(0, count // step)
        def _(k):
            at = pl.ds(pl.multiple_of(first + k * step, step), step)
            body(at, pl.ds(pl.multiple_of(me * rows + lax.rem(k, rows // step) * step, step), step))

    loads[0].wait()
    loads[1].wait()

    def heads_chunk(at, _):
        grad_heads[at] = dot(attn_low[at], w[:, out_cols], ((1,), (0,)), bf16)

    chunks(heads_chunk)
    grad_q[...] = jnp.zeros_like(grad_q)
    grad_kv[...] = jnp.zeros_like(grad_kv)
    gain_qk[...] = jnp.zeros_like(gain_qk)
    for load in loads[2:6]:
        load.wait()

    def kv_copy(j, seq):
        at = pl.ds(seq * rows, rows)
        return pltpu.make_async_remote_copy(
            src_ref=kv.at[j - 1, at], dst_ref=in_kv.at[j - 1, at],
            send_sem=kv_send.at[j - 1, seq], recv_sem=kv_recv.at[j - 1, seq],
            device_id={"ctx": lax.rem(me + n_ctx - j, n_ctx)}, device_id_type=pl.DeviceIdType.MESH,
        )

    def lane_of(at, index):
        lane = lax.broadcasted_iota(jnp.int32, (step, 128), 1)
        return jnp.sum(jnp.where(lane == index, stats[at], 0.0), axis=-1, keepdims=True)

    def block(h, cols, at, keys, values, mask):
        q, g = low[at, cols(0, local)], grad_heads[at, cols(0, local)]
        delta = jnp.sum(g.astype(f32) * head_low[at, cols(0, local)].astype(f32), axis=-1, keepdims=True)
        s = dot(q, keys, ((1,), (1,))) * scale
        p = jnp.exp(s - lane_of(at, h + 2))
        if mask is not None:
            p = jnp.where(mask, p, 0.0)
        dp = dot(g, values, ((1,), (1,)))
        ds = (p * (dp - delta)).astype(bf16)
        grad_q[at, cols(0, local)] += dot(ds, keys, ((1,), (0,))) * scale
        return dot(ds, q, ((0,), (0,))) * scale, dot(p.astype(bf16), g, ((0,), (0,)))

    for j in range(1, n_ctx):

        @pl.when(me >= j)
        def _():
            for seq in range(seqs):
                seq_rows = pl.ds(seq * rows, rows)

                def one_head(h, cols):
                    keys, values = kv[j - 1, seq_rows, cols(0, local)], kv[j - 1, seq_rows, cols(1, local)]
                    dk, dv = 0.0, 0.0
                    for tile in range(rows // step):
                        at = pl.ds(seq * rows + tile * step, step)
                        k_term, v_term = block(h, cols, at, keys, values, None)
                        dk, dv = dk + k_term, dv + v_term
                    kv[j - 1, seq_rows, cols(0, local)] = dk.astype(bf16)
                    kv[j - 1, seq_rows, cols(1, local)] = dv.astype(bf16)

                heads_loop(heads, one_head)
                kv_copy(j, seq).start()

    for seq in range(seqs):

        def one_head(h, cols):
            for tile in range(rows // step):
                at = pl.ds(seq * rows + tile * step, step)
                seen = (tile + 1) * step
                own = pl.ds(seq * rows, seen)
                i_pos = lax.broadcasted_iota(jnp.int32, (step, seen), 0) + tile * step
                j_pos = lax.broadcasted_iota(jnp.int32, (step, seen), 1)
                k_term, v_term = block(
                    h, cols, at, low[own, cols(1, local)], low[own, cols(2, local)], j_pos <= i_pos
                )
                grad_kv[own, cols(0, local)] += k_term
                grad_kv[own, cols(1, local)] += v_term

        heads_loop(heads, one_head)

    blocks = width // WEIGHT_ROWS

    def tile_copy(k, slot, first, columns):
        return pltpu.make_async_copy(
            tiles.at[slot, :, pl.ds(0, columns)],
            weights_out.at[
                pl.ds(pl.multiple_of(k * WEIGHT_ROWS, WEIGHT_ROWS), WEIGHT_ROWS), pl.ds(first, columns)
            ],
            tile_sems.at[slot],
        )

    def weight_tile(k, left, right, first, columns):
        slot = lax.rem(k, 2)

        @pl.when(k >= 2)
        def _():
            tile_copy(k - 2, slot, first, columns).wait()

        at = pl.ds(pl.multiple_of(k * WEIGHT_ROWS, WEIGHT_ROWS), WEIGHT_ROWS)
        tiles[slot, :, :columns] = dot(left[:, at], right[...], ((0,), (0,)), bf16)
        tile_copy(k, slot, first, columns).start()

    def tiles_end(first, columns):
        for k in (blocks - 2, blocks - 1):
            tile_copy(k, k % 2, first, columns).wait()

    def owners(index, first, columns):
        return Owners(
            n_xy, weights_out, first, columns, pair_in, peer_in, low, stage_sem,
            pair_sems.at[index], peer_sems.at[index],
        )

    owners_out, owners_qkv = owners(0, out_at, local), owners(1, 0, out_at)

    @pl.loop(0, blocks)
    def _(k):
        weight_tile(k, attn_low, head_low, out_at, local)

    tiles_end(out_at, local)
    owners_out.start()
    for load in loads[6:]:
        load.wait()

    def turned(at, pos, part, ref, gain):
        inner = 0.0
        for h in range(heads):
            cols = pl.ds(h * HD, HD)
            d = turn(ref[at, cols], cosine[pos], -sine[pos])
            ref[at, cols] = d
            weighted = d * raw[at, pl.ds(part * local + h * HD, HD)] * gain[:, h * HD : (h + 1) * HD]
            inner = inner + jnp.sum(weighted, axis=-1, keepdims=True)
        return inner

    def norm_back(seq):
        for j in range(1, n_ctx):

            @pl.when(me + j < n_ctx)
            def _():
                kv_copy(j, seq).wait_recv()
                at = pl.ds(seq * rows, rows)
                grad_kv[at] += in_kv[j - 1, at].astype(f32)

        def inner_chunk(at, pos):
            both = two_lanes(turned(at, pos, 0, grad_q, gain_q), turned(at, pos, 1, grad_kv, gain_k))
            sums[:, at] = lanes_to_rows(both)

        chunks(inner_chunk, seq)
        seq_rows = pl.ds(seq * rows, rows)
        pairs = [(sums.at[:, seq_rows], theirs.at[:, :, seq_rows])]
        if seq == 0:
            pairs.append((gain_a_own, gain_theirs))
        swap("tp", n_tp, pairs, sum_send.at[seq], sum_recv.at[seq])
        inner_sums = sums[:, seq_rows]
        for slot in range(n_tp - 1):
            inner_sums = inner_sums + theirs[slot, :, seq_rows]
        sums[:, seq_rows] = inner_sums / width

        def out_chunk(at, _):
            inner = rows_to_lanes(sums[:, at])
            for part, ref, gain in ((0, grad_q, gain_q), (1, grad_kv, gain_k)):
                r = stats[at, part : part + 1]
                d, v = ref[at, :local], raw[at, pl.ds(part * local, local)]
                grad_qkv[at, pl.ds((2 - part) * local, local)] = (
                    d * r * gain[...] - v * (r * r * r) * inner[:, part : part + 1]
                ).astype(bf16)
                gain_qk[part : part + 1] += jnp.sum(d * v * r, axis=0, keepdims=True)
            grad_qkv[at, :local] = grad_kv[at, local:].astype(bf16)

        chunks(out_chunk, seq)

    def gain_copies():
        return [
            pltpu.make_async_remote_copy(
                src_ref=gains, dst_ref=gains_theirs.at[k], send_sem=gain_send.at[k], recv_sem=gain_recv.at[k],
                device_id=peer, device_id_type=pl.DeviceIdType.MESH,
            )
            for k, peer in enumerate(others)
        ]

    def send_gains():
        gains[:, :local] = gain_qk[0:1]
        gains[:, local : 2 * local] = gain_qk[1:2]
        gain_total = gain_a_own[...]
        for slot in range(n_tp - 1):
            gain_total = gain_total + gain_theirs[slot]
        gains[:, 2 * local : 2 * local + width] = gain_total
        gains[:, 2 * local + width :] = gain_m_own[...]
        for copy in gain_copies():
            copy.start()

    norm_back(0)
    if seqs == 1:
        send_gains()

    span = n_tp * PIECE

    def group_rows(group):
        return pl.ds(pl.multiple_of(group * span, span), span)

    def branch_copies(group):
        at, slot = group_rows(group), lax.rem(group, 4)
        return [
            pltpu.make_async_copy(attention_hbm.at[at], branches.at[slot, 0], branch_sems.at[slot, 0]),
            pltpu.make_async_copy(down_hbm.at[at], branches.at[slot, 1], branch_sems.at[slot, 1]),
        ]

    def out_copy(group):
        slot = lax.rem(group, 2)
        return pltpu.make_async_copy(outs.at[slot], out_out.at[group_rows(group)], out_sems.at[slot])

    def own(group, total):
        for copy in branch_copies(group):
            copy.start()
        return total + mixed_own[pl.ds(pl.multiple_of(group * PIECE, PIECE), PIECE)]

    def done(group):
        copies = local_copies(
            [(line.piece_ref(group, c), grad_out.at[line.rows(group, c)]) for c in range(n_tp)], piece_sems
        )
        for copy in branch_copies(group):
            copy.wait()

        @pl.when(group >= 2)
        def _():
            out_copy(group - 2).wait()

        slot = lax.rem(group, 4)
        a, d = branches[slot, 0].astype(f32), branches[slot, 1].astype(f32)
        mixed = x[group_rows(group)].astype(f32) + a * scale_of(a) * gain_a[...]
        outs[lax.rem(group, 2)] = (mixed + d * scale_of(d) * gain_m[...]).astype(bf16)
        out_copy(group).start()
        for copy in copies:
            copy.wait()

    tile = 1024
    weights_tick = (seqs - 1) * per_seq
    weights_ticks = -(-blocks // WEIGHT_TILES)

    @pl.loop(0, line.ticks())
    def _(t):
        @pl.when((t < groups) & (lax.rem(t, per_chunk) == 0))
        def _():
            at = pl.ds(pl.multiple_of(t * span, step), step)

            @pl.loop(0, width // tile)
            def _(j):
                cols = pl.ds(pl.multiple_of(j * tile, tile), tile)
                buf[1, at, cols] = dot(grad_qkv[at], w[cols, qkv_cols], ((1,), (1,)), bf16)

        line.tick(t, own, done)

        @pl.when(t == 0)
        def _():
            owners_out.pass_on()

        for seq in range(1, seqs):

            @pl.when(t == seq * per_seq - 1)
            def _():
                norm_back(seq)
                if seq == seqs - 1:
                    send_gains()

        for m in range(WEIGHT_TILES):
            k = (t - weights_tick) * WEIGHT_TILES + m

            @pl.when((k >= 0) & (k < blocks))
            def _():
                weight_tile(k, x, grad_qkv, 0, out_at)

        @pl.when(t == weights_tick + weights_ticks - 1)
        def _():
            tiles_end(0, out_at)
            owners_qkv.start()

        @pl.when(t == weights_tick + weights_ticks)
        def _():
            owners_qkv.pass_on()

    for group in (groups - 2, groups - 1):
        out_copy(group).wait()
    gains_sum[...] = gains[...]
    for k, copy in enumerate(gain_copies()):
        copy.wait()
        gains_sum[...] += gains_theirs[k]
    owners_out.end(grad_q, local)
    owners_qkv.end(grad_q, local)
    result = pltpu.make_async_copy(grad_q.at[pl.ds(0, weights_own.shape[0])], weights_own, stage_sem)
    result.start()
    result.wait()
    for j in range(1, n_ctx):
        for seq in range(seqs):

            @pl.when(me >= j)
            def _():
                kv_copy(j, seq).wait_send()


def back(
    attn_low, w, raw, low, prev, head_low, stats, x, mixed_own, attention, down,
    gain_q, gain_k, gain_a, gain_m, gain_a_own, gain_m_own, cosine, sine, seqs, n_tp, n_xy,
):
    rows, width = x.shape
    local = head_low.shape[1]
    n_fsdp, n_ctx = n_xy
    vmem, anywhere = pl.BlockSpec(memory_space=pltpu.VMEM), pl.BlockSpec(memory_space=pl.ANY)
    shape, dma = jax.ShapeDtypeStruct, pltpu.SemaphoreType.DMA
    devices, peers = n_fsdp * n_ctx, n_fsdp // 2 * n_ctx - 1
    blocks = max(n_ctx - 1, 1)
    block = width // devices
    gains = (1, 2 * (local + width))
    acts = shape(x.shape, bf16)
    span = n_tp * PIECE
    like = lambda a: pltpu.VMEM(a.shape, a.dtype)
    return pl.pallas_call(
        functools.partial(back_kernel, n_tp, n_xy, seqs),
        out_shape=[
            acts, acts, shape(gains, f32), shape((4 * block, local), f32), shape((width, 4 * local), bf16),
        ],
        in_specs=[anywhere] * 11 + [vmem] * 8,
        out_specs=[anywhere, anywhere, vmem, anywhere, anywhere],
        scratch_shapes=line_scratch(n_tp, rows, width) + [
            like(w), like(raw), like(low), like(prev), like(prev), like(head_low), like(stats), like(x), like(mixed_own),
            pltpu.VMEM((rows, local), bf16), pltpu.VMEM((max(rows, 4 * block), local), f32),
            pltpu.VMEM((rows, 2 * local), f32),
            pltpu.VMEM((rows, 3 * local), bf16), pltpu.VMEM((2, WEIGHT_ROWS, 3 * local), bf16),
            pltpu.VMEM((width // 2, 4 * local), bf16), pltpu.VMEM((peers, block, 4 * local), bf16),
            pltpu.VMEM((4, 2, span, width), bf16), pltpu.VMEM((2, span, width), bf16),
            pltpu.VMEM(gains, f32), pltpu.VMEM((devices - 1,) + gains, f32), pltpu.VMEM((8, local), f32),
            pltpu.VMEM((8, rows), f32), pltpu.VMEM((n_tp - 1, 8, rows), f32), pltpu.VMEM((n_tp - 1, 1, width), f32),
            dma((10,)), dma((blocks, seqs)), dma((blocks, seqs)), dma((seqs, 2, n_tp - 1)), dma((seqs, 2, n_tp - 1)),
            dma((2,)), dma, dma((2, 2, n_fsdp // 2)), dma((2, 2, peers)), dma((devices - 1,)), dma((devices - 1,)),
            dma((n_tp,)), dma((4, 2)), dma((2,)),
        ],
        compiler_params=params(3),
        cost_estimate=pl.CostEstimate(flops=200 * 10**9, bytes_accessed=60 << 20, transcendentals=0),
        name="back",
    )(
        attn_low, w, raw, low, prev, head_low, stats, x, mixed_own, attention, down,
        gain_q, gain_k, gain_a, gain_m, gain_a_own, gain_m_own, cosine, sine,
    )


def rotation_tables(length):
    half = HD // 2
    frequency = rope_theta ** (-np.arange(half) * 2.0 / HD)
    angles = np.arange(length)[:, None] * frequency[None, :]
    cosine, sine = np.cos(angles), np.sin(angles)
    return (
        jnp.asarray(np.concatenate([cosine, cosine], axis=1), f32),
        jnp.asarray(np.concatenate([-sine, sine], axis=1), f32),
    )


def per_device(
    tokens, w_query, w_key, w_value, w_output, w_gate, w_up, w_down,
    gain_query, gain_key, gain_attn, gain_mlp, cotangent,
):
    micro_count, rows, width = tokens.shape
    local = w_query.shape[1]
    ctx = lax.axis_size("ctx")
    tp = lax.axis_size("tp")
    cosine, sine = rotation_tables(rows * ctx)
    gain_q = gain_query.astype(f32)
    gain_k = gain_key.astype(f32)
    gain_a = gain_attn.astype(f32)
    gain_m = gain_mlp.astype(f32)
    xy = ("fsdp", "ctx")

    def gather(w):
        return lax.all_gather(w, xy, axis=0, tiled=True)

    w_g = gather(w_gate)
    w_u = gather(w_up)
    w_down_t = gather(w_down.T)

    flat = (micro_count * rows, width)
    x_all, grad_all = tokens.reshape(flat), cotangent.reshape(flat)

    n_xy = (lax.axis_size("fsdp"), ctx)
    raw, low, prev, head_low, stats, attention, mlp_in, w_full, attn_own = front(
        x_all, w_query, w_key, w_value, w_output.T, gain_q[None], gain_k[None], gain_a[None], cosine, sine,
        micro_count, tp, n_xy
    )
    down, _, attn_low, mlp_weights, mixed_own, gain_m_sum, gain_a_sum = mlp(
        mlp_in, grad_all, attn_own, gain_m[None], gain_a[None], w_g, w_u, w_down_t, tp
    )
    def scatter(full):
        return lax.psum_scatter(full, xy, scatter_dimension=0, tiled=True).astype(f32)

    units = w_gate.shape[1]
    d_mlp = scatter(mlp_weights)
    d_down, d_gate, d_up = d_mlp[:, :units].T, d_mlp[:, units : 2 * units], d_mlp[:, 2 * units :]
    grad_tokens, out, gains, d_attn, _ = back(
        attn_low, w_full, raw, low, prev, head_low, stats, x_all, mixed_own, attention, down,
        gain_q[None], gain_k[None], gain_a[None], gain_m[None], gain_a_sum, gain_m_sum, cosine, sine,
        micro_count, tp, n_xy
    )
    gains = gains[0]
    block = w_query.shape[0]
    d_v, d_k, d_q, d_o = (d_attn[k * block : (k + 1) * block] for k in range(4))
    return (
        out.reshape(tokens.shape),
        grad_tokens.reshape(tokens.shape),
        d_q, d_k, d_v, d_o.T, d_gate, d_up, d_down,
        gains[:local], gains[local : 2 * local],
        gains[2 * local : 2 * local + width], gains[2 * local + width :],
    )


def solution(mesh):
    rows, cols = P(("fsdp", "ctx"), "tp"), P("tp", ("fsdp", "ctx"))
    acts = P("fsdp", "ctx", None)
    in_specs = (acts, rows, rows, rows, cols, rows, rows, cols, P("tp"), P("tp"), P(), P(), acts)
    out_specs = (acts, acts, rows, rows, rows, cols, rows, rows, cols, P("tp"), P("tp"), P(), P())
    return jax.shard_map(
        per_device, mesh=mesh, in_specs=in_specs, out_specs=out_specs, check_vma=False
    )
```

```python
import functools

import jax
import jax.numpy as jnp
import numpy as np
from jax import lax
from jax.experimental import pallas as pl
from jax.experimental.pallas import tpu as pltpu
from jax.sharding import PartitionSpec as P

HD = 128
norm_eps = 1e-06
rope_theta = 500000.0
masked_value = -1e30
f32 = jnp.float32
bf16 = jnp.bfloat16


def dot(a, b, dims, out=f32):
    return lax.dot_general(a, b, (dims, ((), ())), preferred_element_type=f32).astype(out)


PIECE = 16
LAG = 1
CHUNK = 256
TILE_ROWS = 256
EXTRA = 5
DOWN_PER_TICK = 2
WEIGHT_ROWS = 256
WEIGHT_TILES = 2
MLP_TILE = 1024
TILES_PER_TICK = 3


class Line:
    def __init__(self, axis, n, groups, buf, total, send, recv):
        self.axis, self.n, self.groups = axis, n, groups
        self.buf, self.total, self.send, self.recv = buf, total, send, recv
        self.i = lax.axis_index(axis)
        self.stages = 2 * n - 1

    def rows(self, group, c, count=1):
        return pl.ds(pl.multiple_of((group * self.n + c) * PIECE, PIECE), count * PIECE)

    def copy(self, way, step, group, c, source):
        rows = self.rows(group, c)
        return pltpu.make_async_remote_copy(
            src_ref=self.buf.at[source, rows],
            dst_ref=self.buf.at[0 if way == 0 else 2, rows],
            send_sem=self.send.at[way, step, group],
            recv_sem=self.recv.at[way, step, group],
            device_id={self.axis: self.i + (1 if way == 0 else -1)},
            device_id_type=pl.DeviceIdType.MESH,
        )

    def add(self, c, group, source):
        rows = self.rows(group, c)
        both = self.buf[1, rows].astype(f32) + self.buf[source, rows].astype(f32)
        self.buf[1, rows] = both.astype(bf16)

    def reduce_step(self, s, group):
        i, n = self.i, self.n

        @pl.when(i <= min(s - 1, n - 2))
        def _():
            c = n - s + i
            if s >= 2:

                @pl.when(i >= 1)
                def _():
                    self.copy(0, s - 2, group, c, 1).wait_recv()
                    self.add(c, group, 0)

            self.copy(0, s - 1, group, c, 1).start()

        @pl.when(i >= max(n - s, 1))
        def _():
            c = s + i - n
            if s >= 2:

                @pl.when(i <= n - 2)
                def _():
                    self.copy(1, s - 2, group, c, 1).wait_recv()
                    self.add(c, group, 2)

            self.copy(1, s - 1, group, c, 1).start()

    def finish(self, group, then):
        i, n = self.i, self.n
        rows = self.rows(group, i)
        self.total[...] = self.buf[1, rows].astype(f32)

        @pl.when(i >= 1)
        def _():
            self.copy(0, n - 2, group, i, 1).wait_recv()
            self.total[...] += self.buf[0, rows].astype(f32)

        @pl.when(i <= n - 2)
        def _():
            self.copy(1, n - 2, group, i, 1).wait_recv()
            self.total[...] += self.buf[2, rows].astype(f32)

        self.buf[1, rows] = then(group, self.total[...]).astype(bf16)

        @pl.when(i <= n - 2)
        def _():
            self.copy(0, n - 1, group, i, 1).start()

        @pl.when(i >= 1)
        def _():
            self.copy(1, n - 1, group, i, 1).start()

    def gather_step(self, s, group):
        i, n = self.i, self.n

        @pl.when(i >= s - 1)
        def _():
            c = i - s + 1
            self.copy(0, n + s - 3, group, c, 0).wait_recv()
            if s <= n - 1:

                @pl.when(i <= n - 2)
                def _():
                    self.copy(0, n + s - 2, group, c, 0).start()

        @pl.when(i <= n - s)
        def _():
            c = i + s - 1
            self.copy(1, n + s - 3, group, c, 2).wait_recv()
            if s <= n - 1:

                @pl.when(i >= 1)
                def _():
                    self.copy(1, n + s - 2, group, c, 2).start()

    def sent(self, group):
        i, n = self.i, self.n
        for s in range(1, n):

            @pl.when(i <= min(s - 1, n - 2))
            def _():
                self.copy(0, s - 1, group, n - s + i, 1).wait_send()

            @pl.when(i >= max(n - s, 1))
            def _():
                self.copy(1, s - 1, group, s + i - n, 1).wait_send()

            @pl.when((i >= s - 1) & (i <= n - 2))
            def _():
                self.copy(0, n + s - 2, group, i - s + 1, 1 if s == 1 else 0).wait_send()

            @pl.when((i <= n - s) & (i >= 1))
            def _():
                self.copy(1, n + s - 2, group, i + s - 1, 1 if s == 1 else 2).wait_send()

    def piece(self, group, c):
        slot = jnp.where(c < self.i, 0, jnp.where(c > self.i, 2, 1))
        return self.buf[slot, self.rows(group, c)]

    def piece_ref(self, group, c):
        slot = jnp.where(c < self.i, 0, jnp.where(c > self.i, 2, 1))
        return self.buf.at[slot, self.rows(group, c)]

    def tick(self, t, then, done):
        n = self.n

        def stage(index, body):
            group = t - index * LAG

            @pl.when((group >= 0) & (group < self.groups))
            def _():
                body(group)

        for s in range(1, n):
            stage(s - 1, functools.partial(self.reduce_step, s))
        stage(n - 1, lambda group: self.finish(group, then))
        for s in range(2, n):
            stage(n + s - 2, functools.partial(self.gather_step, s))

        def last(group):
            self.gather_step(n, group)
            self.sent(group)
            done(group)

        stage(2 * n - 2, last)

    def ticks(self):
        return self.groups + (2 * self.n - 2) * LAG


def greet(axis, n, others=()):
    i = lax.axis_index(axis)
    barrier = pltpu.get_barrier_semaphore()
    for peer in others:
        pl.semaphore_signal(barrier, inc=1, device_id=peer, device_id_type=pl.DeviceIdType.MESH)

    @pl.when(i >= 1)
    def _():
        pl.semaphore_signal(barrier, inc=1, device_id={axis: i - 1}, device_id_type=pl.DeviceIdType.MESH)

    @pl.when(i <= n - 2)
    def _():
        pl.semaphore_signal(barrier, inc=1, device_id={axis: i + 1}, device_id_type=pl.DeviceIdType.MESH)

    pl.semaphore_wait(barrier, len(others) + jnp.minimum(i, 1) + jnp.minimum(n - 1 - i, 1))


def line_scratch(n, rows, width):
    sems = pltpu.SemaphoreType.DMA((2, 2 * n - 2, rows // (n * PIECE)))
    return [pltpu.VMEM((3, rows, width), bf16), pltpu.VMEM((PIECE, width), f32), sems, sems]


def params(collective_id):
    return pltpu.CompilerParams(
        collective_id=collective_id, has_side_effects=True, vmem_limit_bytes=63 << 20
    )


def scale_of(a):
    return lax.rsqrt(jnp.mean(a * a, axis=-1, keepdims=True) + norm_eps)


def local_copies(pairs, sems):
    copies = [pltpu.make_async_copy(a, b, sems.at[k]) for k, (a, b) in enumerate(pairs)]
    for copy in copies:
        copy.start()
    return copies


def mlp_kernel(
    n, n_xy, mlp_in, grad_hbm, attn_own, gain_m, gain_a, w_g_hbm, w_u_hbm, w_d_hbm,
    down_out, hidden_out, attn_low_out, weights_out, down_full, down_pair, down_blocks, mixed_own, gain_m_sum, gain_a_sum,
    buf, total, send, recv, w_g, w_u, w_d, mlp_rows, hidden, down_low, gate, up,
    ready, w_sems, io_sems, piece_sems, tile_sems, gain_m_acc, gain_a_acc,
    grad, pair_sems, peer_sems, down_sem,
):
    rows, width = grad.shape
    units = w_g.shape[1]
    groups = rows // (n * PIECE)
    per_chunk = CHUNK // (n * PIECE)
    line = Line("tp", n, groups, buf, total, send, recv)
    i = line.i
    tile = MLP_TILE

    def weight_copies(j):
        cols = pl.ds(pl.multiple_of(j * tile, tile), tile)
        return [
            pltpu.make_async_copy(w_g_hbm.at[:, cols], w_g.at[:, cols], w_sems.at[0, j]),
            pltpu.make_async_copy(w_u_hbm.at[:, cols], w_u.at[:, cols], w_sems.at[1, j]),
        ]

    for j in range(units // tile):
        for copy in weight_copies(j):
            copy.start()
    down_weights = pltpu.make_async_copy(w_d_hbm, w_d, w_sems.at[2, 0])
    down_weights.start()
    grad_in = pltpu.make_async_copy(grad_hbm, grad, down_sem)
    grad_in.start()
    gain_m_acc[...] = jnp.zeros_like(gain_m_acc)
    gain_a_acc[...] = jnp.zeros_like(gain_a_acc)
    fsdp, n_ctx = lax.axis_index("fsdp"), n_xy[1]
    core, spots = lax.rem(fsdp, 2), n_xy[0] // 2 * n_ctx
    spot = lax.div(fsdp, 2) * n_ctx + lax.axis_index("ctx")
    other_core = {"fsdp": fsdp + 1 - 2 * core}
    peers = []
    for k in range(1, spots):
        peer = lax.rem(spot + k, spots)
        peers.append({"fsdp": 2 * lax.div(peer, n_ctx) + core, "ctx": lax.rem(peer, n_ctx)})
    greet("tp", n, [other_core] + peers)
    offset = per_chunk + line.stages + EXTRA

    def chunk_rows(chunk):
        return pl.ds(pl.multiple_of(chunk * CHUNK, CHUNK), CHUNK)

    def hidden_copy(chunk):
        return pltpu.make_async_copy(hidden, hidden_out.at[chunk_rows(chunk)], io_sems.at[1])

    def forward(chunk, first=False):
        at = chunk_rows(chunk)
        fetch = pltpu.make_async_copy(mlp_in.at[at], mlp_rows, io_sems.at[0])
        fetch.start()
        if not first:
            hidden_copy(chunk - 1).wait()
        fetch.wait()

        @pl.loop(0, units // tile)
        def _(j):
            if first:
                for copy in weight_copies(j):
                    copy.wait()
            cols = pl.ds(pl.multiple_of(j * tile, tile), tile)
            gate_proj = dot(mlp_rows[...], w_g[:, cols], ((1,), (0,)))
            up_proj = dot(mlp_rows[...], w_u[:, cols], ((1,), (0,)))
            gate[at, cols] = gate_proj.astype(bf16)
            up[at, cols] = up_proj.astype(bf16)
            hidden[:, cols] = (gate_proj / (1.0 + jnp.exp(-gate_proj)) * up_proj).astype(bf16)

        hidden_copy(chunk).start()

    def forward_down(chunk):
        at = chunk_rows(chunk)

        @pl.loop(0, width // tile)
        def _(j):
            cols = pl.ds(pl.multiple_of(j * tile, tile), tile)
            buf[1, at, cols] = dot(hidden[...], w_d[cols], ((1,), (1,)), bf16)

    def backward(chunk):
        at = chunk_rows(chunk)

        @pl.loop(0, units // tile)
        def _(j):
            cols = pl.ds(pl.multiple_of(j * tile, tile), tile)
            gate_proj, up_proj = gate[at, cols].astype(f32), up[at, cols].astype(f32)
            sig = 1.0 / (1.0 + jnp.exp(-gate_proj))
            grad_hidden = dot(down_low[at], w_d[:, cols], ((1,), (0,)))
            up[at, cols] = (grad_hidden * gate_proj * sig).astype(bf16)
            gate[at, cols] = (grad_hidden * up_proj * sig * (1.0 + gate_proj * (1.0 - sig))).astype(bf16)

    def backward_in(chunk):
        at = chunk_rows(chunk)

        @pl.loop(0, width // tile)
        def _(j):
            cols = pl.ds(pl.multiple_of(j * tile, tile), tile)
            buf[1, at, cols] = (
                dot(gate[at], w_g[cols], ((1,), (1,))) + dot(up[at], w_u[cols], ((1,), (1,)))
            ).astype(bf16)

    whole = pl.ds(0, rows)
    per_part = width // TILE_ROWS
    late_in = pltpu.make_async_copy(mlp_in, w_u.at[whole], w_sems.at[1, 0])

    def tile_rows(k):
        return pl.ds(pl.multiple_of(k * TILE_ROWS, TILE_ROWS), TILE_ROWS)

    def tile_copy(k, slot):
        part, row = lax.div(k, per_part), lax.rem(k, per_part)
        return pltpu.make_async_copy(
            w_d.at[tile_rows(slot)],
            weights_out.at[tile_rows(row), pl.ds(pl.multiple_of(part * units, units), units)],
            tile_sems.at[slot],
        )

    def weight_tile(k):
        slot = lax.rem(k, 2)
        at = tile_rows(lax.rem(k, per_part))

        @pl.when(k >= 2)
        def _():
            tile_copy(k - 2, slot).wait()

        def fill(right):
            w_d[tile_rows(slot)] = dot(w_u[whole, at], right[...], ((0,), (0,)), bf16)

        @pl.when(k < per_part)
        def _():
            fill(gate)

        @pl.when(k >= per_part)
        def _():
            fill(up)

        tile_copy(k, slot).start()

    def down_copy(k):
        return pltpu.make_async_copy(hidden, down_full.at[tile_rows(k)], down_sem)

    hidden_in = pltpu.make_async_copy(hidden_out, grad, io_sems.at[0])

    def down_tile(k):
        @pl.when(k >= 1)
        def _():
            down_copy(k - 1).wait()

        hidden[...] = dot(down_low[:, tile_rows(k)], grad[...], ((0,), (0,)), bf16)
        down_copy(k).start()

    block = width // (n_xy[0] * n_ctx)
    pair_span = n_ctx * block

    def pair_copy(chip):
        rows_at = pl.ds(pl.multiple_of((2 * chip + 1 - core) * pair_span, pair_span), pair_span)
        return pltpu.make_async_remote_copy(
            src_ref=down_full.at[rows_at], dst_ref=down_pair.at[pl.ds(chip * pair_span, pair_span)],
            send_sem=pair_sems.at[0, chip], recv_sem=pair_sems.at[1, chip],
            device_id=other_core, device_id_type=pl.DeviceIdType.MESH,
        )

    def pair_unit(u):
        chip, inside = u * CHUNK // pair_span, u * CHUNK % pair_span
        if inside == 0:
            pair_copy(chip).wait_recv()
        mine = pl.ds(pl.multiple_of((2 * chip + core) * pair_span + inside, CHUNK), CHUNK)
        there = down_pair.at[pl.ds(u * CHUNK, CHUNK)]
        loads = local_copies([(down_full.at[mine], hidden), (there, mlp_rows)], io_sems)
        for load in loads:
            load.wait()
        mlp_rows[...] = (mlp_rows[...].astype(f32) + hidden[...].astype(f32)).astype(bf16)
        store = pltpu.make_async_copy(mlp_rows, there, down_sem)
        store.start()
        store.wait()

    def spot_rows(which):
        return down_pair.at[pl.ds(pl.multiple_of(which * block, block), block)]

    def peer_copies():
        copies = [pltpu.make_async_copy(spot_rows(spot), down_blocks.at[spots - 1], peer_sems.at[0, spots - 1])]
        for k, device in enumerate(peers):
            copies.append(
                pltpu.make_async_remote_copy(
                    src_ref=spot_rows(lax.rem(spot + k + 1, spots)), dst_ref=down_blocks.at[k],
                    send_sem=peer_sems.at[0, k], recv_sem=peer_sems.at[1, k],
                    device_id=device, device_id_type=pl.DeviceIdType.MESH,
                )
            )
        return copies

    def let_in():
        @pl.when(i >= 1)
        def _():
            pl.semaphore_signal(
                ready.at[1], inc=1, device_id={"tp": i - 1}, device_id_type=pl.DeviceIdType.MESH
            )

        @pl.when(i <= n - 2)
        def _():
            pl.semaphore_signal(
                ready.at[0], inc=1, device_id={"tp": i + 1}, device_id_type=pl.DeviceIdType.MESH
            )

    def pieces_out(group, out):
        return local_copies([(line.piece_ref(group, c), out.at[line.rows(group, c)]) for c in range(n)], piece_sems)

    def down_done(group):
        copies = pieces_out(group, down_out)
        for c in range(n):
            at = line.rows(group, c)
            branch = line.piece(group, c).astype(f32)
            r = scale_of(branch)
            g = grad[at].astype(f32)
            scaled = g * gain_m[...]
            inner = jnp.mean(scaled * branch, axis=-1, keepdims=True)
            gain_m_acc[...] += g * branch * r

            @pl.when(i == c)
            def _():
                mixed_own[pl.ds(pl.multiple_of(group * PIECE, PIECE), PIECE)] = g

            down_low[at] = (r * scaled - branch * (r * r * r) * inner).astype(bf16)
        for copy in copies:
            copy.wait()

    def attn_grad(group, total):
        at = pl.ds(pl.multiple_of(group * PIECE, PIECE), PIECE)
        mixed = mixed_own[at] + total
        mixed_own[at] = mixed
        branch = attn_own[at].astype(f32)
        r = scale_of(branch)
        scaled = mixed * gain_a[...]
        inner = jnp.mean(scaled * branch, axis=-1, keepdims=True)
        gain_a_acc[...] += mixed * branch * r
        return r * scaled - branch * (r * r * r) * inner

    def attn_done(group):
        for copy in pieces_out(group, attn_low_out):
            copy.wait()

    forward(0, True)
    down_weights.wait()
    grad_in.wait()
    forward_down(0)

    @pl.loop(0, offset + line.ticks())
    def _(t):
        back = t - offset

        @pl.when((back >= 0) & (back < groups) & (lax.rem(back + groups, per_chunk) == 0))
        def _():
            @pl.when(i >= 1)
            def _():
                pl.semaphore_wait(ready.at[0], 1)

            @pl.when(i <= n - 2)
            def _():
                pl.semaphore_wait(ready.at[1], 1)

        line.tick(back, attn_grad, attn_done)
        line.tick(t, lambda group, total: total, down_done)
        for ahead, work in ((2, forward), (1, forward_down)):
            due = t + ahead

            @pl.when((due >= per_chunk) & (due < groups) & (lax.rem(due, per_chunk) == 0))
            def _():
                work(lax.div(due, per_chunk))

        for ahead, work in ((2, backward), (1, backward_in)):
            due = t + ahead - offset

            @pl.when((due >= 0) & (due < groups) & (lax.rem(due + groups, per_chunk) == 0))
            def _():
                if ahead == 1:
                    let_in()
                work(lax.div(due, per_chunk))

        down_tick = groups + line.stages - 1
        down_ticks = per_part // DOWN_PER_TICK

        @pl.when((t >= down_tick) & (t < down_tick + down_ticks))
        def _():
            @pl.when(t == down_tick)
            def _():
                hidden_copy(rows // CHUNK - 1).wait()
                hidden_in.start()
                hidden_in.wait()

            for m in range(DOWN_PER_TICK):
                down_tile((t - down_tick) * DOWN_PER_TICK + m)

        @pl.when(t == down_tick + down_ticks - 1)
        def _():
            down_copy(per_part - 1).wait()
            for chip in range(n_xy[0] // 2):
                pair_copy(chip).start()

        pair_tick = down_tick + down_ticks + 1
        units_of_pair = width // 2 // CHUNK
        for u in range(units_of_pair):

            @pl.when(t == pair_tick + u // 2)
            def _():
                pair_unit(u)
                if u == units_of_pair - 1:
                    for copy in peer_copies():
                        copy.start()

        last = offset + groups - per_chunk - 1

        @pl.when(t == last)
        def _():
            late_in.start()

        @pl.when(t == last + 1)
        def _():
            late_in.wait()

        for m in range(TILES_PER_TICK):
            k = (t - last - 1) * TILES_PER_TICK + m

            @pl.when((k >= 0) & (k < 2 * per_part))
            def _():
                weight_tile(k)

    for k in (2 * per_part - 2, 2 * per_part - 1):
        tile_copy(k, k % 2).wait()
    for copy in peer_copies():
        copy.wait()
    for chip in range(n_xy[0] // 2):
        pair_copy(chip).wait_send()
    gain_m_sum[...] = jnp.sum(gain_m_acc[...], axis=0, keepdims=True)
    gain_a_sum[...] = jnp.sum(gain_a_acc[...], axis=0, keepdims=True)


def mlp(mlp_in, grad, attn_own, gain_m, gain_a, w_g, w_u, w_d, n, n_xy):
    rows, width = grad.shape
    units = w_g.shape[1]
    vmem, anywhere = pl.BlockSpec(memory_space=pltpu.VMEM), pl.BlockSpec(memory_space=pl.ANY)
    acts = jax.ShapeDtypeStruct((rows, width), bf16)
    inner = jax.ShapeDtypeStruct((rows, units), bf16)
    spots = n_xy[0] // 2 * n_xy[1]
    gain_shape = jax.ShapeDtypeStruct((1, width), f32)
    return pl.pallas_call(
        functools.partial(mlp_kernel, n, n_xy),
        out_shape=[
            acts, inner, acts, jax.ShapeDtypeStruct((width, 2 * units), bf16),
            jax.ShapeDtypeStruct((width, units), bf16), jax.ShapeDtypeStruct((width // 2, units), bf16),
            jax.ShapeDtypeStruct((spots, width // (2 * spots), units), bf16),
            jax.ShapeDtypeStruct((rows // n, width), f32), gain_shape, gain_shape,
        ],
        in_specs=[anywhere] * 2 + [vmem] * 3 + [anywhere] * 3,
        out_specs=[anywhere] * 7 + [vmem] * 3,
        scratch_shapes=line_scratch(n, rows, width) + [
            pltpu.VMEM(w_g.shape, bf16), pltpu.VMEM(w_u.shape, bf16), pltpu.VMEM(w_d.shape, bf16),
            pltpu.VMEM((CHUNK, width), bf16), pltpu.VMEM((CHUNK, units), bf16), pltpu.VMEM((rows, width), bf16),
            pltpu.VMEM((rows, units), bf16), pltpu.VMEM((rows, units), bf16),
            pltpu.SemaphoreType.REGULAR((2,)),
            pltpu.SemaphoreType.DMA((3, units // 512)), pltpu.SemaphoreType.DMA((2,)), pltpu.SemaphoreType.DMA((n,)),
            pltpu.SemaphoreType.DMA((2,)),
            pltpu.VMEM((PIECE, width), f32), pltpu.VMEM((PIECE, width), f32),
            pltpu.VMEM((rows, width), bf16),
            pltpu.SemaphoreType.DMA((2, n_xy[0] // 2)), pltpu.SemaphoreType.DMA((2, spots)), pltpu.SemaphoreType.DMA,
        ],
        compiler_params=params(2),
        cost_estimate=pl.CostEstimate(flops=200 * 10**9, bytes_accessed=60 << 20, transcendentals=0),
        name="mlp",
    )(mlp_in, grad, attn_own, gain_m, gain_a, w_g, w_u, w_d)


def peers_of(axis, n):
    i = lax.axis_index(axis)
    return [(k - 1, lax.rem(i + k, n)) for k in range(1, n)]


def meet(axes, others=()):
    barrier = pltpu.get_barrier_semaphore()
    count = len(others)
    for peer in others:
        pl.semaphore_signal(barrier, inc=1, device_id=peer, device_id_type=pl.DeviceIdType.MESH)
    for axis, n in axes:
        for _, peer in peers_of(axis, n):
            pl.semaphore_signal(barrier, inc=1, device_id={axis: peer}, device_id_type=pl.DeviceIdType.MESH)
            count += 1
    pl.semaphore_wait(barrier, count)


def swap(axis, n, pairs, send, recv):
    copies = []
    for k, (mine, theirs) in enumerate(pairs):
        for slot, peer in peers_of(axis, n):
            copy = pltpu.make_async_remote_copy(
                src_ref=mine, dst_ref=theirs.at[slot],
                send_sem=send.at[k, slot], recv_sem=recv.at[k, slot],
                device_id={axis: peer}, device_id_type=pl.DeviceIdType.MESH,
            )
            copy.start()
            copies.append(copy)
    for copy in copies:
        copy.wait()


def lanes_to_rows(columns):
    return jnp.transpose(columns)[:8]


def rows_to_lanes(packed):
    rows = packed.shape[1]
    return jnp.transpose(jnp.concatenate([packed, jnp.zeros((120, rows), f32)], axis=0))


def two_lanes(first, second):
    lane = lax.broadcasted_iota(jnp.int32, (first.shape[0], 128), 1)
    return jnp.where(lane == 0, first, jnp.where(lane == 1, second, 0.0))


def turn(values, cosine, sine):
    return values * cosine + pltpu.roll(values, HD // 2, 1) * sine


def heads_loop(heads, body):
    @pl.loop(0, heads)
    def _(h):
        body(h, lambda part, width: pl.ds(pl.multiple_of(part * width + h * HD, HD), HD))


class Gather:
    def __init__(self, n_xy, parts, full, local_sems, sems):
        n_fsdp, self.n_ctx = n_xy
        self.chips = n_fsdp // 2
        self.parts, self.full, self.local_sems, self.sems = parts, full, local_sems, sems
        fsdp = lax.axis_index("fsdp")
        self.chip, self.core = lax.div(fsdp, 2), lax.rem(fsdp, 2)
        self.ctx = lax.axis_index("ctx")
        self.block = parts[0].shape[0]

    def place(self, part, chip, core, ctx):
        columns = self.parts[part].shape[1]
        first = sum(p.shape[1] for p in self.parts[:part])
        row = ((2 * chip + core) * self.n_ctx + ctx) * self.block
        return self.full.at[pl.ds(pl.multiple_of(row, self.block), self.block), pl.ds(first, columns)]

    def send(self, part, slot, source, target, device):
        return pltpu.make_async_remote_copy(
            src_ref=source, dst_ref=target,
            send_sem=self.sems.at[0, part, slot], recv_sem=self.sems.at[1, part, slot],
            device_id=device, device_id_type=pl.DeviceIdType.MESH,
        )

    def keep(self, part):
        return pltpu.make_async_copy(
            self.parts[part], self.place(part, self.chip, self.core, self.ctx), self.local_sems.at[part]
        )

    def to_ctx(self, part, k):
        target = self.place(part, self.chip, self.core, self.ctx)
        return self.send(part, k - 1, self.parts[part], target, {"ctx": lax.rem(self.ctx + k, self.n_ctx)})

    def to_chip(self, part, c, k):
        ctx = lax.rem(self.ctx + self.n_ctx - c, self.n_ctx)
        target = self.place(part, self.chip, self.core, ctx)
        source = self.parts[part] if c == 0 else target
        slot = self.n_ctx - 1 + c * (self.chips - 1) + k - 1
        chip = lax.rem(self.chip + k, self.chips)
        return self.send(part, slot, source, target, {"fsdp": 2 * chip + self.core})

    def to_core(self, part, c, k):
        ctx = lax.rem(self.ctx + self.n_ctx - c, self.n_ctx)
        chip = lax.rem(self.chip + self.chips - k, self.chips)
        target = self.place(part, chip, self.core, ctx)
        source = self.parts[part] if c == 0 and k == 0 else target
        slot = self.n_ctx - 1 + self.n_ctx * (self.chips - 1) + c * self.chips + k
        return self.send(part, slot, source, target, {"fsdp": 2 * self.chip + 1 - self.core})

    def slots(self):
        return self.n_ctx - 1 + self.n_ctx * (self.chips - 1) + self.n_ctx * self.chips

    def start(self, part):
        self.keep(part).start()
        for k in range(1, self.n_ctx):
            self.to_ctx(part, k).start()
        for k in range(1, self.chips):
            self.to_chip(part, 0, k).start()
        self.to_core(part, 0, 0).start()

    def pass_on(self, part):
        for c in range(1, self.n_ctx):
            self.to_ctx(part, c).wait_recv()
            for k in range(1, self.chips):
                self.to_chip(part, c, k).start()
            self.to_core(part, c, 0).start()
        for c in range(self.n_ctx):
            for k in range(1, self.chips):
                self.to_chip(part, c, k).wait_recv()
                self.to_core(part, c, k).start()

    def end(self, part):
        for c in range(self.n_ctx):
            for k in range(self.chips):
                self.to_core(part, c, k).wait_recv()
        self.keep(part).wait()

    def sent(self, part):
        for k in range(1, self.n_ctx):
            self.to_ctx(part, k).wait_send()
        for c in range(self.n_ctx):
            for k in range(1, self.chips):
                self.to_chip(part, c, k).wait_send()
            for k in range(self.chips):
                self.to_core(part, c, k).wait_send()


def front_kernel(
    n_tp, n_xy, seqs, x_hbm, w_q, w_k, w_v, w_o, gain_q, gain_k, gain_a, cosine, sine,
    raw_out, low_out, prev_out, head_low_out, stats_out, attention_out, mlp_in_out, w_out, attn_own_out,
    buf, total, send, recv, x, w, raw, low, prev, head_low, stats, mlp_in, attn_own,
    sums, theirs, kv_send, kv_recv, sum_send, sum_recv, w_local_sems, w_sems, io_sems, piece_sems, group_sems,
):
    n_ctx = n_xy[1]
    rows_all, width = x.shape
    rows = rows_all // seqs
    local = w_q.shape[1]
    heads = local // HD
    me = lax.axis_index("ctx")
    scale = HD ** (-0.5)
    step = min(256, rows)
    fetch_x = pltpu.make_async_copy(x_hbm, x, io_sems.at[0])
    fetch_x.start()
    gather = Gather(n_xy, [w_v, w_k, w_q, w_o], w, w_local_sems, w_sems)
    value_at, key_at, query_at, out_at = 0, local, 2 * local, 3 * local
    fsdp = lax.axis_index("fsdp")
    meet(
        [("tp", n_tp), ("ctx", n_ctx)],
        [{"fsdp": 2 * lax.div(fsdp, 2) + 1 - lax.rem(fsdp, 2)}]
        + [{"fsdp": lax.rem(fsdp + 2 * k, n_xy[0])} for k in range(1, n_xy[0] // 2)],
    )
    for part in range(4):
        gather.start(part)

    def chunks(body):
        @pl.loop(0, rows_all // step)
        def _(k):
            at = pl.ds(pl.multiple_of(k * step, step), step)
            body(at, pl.ds(pl.multiple_of(me * rows + lax.rem(k, rows // step) * step, step), step))

    for j in range(1, n_ctx):

        @pl.when(me < j)
        def _():
            prev[j - 1] = jnp.zeros(prev.shape[1:], bf16)

    def kv_copy(j, part, seq):
        at = pl.ds(seq * rows, rows)
        return pltpu.make_async_remote_copy(
            src_ref=low.at[at, pl.ds((1 + part) * local, local)],
            dst_ref=prev.at[j - 1, at, pl.ds(part * local, local)],
            send_sem=kv_send.at[j - 1, part, seq], recv_sem=kv_recv.at[j - 1, part, seq],
            device_id={"ctx": lax.rem(me + j, n_ctx)}, device_id_type=pl.DeviceIdType.MESH,
        )

    def kv_each(method, part, seq, here):
        for j in range(1, n_ctx):

            @pl.when((me >= j) if here else (me + j < n_ctx))
            def _():
                getattr(kv_copy(j, part, seq), method)()

    gather.pass_on(0)
    gather.pass_on(1)
    gather.end(0)
    fetch_x.wait()

    def value_chunk(at, _):
        low[at, 2 * local :] = dot(x[at], w[:, value_at : value_at + local], ((1,), (0,)), bf16)

    chunks(value_chunk)
    for seq in range(seqs):
        kv_each("start", 1, seq, False)
    gather.pass_on(2)
    gather.end(1)

    def raw_chunk(part, first):
        def chunk(at, _):
            v = dot(x[at], w[:, first : first + local], ((1,), (0,)))
            raw[at, part * local : (part + 1) * local] = v
            square = jnp.sum(v * v, axis=-1, keepdims=True)
            lane = lax.broadcasted_iota(jnp.int32, (step, 128), 1)
            stats[at] = jnp.where(lane == part, square, stats[at] if part == 0 else 0.0)

        chunks(chunk)

    raw_chunk(1, key_at)
    gather.pass_on(3)
    gather.end(2)
    raw_chunk(0, query_at)

    def sums_chunk(at, _):
        sums[:, at] = lanes_to_rows(stats[at])

    chunks(sums_chunk)
    swap("tp", n_tp, [(sums, theirs)], sum_send, sum_recv)
    square_sums = sums[...]
    for slot in range(n_tp - 1):
        square_sums = square_sums + theirs[slot]
    stats[...] = rows_to_lanes(lax.rsqrt(square_sums / width + norm_eps))

    def turned(part, gain):
        def chunk(at, pos):
            r = stats[at, part : part + 1]
            for h in range(heads):
                cols = pl.ds(part * local + h * HD, HD)
                v = raw[at, cols] * r * gain[:, h * HD : (h + 1) * HD]
                low[at, cols] = turn(v, cosine[pos], sine[pos]).astype(bf16)

        chunks(chunk)

    turned(1, gain_k)
    for seq in range(seqs):
        kv_each("start", 0, seq, False)
    turned(0, gain_q)
    lane = lax.broadcasted_iota(jnp.int32, (step, 128), 1)

    def attention(seq):
        for part in range(2):
            kv_each("wait_recv", part, seq, True)
        seq_rows = pl.ds(seq * rows, rows)

        def one_head(h, cols):
            for tile in range(rows // step):
                at = pl.ds(seq * rows + tile * step, step)
                q = low[at, cols(0, local)]
                seen = (tile + 1) * step
                own = pl.ds(seq * rows, seen)
                s = dot(q, low[own, cols(1, local)], ((1,), (1,))) * scale
                i_pos = lax.broadcasted_iota(jnp.int32, (step, seen), 0) + tile * step
                j_pos = lax.broadcasted_iota(jnp.int32, (step, seen), 1)
                scores = [jnp.where(j_pos <= i_pos, s, masked_value)]
                values = [low[own, cols(2, local)]]
                for j in range(1, n_ctx):
                    s = dot(q, prev[j - 1, seq_rows, cols(0, local)], ((1,), (1,))) * scale
                    scores.append(jnp.where(me >= j, s, masked_value))
                    values.append(prev[j - 1, seq_rows, cols(1, local)])
                top = scores[0].max(-1, keepdims=True)
                for s in scores[1:]:
                    top = jnp.maximum(top, s.max(-1, keepdims=True))
                total, weighted = 0.0, 0.0
                for s, v in zip(scores, values):
                    e = jnp.exp(s - top)
                    total = total + e.sum(-1, keepdims=True)
                    weighted = weighted + dot(e.astype(bf16), v, ((1,), (0,)))
                head_low[at, cols(0, local)] = (weighted / total).astype(bf16)
                stats[at] = jnp.where(lane == h + 2, top + jnp.log(total), stats[at])

        heads_loop(heads, one_head)

    attention(0)
    gather.end(3)

    groups = rows_all // (n_tp * PIECE)
    line = Line("tp", n_tp, groups, buf, total, send, recv)
    per_chunk, per_seq = step // (n_tp * PIECE), rows // (n_tp * PIECE)
    tile = 512

    def group_rows(group):
        return pl.ds(pl.multiple_of(group * n_tp * PIECE, n_tp * PIECE), n_tp * PIECE)

    def mlp_copy(group):
        at = group_rows(group)
        return pltpu.make_async_copy(mlp_in.at[at], mlp_in_out.at[at], group_sems.at[group])

    def own(group, total):
        attn_own[pl.ds(pl.multiple_of(group * PIECE, PIECE), PIECE)] = total.astype(bf16)
        return total

    def done(group):
        copies = local_copies(
            [(line.piece_ref(group, c), attention_out.at[line.rows(group, c)]) for c in range(n_tp)], piece_sems
        )
        for c in range(n_tp):
            at = line.rows(group, c)
            a = line.piece(group, c).astype(f32)
            mlp_in[at] = (x[at].astype(f32) + a * scale_of(a) * gain_a[...]).astype(bf16)
        mlp_copy(group).start()
        for copy in copies:
            copy.wait()

    saves = [
        (raw, raw_out), (low, low_out), (prev, prev_out), (head_low, head_low_out), (stats, stats_out), (w, w_out),
    ]

    @pl.loop(0, line.ticks())
    def _(t):
        @pl.when((t < groups) & (lax.rem(t, per_chunk) == 0))
        def _():
            at = pl.ds(pl.multiple_of(t * n_tp * PIECE, step), step)

            @pl.loop(0, width // tile)
            def _(j):
                cols = pl.ds(pl.multiple_of(j * tile, tile), tile)
                buf[1, at, cols] = dot(head_low[at], w[cols, out_at : out_at + local], ((1,), (1,)), bf16)

        line.tick(t, own, done)
        for seq in range(1, seqs):

            @pl.when(t == seq * per_seq - 1)
            def _():
                attention(seq)

        @pl.when(t == (seqs - 1) * per_seq)
        def _():
            for k, (source, target) in enumerate(saves):
                pltpu.make_async_copy(source, target, io_sems.at[k]).start()

    own_out = pltpu.make_async_copy(attn_own, attn_own_out, piece_sems.at[0])
    own_out.start()
    for k, (source, target) in enumerate(saves):
        pltpu.make_async_copy(source, target, io_sems.at[k]).wait()
    own_out.wait()

    @pl.loop(0, groups)
    def _(group):
        mlp_copy(group).wait()

    for part in range(4):
        gather.sent(part)
    for seq in range(seqs):
        for part in range(2):
            kv_each("wait_send", part, seq, False)


def front(x, w_q, w_k, w_v, w_o, gain_q, gain_k, gain_a, cosine, sine, seqs, n_tp, n_xy):
    rows, width = x.shape
    local = w_q.shape[1]
    n_fsdp, n_ctx = n_xy
    chips = n_fsdp // 2
    vmem, anywhere = pl.BlockSpec(memory_space=pltpu.VMEM), pl.BlockSpec(memory_space=pl.ANY)
    shape = jax.ShapeDtypeStruct
    dma = pltpu.SemaphoreType.DMA
    saved = [
        shape((rows, 2 * local), f32), shape((rows, 3 * local), bf16),
        shape((max(n_ctx - 1, 1), rows, 2 * local), bf16),
        shape((rows, local), bf16), shape((rows, 128), f32),
    ]
    acts, full = shape(x.shape, bf16), shape((width, 4 * local), bf16)
    vmem_of = [pltpu.VMEM(a.shape, a.dtype) for a in saved]
    slots = n_ctx - 1 + n_ctx * (chips - 1) + n_ctx * chips
    kv_sems, sum_sems = dma((max(n_ctx - 1, 1), 2, seqs)), dma((1, n_tp - 1))
    return pl.pallas_call(
        functools.partial(front_kernel, n_tp, n_xy, seqs),
        out_shape=saved + [acts, acts, full, shape((rows // n_tp, width), bf16)],
        in_specs=[anywhere] + [vmem] * 9,
        out_specs=[anywhere] * 9,
        scratch_shapes=line_scratch(n_tp, rows, width) + [
            pltpu.VMEM(x.shape, bf16), pltpu.VMEM(full.shape, bf16), *vmem_of, pltpu.VMEM(x.shape, bf16),
            pltpu.VMEM((rows // n_tp, width), bf16),
            pltpu.VMEM((8, rows), f32), pltpu.VMEM((n_tp - 1, 8, rows), f32),
            kv_sems, kv_sems, sum_sems, sum_sems, dma((4,)), dma((2, 4, slots)), dma((7,)), dma((n_tp,)),
            dma((rows // (n_tp * PIECE),)),
        ],
        compiler_params=params(1),
        cost_estimate=pl.CostEstimate(flops=150 * 10**9, bytes_accessed=30 << 20, transcendentals=0),
        name="front",
    )(x, w_q, w_k, w_v, w_o, gain_q, gain_k, gain_a, cosine, sine)


class Owners:
    def __init__(self, n_xy, full, first, columns, pair_in, peer_in, stage, stage_sem, pair_sems, peer_sems):
        n_fsdp, self.n_ctx = n_xy
        self.chips = n_fsdp // 2
        self.first, self.columns = first, columns
        self.full, self.pair_in, self.peer_in = full, pair_in, peer_in
        self.stage, self.stage_sem = stage, stage_sem
        self.pair_sems, self.peer_sems = pair_sems, peer_sems
        fsdp = lax.axis_index("fsdp")
        self.chip, self.core = lax.div(fsdp, 2), lax.rem(fsdp, 2)
        self.place = self.chip * self.n_ctx + lax.axis_index("ctx")
        self.block = full.shape[0] // (n_fsdp * self.n_ctx)
        self.span = self.n_ctx * self.block

    def cols(self):
        return pl.ds(self.first, self.columns)

    def pair_copy(self, chip):
        there = 1 - self.core
        rows = pl.ds(pl.multiple_of((2 * chip + there) * self.span, self.span), self.span)
        return pltpu.make_async_remote_copy(
            src_ref=self.full.at[rows, self.cols()],
            dst_ref=self.pair_in.at[pl.ds(chip * self.span, self.span), self.cols()],
            send_sem=self.pair_sems.at[0, chip], recv_sem=self.pair_sems.at[1, chip],
            device_id={"fsdp": 2 * self.chip + there}, device_id_type=pl.DeviceIdType.MESH,
        )

    def peer_copy(self, k):
        place = lax.rem(self.place + k, self.chips * self.n_ctx)
        return pltpu.make_async_remote_copy(
            src_ref=self.pair_in.at[self.block_rows(place), self.cols()],
            dst_ref=self.peer_in.at[k - 1, :, self.cols()],
            send_sem=self.peer_sems.at[0, k - 1], recv_sem=self.peer_sems.at[1, k - 1],
            device_id={"fsdp": 2 * lax.div(place, self.n_ctx) + self.core, "ctx": lax.rem(place, self.n_ctx)},
            device_id_type=pl.DeviceIdType.MESH,
        )

    def block_rows(self, place):
        return pl.ds(pl.multiple_of(place * self.block, self.block), self.block)

    def start(self):
        for chip in range(self.chips):
            self.pair_copy(chip).start()

    def pass_on(self):
        unit = min(self.span, self.stage.shape[0])
        for chip in range(self.chips):
            for u in range(self.span // unit):
                mine = pl.multiple_of((2 * chip + self.core) * self.span + u * unit, unit)
                fetch = pltpu.make_async_copy(
                    self.full.at[pl.ds(mine, unit), self.cols()],
                    self.stage.at[pl.ds(0, unit), pl.ds(0, self.columns)], self.stage_sem,
                )
                fetch.start()
                if u == 0:
                    self.pair_copy(chip).wait_recv()
                fetch.wait()
                rows = pl.ds(chip * self.span + u * unit, unit)
                both = self.pair_in[rows, self.cols()].astype(f32) + self.stage[:unit, : self.columns].astype(f32)
                self.pair_in[rows, self.cols()] = both.astype(bf16)
        for k in range(1, self.chips * self.n_ctx):
            self.peer_copy(k).start()

    def end(self, result, width):
        for k in range(1, self.chips * self.n_ctx):
            self.peer_copy(k).wait()
        for part in range(self.first // width, (self.first + self.columns) // width):
            cols = pl.ds(part * width, width)
            sums = self.pair_in[self.block_rows(self.place), cols].astype(f32)
            for k in range(1, self.chips * self.n_ctx):
                sums = sums + self.peer_in[k - 1, :, cols].astype(f32)
            result[part * self.block : (part + 1) * self.block] = sums
        for chip in range(self.chips):
            self.pair_copy(chip).wait_send()


def back_kernel(
    n_tp, n_xy, seqs,
    attn_low_hbm, w_hbm, raw_hbm, low_hbm, prev_hbm, head_low_hbm, stats_hbm, x_hbm, mixed_own_hbm,
    attention_hbm, down_hbm, gain_q, gain_k, gain_a, gain_m, gain_a_own, gain_m_own, cosine, sine,
    grad_out, out_out, gains_sum, weights_own, weights_out,
    buf, total, send, recv, w, raw, low, kv, in_kv, head_low, stats, x, mixed_own, grad_heads, grad_q, grad_kv,
    grad_qkv, tiles, pair_in, peer_in, branches, outs, gains, gains_theirs, gain_qk,
    sums, theirs, gain_theirs, load_sems, kv_send, kv_recv, sum_send, sum_recv, tile_sems, stage_sem,
    pair_sems, peer_sems, gain_send, gain_recv, piece_sems, branch_sems, out_sems,
):
    n_fsdp, n_ctx = n_xy
    rows_all, width = x.shape
    rows = rows_all // seqs
    local = head_low.shape[1]
    heads = local // HD
    me = lax.axis_index("ctx")
    scale = HD ** (-0.5)
    step = min(256, rows)
    out_at = 3 * local
    groups = rows_all // (n_tp * PIECE)
    line = Line("tp", n_tp, groups, buf, total, send, recv)
    per_chunk, per_seq = step // (n_tp * PIECE), rows // (n_tp * PIECE)
    attn_low = buf.at[1]
    qkv_cols, out_cols = pl.ds(0, out_at), pl.ds(out_at, local)
    loads = local_copies(
        [
            (attn_low_hbm, attn_low), (w_hbm.at[:, out_cols], w.at[:, out_cols]), (prev_hbm, kv), (low_hbm, low),
            (head_low_hbm, head_low), (stats_hbm, stats), (raw_hbm, raw), (x_hbm, x),
            (w_hbm.at[:, qkv_cols], w.at[:, qkv_cols]), (mixed_own_hbm, mixed_own),
        ],
        load_sems,
    )
    place = lax.axis_index("fsdp") * n_ctx + me
    others = []
    for k in range(1, n_fsdp * n_ctx):
        peer = lax.rem(place + k, n_fsdp * n_ctx)
        others.append({"fsdp": lax.div(peer, n_ctx), "ctx": lax.rem(peer, n_ctx)})
    meet([("tp", n_tp)], others)

    def chunks(body, seq=None):
        count = rows_all if seq is None else rows
        first = 0 if seq is None else seq * rows

        @pl.loop(0, count // step)
        def _(k):
            at = pl.ds(pl.multiple_of(first + k * step, step), step)
            body(at, pl.ds(pl.multiple_of(me * rows + lax.rem(k, rows // step) * step, step), step))

    loads[0].wait()
    loads[1].wait()

    def heads_chunk(at, _):
        grad_heads[at] = dot(attn_low[at], w[:, out_cols], ((1,), (0,)), bf16)

    chunks(heads_chunk)
    grad_q[...] = jnp.zeros_like(grad_q)
    grad_kv[...] = jnp.zeros_like(grad_kv)
    gain_qk[...] = jnp.zeros_like(gain_qk)
    for load in loads[2:6]:
        load.wait()

    def kv_copy(j, seq):
        at = pl.ds(seq * rows, rows)
        return pltpu.make_async_remote_copy(
            src_ref=kv.at[j - 1, at], dst_ref=in_kv.at[j - 1, at],
            send_sem=kv_send.at[j - 1, seq], recv_sem=kv_recv.at[j - 1, seq],
            device_id={"ctx": lax.rem(me + n_ctx - j, n_ctx)}, device_id_type=pl.DeviceIdType.MESH,
        )

    def lane_of(at, index):
        lane = lax.broadcasted_iota(jnp.int32, (step, 128), 1)
        return jnp.sum(jnp.where(lane == index, stats[at], 0.0), axis=-1, keepdims=True)

    def block(h, cols, at, keys, values, mask):
        q, g = low[at, cols(0, local)], grad_heads[at, cols(0, local)]
        delta = jnp.sum(g.astype(f32) * head_low[at, cols(0, local)].astype(f32), axis=-1, keepdims=True)
        s = dot(q, keys, ((1,), (1,))) * scale
        p = jnp.exp(s - lane_of(at, h + 2))
        if mask is not None:
            p = jnp.where(mask, p, 0.0)
        dp = dot(g, values, ((1,), (1,)))
        ds = (p * (dp - delta)).astype(bf16)
        grad_q[at, cols(0, local)] += dot(ds, keys, ((1,), (0,))) * scale
        return dot(ds, q, ((0,), (0,))) * scale, dot(p.astype(bf16), g, ((0,), (0,)))

    for j in range(1, n_ctx):

        @pl.when(me >= j)
        def _():
            for seq in range(seqs):
                seq_rows = pl.ds(seq * rows, rows)

                def one_head(h, cols):
                    keys, values = kv[j - 1, seq_rows, cols(0, local)], kv[j - 1, seq_rows, cols(1, local)]
                    dk, dv = 0.0, 0.0
                    for tile in range(rows // step):
                        at = pl.ds(seq * rows + tile * step, step)
                        k_term, v_term = block(h, cols, at, keys, values, None)
                        dk, dv = dk + k_term, dv + v_term
                    kv[j - 1, seq_rows, cols(0, local)] = dk.astype(bf16)
                    kv[j - 1, seq_rows, cols(1, local)] = dv.astype(bf16)

                heads_loop(heads, one_head)
                kv_copy(j, seq).start()

    for seq in range(seqs):

        def one_head(h, cols):
            for tile in range(rows // step):
                at = pl.ds(seq * rows + tile * step, step)
                seen = (tile + 1) * step
                own = pl.ds(seq * rows, seen)
                i_pos = lax.broadcasted_iota(jnp.int32, (step, seen), 0) + tile * step
                j_pos = lax.broadcasted_iota(jnp.int32, (step, seen), 1)
                k_term, v_term = block(
                    h, cols, at, low[own, cols(1, local)], low[own, cols(2, local)], j_pos <= i_pos
                )
                grad_kv[own, cols(0, local)] += k_term
                grad_kv[own, cols(1, local)] += v_term

        heads_loop(heads, one_head)

    blocks = width // WEIGHT_ROWS

    def tile_copy(k, slot, first, columns):
        return pltpu.make_async_copy(
            tiles.at[slot, :, pl.ds(0, columns)],
            weights_out.at[
                pl.ds(pl.multiple_of(k * WEIGHT_ROWS, WEIGHT_ROWS), WEIGHT_ROWS), pl.ds(first, columns)
            ],
            tile_sems.at[slot],
        )

    def weight_tile(k, left, right, first, columns):
        slot = lax.rem(k, 2)

        @pl.when(k >= 2)
        def _():
            tile_copy(k - 2, slot, first, columns).wait()

        at = pl.ds(pl.multiple_of(k * WEIGHT_ROWS, WEIGHT_ROWS), WEIGHT_ROWS)
        tiles[slot, :, :columns] = dot(left[:, at], right[...], ((0,), (0,)), bf16)
        tile_copy(k, slot, first, columns).start()

    def tiles_end(first, columns):
        for k in (blocks - 2, blocks - 1):
            tile_copy(k, k % 2, first, columns).wait()

    def owners(index, first, columns):
        return Owners(
            n_xy, weights_out, first, columns, pair_in, peer_in, low, stage_sem,
            pair_sems.at[index], peer_sems.at[index],
        )

    owners_out, owners_qkv = owners(0, out_at, local), owners(1, 0, out_at)

    @pl.loop(0, blocks)
    def _(k):
        weight_tile(k, attn_low, head_low, out_at, local)

    tiles_end(out_at, local)
    owners_out.start()
    for load in loads[6:]:
        load.wait()

    def turned(at, pos, part, ref, gain):
        inner = 0.0
        for h in range(heads):
            cols = pl.ds(h * HD, HD)
            d = turn(ref[at, cols], cosine[pos], -sine[pos])
            ref[at, cols] = d
            weighted = d * raw[at, pl.ds(part * local + h * HD, HD)] * gain[:, h * HD : (h + 1) * HD]
            inner = inner + jnp.sum(weighted, axis=-1, keepdims=True)
        return inner

    def norm_back(seq):
        for j in range(1, n_ctx):

            @pl.when(me + j < n_ctx)
            def _():
                kv_copy(j, seq).wait_recv()
                at = pl.ds(seq * rows, rows)
                grad_kv[at] += in_kv[j - 1, at].astype(f32)

        def inner_chunk(at, pos):
            both = two_lanes(turned(at, pos, 0, grad_q, gain_q), turned(at, pos, 1, grad_kv, gain_k))
            sums[:, at] = lanes_to_rows(both)

        chunks(inner_chunk, seq)
        seq_rows = pl.ds(seq * rows, rows)
        pairs = [(sums.at[:, seq_rows], theirs.at[:, :, seq_rows])]
        if seq == 0:
            pairs.append((gain_a_own, gain_theirs))
        swap("tp", n_tp, pairs, sum_send.at[seq], sum_recv.at[seq])
        inner_sums = sums[:, seq_rows]
        for slot in range(n_tp - 1):
            inner_sums = inner_sums + theirs[slot, :, seq_rows]
        sums[:, seq_rows] = inner_sums / width

        def out_chunk(at, _):
            inner = rows_to_lanes(sums[:, at])
            for part, ref, gain in ((0, grad_q, gain_q), (1, grad_kv, gain_k)):
                r = stats[at, part : part + 1]
                d, v = ref[at, :local], raw[at, pl.ds(part * local, local)]
                grad_qkv[at, pl.ds((2 - part) * local, local)] = (
                    d * r * gain[...] - v * (r * r * r) * inner[:, part : part + 1]
                ).astype(bf16)
                gain_qk[part : part + 1] += jnp.sum(d * v * r, axis=0, keepdims=True)
            grad_qkv[at, :local] = grad_kv[at, local:].astype(bf16)

        chunks(out_chunk, seq)

    def gain_copies():
        return [
            pltpu.make_async_remote_copy(
                src_ref=gains, dst_ref=gains_theirs.at[k], send_sem=gain_send.at[k], recv_sem=gain_recv.at[k],
                device_id=peer, device_id_type=pl.DeviceIdType.MESH,
            )
            for k, peer in enumerate(others)
        ]

    def send_gains():
        gains[:, :local] = gain_qk[0:1]
        gains[:, local : 2 * local] = gain_qk[1:2]
        gain_total = gain_a_own[...]
        for slot in range(n_tp - 1):
            gain_total = gain_total + gain_theirs[slot]
        gains[:, 2 * local : 2 * local + width] = gain_total
        gains[:, 2 * local + width :] = gain_m_own[...]
        for copy in gain_copies():
            copy.start()

    norm_back(0)
    if seqs == 1:
        send_gains()

    span = n_tp * PIECE

    def group_rows(group):
        return pl.ds(pl.multiple_of(group * span, span), span)

    def branch_copies(group):
        at, slot = group_rows(group), lax.rem(group, 4)
        return [
            pltpu.make_async_copy(attention_hbm.at[at], branches.at[slot, 0], branch_sems.at[slot, 0]),
            pltpu.make_async_copy(down_hbm.at[at], branches.at[slot, 1], branch_sems.at[slot, 1]),
        ]

    def out_copy(group):
        slot = lax.rem(group, 2)
        return pltpu.make_async_copy(outs.at[slot], out_out.at[group_rows(group)], out_sems.at[slot])

    def own(group, total):
        for copy in branch_copies(group):
            copy.start()
        return total + mixed_own[pl.ds(pl.multiple_of(group * PIECE, PIECE), PIECE)]

    def done(group):
        copies = local_copies(
            [(line.piece_ref(group, c), grad_out.at[line.rows(group, c)]) for c in range(n_tp)], piece_sems
        )
        for copy in branch_copies(group):
            copy.wait()

        @pl.when(group >= 2)
        def _():
            out_copy(group - 2).wait()

        slot = lax.rem(group, 4)
        a, d = branches[slot, 0].astype(f32), branches[slot, 1].astype(f32)
        mixed = x[group_rows(group)].astype(f32) + a * scale_of(a) * gain_a[...]
        outs[lax.rem(group, 2)] = (mixed + d * scale_of(d) * gain_m[...]).astype(bf16)
        out_copy(group).start()
        for copy in copies:
            copy.wait()

    tile = 1024
    weights_tick = (seqs - 1) * per_seq
    weights_ticks = -(-blocks // WEIGHT_TILES)

    @pl.loop(0, line.ticks())
    def _(t):
        @pl.when((t < groups) & (lax.rem(t, per_chunk) == 0))
        def _():
            at = pl.ds(pl.multiple_of(t * span, step), step)

            @pl.loop(0, width // tile)
            def _(j):
                cols = pl.ds(pl.multiple_of(j * tile, tile), tile)
                buf[1, at, cols] = dot(grad_qkv[at], w[cols, qkv_cols], ((1,), (1,)), bf16)

        line.tick(t, own, done)

        @pl.when(t == 0)
        def _():
            owners_out.pass_on()

        for seq in range(1, seqs):

            @pl.when(t == seq * per_seq - 1)
            def _():
                norm_back(seq)
                if seq == seqs - 1:
                    send_gains()

        for m in range(WEIGHT_TILES):
            k = (t - weights_tick) * WEIGHT_TILES + m

            @pl.when((k >= 0) & (k < blocks))
            def _():
                weight_tile(k, x, grad_qkv, 0, out_at)

        @pl.when(t == weights_tick + weights_ticks - 1)
        def _():
            tiles_end(0, out_at)
            owners_qkv.start()

        @pl.when(t == weights_tick + weights_ticks)
        def _():
            owners_qkv.pass_on()

    for group in (groups - 2, groups - 1):
        out_copy(group).wait()
    gains_sum[...] = gains[...]
    for k, copy in enumerate(gain_copies()):
        copy.wait()
        gains_sum[...] += gains_theirs[k]
    owners_out.end(grad_q, local)
    owners_qkv.end(grad_q, local)
    result = pltpu.make_async_copy(grad_q.at[pl.ds(0, weights_own.shape[0])], weights_own, stage_sem)
    result.start()
    result.wait()
    for j in range(1, n_ctx):
        for seq in range(seqs):

            @pl.when(me >= j)
            def _():
                kv_copy(j, seq).wait_send()


def back(
    attn_low, w, raw, low, prev, head_low, stats, x, mixed_own, attention, down,
    gain_q, gain_k, gain_a, gain_m, gain_a_own, gain_m_own, cosine, sine, seqs, n_tp, n_xy,
):
    rows, width = x.shape
    local = head_low.shape[1]
    n_fsdp, n_ctx = n_xy
    vmem, anywhere = pl.BlockSpec(memory_space=pltpu.VMEM), pl.BlockSpec(memory_space=pl.ANY)
    shape, dma = jax.ShapeDtypeStruct, pltpu.SemaphoreType.DMA
    devices, peers = n_fsdp * n_ctx, n_fsdp // 2 * n_ctx - 1
    blocks = max(n_ctx - 1, 1)
    block = width // devices
    gains = (1, 2 * (local + width))
    acts = shape(x.shape, bf16)
    span = n_tp * PIECE
    like = lambda a: pltpu.VMEM(a.shape, a.dtype)
    return pl.pallas_call(
        functools.partial(back_kernel, n_tp, n_xy, seqs),
        out_shape=[
            acts, acts, shape(gains, f32), shape((4 * block, local), f32), shape((width, 4 * local), bf16),
        ],
        in_specs=[anywhere] * 11 + [vmem] * 8,
        out_specs=[anywhere, anywhere, vmem, anywhere, anywhere],
        scratch_shapes=line_scratch(n_tp, rows, width) + [
            like(w), like(raw), like(low), like(prev), like(prev), like(head_low), like(stats), like(x), like(mixed_own),
            pltpu.VMEM((rows, local), bf16), pltpu.VMEM((max(rows, 4 * block), local), f32),
            pltpu.VMEM((rows, 2 * local), f32),
            pltpu.VMEM((rows, 3 * local), bf16), pltpu.VMEM((2, WEIGHT_ROWS, 3 * local), bf16),
            pltpu.VMEM((width // 2, 4 * local), bf16), pltpu.VMEM((peers, block, 4 * local), bf16),
            pltpu.VMEM((4, 2, span, width), bf16), pltpu.VMEM((2, span, width), bf16),
            pltpu.VMEM(gains, f32), pltpu.VMEM((devices - 1,) + gains, f32), pltpu.VMEM((8, local), f32),
            pltpu.VMEM((8, rows), f32), pltpu.VMEM((n_tp - 1, 8, rows), f32), pltpu.VMEM((n_tp - 1, 1, width), f32),
            dma((10,)), dma((blocks, seqs)), dma((blocks, seqs)), dma((seqs, 2, n_tp - 1)), dma((seqs, 2, n_tp - 1)),
            dma((2,)), dma, dma((2, 2, n_fsdp // 2)), dma((2, 2, peers)), dma((devices - 1,)), dma((devices - 1,)),
            dma((n_tp,)), dma((4, 2)), dma((2,)),
        ],
        compiler_params=params(3),
        cost_estimate=pl.CostEstimate(flops=200 * 10**9, bytes_accessed=60 << 20, transcendentals=0),
        name="back",
    )(
        attn_low, w, raw, low, prev, head_low, stats, x, mixed_own, attention, down,
        gain_q, gain_k, gain_a, gain_m, gain_a_own, gain_m_own, cosine, sine,
    )


def rotation_tables(length):
    half = HD // 2
    frequency = rope_theta ** (-np.arange(half) * 2.0 / HD)
    angles = np.arange(length)[:, None] * frequency[None, :]
    cosine, sine = np.cos(angles), np.sin(angles)
    return (
        jnp.asarray(np.concatenate([cosine, cosine], axis=1), f32),
        jnp.asarray(np.concatenate([-sine, sine], axis=1), f32),
    )


def per_device(
    tokens, w_query, w_key, w_value, w_output, w_gate, w_up, w_down,
    gain_query, gain_key, gain_attn, gain_mlp, cotangent,
):
    micro_count, rows, width = tokens.shape
    local = w_query.shape[1]
    ctx = lax.axis_size("ctx")
    tp = lax.axis_size("tp")
    cosine, sine = rotation_tables(rows * ctx)
    gain_q = gain_query.astype(f32)
    gain_k = gain_key.astype(f32)
    gain_a = gain_attn.astype(f32)
    gain_m = gain_mlp.astype(f32)
    xy = ("fsdp", "ctx")

    def gather(w):
        return lax.all_gather(w, xy, axis=0, tiled=True)

    w_g = gather(w_gate)
    w_u = gather(w_up)
    w_down_t = gather(w_down.T)

    flat = (micro_count * rows, width)
    x_all, grad_all = tokens.reshape(flat), cotangent.reshape(flat)

    n_xy = (lax.axis_size("fsdp"), ctx)
    raw, low, prev, head_low, stats, attention, mlp_in, w_full, attn_own = front(
        x_all, w_query, w_key, w_value, w_output.T, gain_q[None], gain_k[None], gain_a[None], cosine, sine,
        micro_count, tp, n_xy
    )
    down, _, attn_low, mlp_weights, _, _, down_blocks, mixed_own, gain_m_sum, gain_a_sum = mlp(
        mlp_in, grad_all, attn_own, gain_m[None], gain_a[None], w_g, w_u, w_down_t, tp, n_xy
    )
    def scatter(full):
        return lax.psum_scatter(full, xy, scatter_dimension=0, tiled=True).astype(f32)

    units = w_gate.shape[1]
    d_mlp = scatter(mlp_weights)
    d_down = jnp.sum(down_blocks.astype(f32), axis=0).T
    d_gate, d_up = d_mlp[:, :units], d_mlp[:, units:]
    grad_tokens, out, gains, d_attn, _ = back(
        attn_low, w_full, raw, low, prev, head_low, stats, x_all, mixed_own, attention, down,
        gain_q[None], gain_k[None], gain_a[None], gain_m[None], gain_a_sum, gain_m_sum, cosine, sine,
        micro_count, tp, n_xy
    )
    gains = gains[0]
    block = w_query.shape[0]
    d_v, d_k, d_q, d_o = (d_attn[k * block : (k + 1) * block] for k in range(4))
    return (
        out.reshape(tokens.shape),
        grad_tokens.reshape(tokens.shape),
        d_q, d_k, d_v, d_o.T, d_gate, d_up, d_down,
        gains[:local], gains[local : 2 * local],
        gains[2 * local : 2 * local + width], gains[2 * local + width :],
    )


def solution(mesh):
    rows, cols = P(("fsdp", "ctx"), "tp"), P("tp", ("fsdp", "ctx"))
    acts = P("fsdp", "ctx", None)
    in_specs = (acts, rows, rows, rows, cols, rows, rows, cols, P("tp"), P("tp"), P(), P(), acts)
    out_specs = (acts, acts, rows, rows, rows, cols, rows, rows, cols, P("tp"), P("tp"), P(), P())
    return jax.shard_map(
        per_device, mesh=mesh, in_specs=in_specs, out_specs=out_specs, check_vma=False
    )
```

```python
import functools

import jax
import jax.numpy as jnp
import numpy as np
from jax import lax
from jax.experimental import pallas as pl
from jax.experimental.pallas import tpu as pltpu
from jax.sharding import PartitionSpec as P

HD = 128
norm_eps = 1e-06
rope_theta = 500000.0
masked_value = -1e30
f32 = jnp.float32
bf16 = jnp.bfloat16


def dot(a, b, dims, out=f32):
    return lax.dot_general(a, b, (dims, ((), ())), preferred_element_type=f32).astype(out)


PIECE = 16
LAG = 1
CHUNK = 256
TILE_ROWS = 256
EXTRA = 5
DOWN_PER_TICK = 2
WEIGHT_ROWS = 256
WEIGHT_TILES = 4
MLP_TILE = 1024
TILES_PER_TICK = 3


class Line:
    def __init__(self, axis, n, groups, buf, total, send, recv):
        self.axis, self.n, self.groups = axis, n, groups
        self.buf, self.total, self.send, self.recv = buf, total, send, recv
        self.i = lax.axis_index(axis)
        self.stages = 2 * n - 1

    def rows(self, group, c, count=1):
        return pl.ds(pl.multiple_of((group * self.n + c) * PIECE, PIECE), count * PIECE)

    def copy(self, way, step, group, c, source):
        rows = self.rows(group, c)
        return pltpu.make_async_remote_copy(
            src_ref=self.buf.at[source, rows],
            dst_ref=self.buf.at[0 if way == 0 else 2, rows],
            send_sem=self.send.at[way, step, group],
            recv_sem=self.recv.at[way, step, group],
            device_id={self.axis: self.i + (1 if way == 0 else -1)},
            device_id_type=pl.DeviceIdType.MESH,
        )

    def add(self, c, group, source):
        rows = self.rows(group, c)
        both = self.buf[1, rows].astype(f32) + self.buf[source, rows].astype(f32)
        self.buf[1, rows] = both.astype(bf16)

    def reduce_step(self, s, group):
        i, n = self.i, self.n

        @pl.when(i <= min(s - 1, n - 2))
        def _():
            c = n - s + i
            if s >= 2:

                @pl.when(i >= 1)
                def _():
                    self.copy(0, s - 2, group, c, 1).wait_recv()
                    self.add(c, group, 0)

            self.copy(0, s - 1, group, c, 1).start()

        @pl.when(i >= max(n - s, 1))
        def _():
            c = s + i - n
            if s >= 2:

                @pl.when(i <= n - 2)
                def _():
                    self.copy(1, s - 2, group, c, 1).wait_recv()
                    self.add(c, group, 2)

            self.copy(1, s - 1, group, c, 1).start()

    def finish(self, group, then):
        i, n = self.i, self.n
        rows = self.rows(group, i)
        self.total[...] = self.buf[1, rows].astype(f32)

        @pl.when(i >= 1)
        def _():
            self.copy(0, n - 2, group, i, 1).wait_recv()
            self.total[...] += self.buf[0, rows].astype(f32)

        @pl.when(i <= n - 2)
        def _():
            self.copy(1, n - 2, group, i, 1).wait_recv()
            self.total[...] += self.buf[2, rows].astype(f32)

        self.buf[1, rows] = then(group, self.total[...]).astype(bf16)

        @pl.when(i <= n - 2)
        def _():
            self.copy(0, n - 1, group, i, 1).start()

        @pl.when(i >= 1)
        def _():
            self.copy(1, n - 1, group, i, 1).start()

    def gather_step(self, s, group):
        i, n = self.i, self.n

        @pl.when(i >= s - 1)
        def _():
            c = i - s + 1
            self.copy(0, n + s - 3, group, c, 0).wait_recv()
            if s <= n - 1:

                @pl.when(i <= n - 2)
                def _():
                    self.copy(0, n + s - 2, group, c, 0).start()

        @pl.when(i <= n - s)
        def _():
            c = i + s - 1
            self.copy(1, n + s - 3, group, c, 2).wait_recv()
            if s <= n - 1:

                @pl.when(i >= 1)
                def _():
                    self.copy(1, n + s - 2, group, c, 2).start()

    def sent(self, group):
        i, n = self.i, self.n
        for s in range(1, n):

            @pl.when(i <= min(s - 1, n - 2))
            def _():
                self.copy(0, s - 1, group, n - s + i, 1).wait_send()

            @pl.when(i >= max(n - s, 1))
            def _():
                self.copy(1, s - 1, group, s + i - n, 1).wait_send()

            @pl.when((i >= s - 1) & (i <= n - 2))
            def _():
                self.copy(0, n + s - 2, group, i - s + 1, 1 if s == 1 else 0).wait_send()

            @pl.when((i <= n - s) & (i >= 1))
            def _():
                self.copy(1, n + s - 2, group, i + s - 1, 1 if s == 1 else 2).wait_send()

    def piece(self, group, c):
        slot = jnp.where(c < self.i, 0, jnp.where(c > self.i, 2, 1))
        return self.buf[slot, self.rows(group, c)]

    def piece_ref(self, group, c):
        slot = jnp.where(c < self.i, 0, jnp.where(c > self.i, 2, 1))
        return self.buf.at[slot, self.rows(group, c)]

    def tick(self, t, then, done):
        n = self.n

        def stage(index, body):
            group = t - index * LAG

            @pl.when((group >= 0) & (group < self.groups))
            def _():
                body(group)

        for s in range(1, n):
            stage(s - 1, functools.partial(self.reduce_step, s))
        stage(n - 1, lambda group: self.finish(group, then))
        for s in range(2, n):
            stage(n + s - 2, functools.partial(self.gather_step, s))

        def last(group):
            self.gather_step(n, group)
            self.sent(group)
            done(group)

        stage(2 * n - 2, last)

    def ticks(self):
        return self.groups + (2 * self.n - 2) * LAG


def greet(axis, n, others=()):
    i = lax.axis_index(axis)
    barrier = pltpu.get_barrier_semaphore()
    for peer in others:
        pl.semaphore_signal(barrier, inc=1, device_id=peer, device_id_type=pl.DeviceIdType.MESH)

    @pl.when(i >= 1)
    def _():
        pl.semaphore_signal(barrier, inc=1, device_id={axis: i - 1}, device_id_type=pl.DeviceIdType.MESH)

    @pl.when(i <= n - 2)
    def _():
        pl.semaphore_signal(barrier, inc=1, device_id={axis: i + 1}, device_id_type=pl.DeviceIdType.MESH)

    pl.semaphore_wait(barrier, len(others) + jnp.minimum(i, 1) + jnp.minimum(n - 1 - i, 1))


def line_scratch(n, rows, width):
    sems = pltpu.SemaphoreType.DMA((2, 2 * n - 2, rows // (n * PIECE)))
    return [pltpu.VMEM((3, rows, width), bf16), pltpu.VMEM((PIECE, width), f32), sems, sems]


def params(collective_id):
    return pltpu.CompilerParams(
        collective_id=collective_id, has_side_effects=True, vmem_limit_bytes=63 << 20
    )


def scale_of(a):
    return lax.rsqrt(jnp.mean(a * a, axis=-1, keepdims=True) + norm_eps)


def local_copies(pairs, sems):
    copies = [pltpu.make_async_copy(a, b, sems.at[k]) for k, (a, b) in enumerate(pairs)]
    for copy in copies:
        copy.start()
    return copies


def mlp_kernel(
    n, n_xy, mlp_in, grad_hbm, attn_own, gain_m, gain_a, w_g_hbm, w_u_hbm, w_d_hbm,
    down_out, hidden_out, attn_low_out, weights_out, down_full, down_pair, down_blocks, mixed_own, gain_m_sum, gain_a_sum,
    buf, total, send, recv, w_g, w_u, w_d, mlp_rows, hidden, down_low, gate, up,
    ready, w_sems, io_sems, piece_sems, tile_sems, gain_m_acc, gain_a_acc,
    grad, pair_sems, peer_sems, down_sem,
):
    rows, width = grad.shape
    units = w_g.shape[1]
    groups = rows // (n * PIECE)
    per_chunk = CHUNK // (n * PIECE)
    line = Line("tp", n, groups, buf, total, send, recv)
    i = line.i
    tile = MLP_TILE

    def weight_copies(j):
        cols = pl.ds(pl.multiple_of(j * tile, tile), tile)
        return [
            pltpu.make_async_copy(w_g_hbm.at[:, cols], w_g.at[:, cols], w_sems.at[0, j]),
            pltpu.make_async_copy(w_u_hbm.at[:, cols], w_u.at[:, cols], w_sems.at[1, j]),
        ]

    for j in range(units // tile):
        for copy in weight_copies(j):
            copy.start()
    down_weights = pltpu.make_async_copy(w_d_hbm, w_d, w_sems.at[2, 0])
    down_weights.start()
    grad_in = pltpu.make_async_copy(grad_hbm, grad, down_sem)
    grad_in.start()
    gain_m_acc[...] = jnp.zeros_like(gain_m_acc)
    gain_a_acc[...] = jnp.zeros_like(gain_a_acc)
    fsdp, n_ctx = lax.axis_index("fsdp"), n_xy[1]
    core, spots = lax.rem(fsdp, 2), n_xy[0] // 2 * n_ctx
    spot = lax.div(fsdp, 2) * n_ctx + lax.axis_index("ctx")
    other_core = {"fsdp": fsdp + 1 - 2 * core}
    peers = []
    for k in range(1, spots):
        peer = lax.rem(spot + k, spots)
        peers.append({"fsdp": 2 * lax.div(peer, n_ctx) + core, "ctx": lax.rem(peer, n_ctx)})
    greet("tp", n, [other_core] + peers)
    offset = per_chunk + line.stages + EXTRA

    def chunk_rows(chunk):
        return pl.ds(pl.multiple_of(chunk * CHUNK, CHUNK), CHUNK)

    def hidden_copy(chunk):
        return pltpu.make_async_copy(hidden, hidden_out.at[chunk_rows(chunk)], io_sems.at[1])

    def forward(chunk, first=False):
        at = chunk_rows(chunk)
        fetch = pltpu.make_async_copy(mlp_in.at[at], mlp_rows, io_sems.at[0])
        fetch.start()
        if not first:
            hidden_copy(chunk - 1).wait()
        fetch.wait()

        @pl.loop(0, units // tile)
        def _(j):
            if first:
                for copy in weight_copies(j):
                    copy.wait()
            cols = pl.ds(pl.multiple_of(j * tile, tile), tile)
            gate_proj = dot(mlp_rows[...], w_g[:, cols], ((1,), (0,)))
            up_proj = dot(mlp_rows[...], w_u[:, cols], ((1,), (0,)))
            gate[at, cols] = gate_proj.astype(bf16)
            up[at, cols] = up_proj.astype(bf16)
            hidden[:, cols] = (gate_proj / (1.0 + jnp.exp(-gate_proj)) * up_proj).astype(bf16)

        hidden_copy(chunk).start()

    def forward_down(chunk):
        at = chunk_rows(chunk)

        @pl.loop(0, width // tile)
        def _(j):
            cols = pl.ds(pl.multiple_of(j * tile, tile), tile)
            buf[1, at, cols] = dot(hidden[...], w_d[cols], ((1,), (1,)), bf16)

    def backward(chunk):
        at = chunk_rows(chunk)

        @pl.loop(0, units // tile)
        def _(j):
            cols = pl.ds(pl.multiple_of(j * tile, tile), tile)
            gate_proj, up_proj = gate[at, cols].astype(f32), up[at, cols].astype(f32)
            sig = 1.0 / (1.0 + jnp.exp(-gate_proj))
            grad_hidden = dot(down_low[at], w_d[:, cols], ((1,), (0,)))
            up[at, cols] = (grad_hidden * gate_proj * sig).astype(bf16)
            gate[at, cols] = (grad_hidden * up_proj * sig * (1.0 + gate_proj * (1.0 - sig))).astype(bf16)

    def backward_in(chunk):
        at = chunk_rows(chunk)

        @pl.loop(0, width // tile)
        def _(j):
            cols = pl.ds(pl.multiple_of(j * tile, tile), tile)
            buf[1, at, cols] = (
                dot(gate[at], w_g[cols], ((1,), (1,))) + dot(up[at], w_u[cols], ((1,), (1,)))
            ).astype(bf16)

    whole = pl.ds(0, rows)
    per_part = width // TILE_ROWS
    late_in = pltpu.make_async_copy(mlp_in, w_u.at[whole], w_sems.at[1, 0])

    def tile_rows(k):
        return pl.ds(pl.multiple_of(k * TILE_ROWS, TILE_ROWS), TILE_ROWS)

    def tile_copy(k, slot):
        part, row = lax.div(k, per_part), lax.rem(k, per_part)
        return pltpu.make_async_copy(
            w_d.at[tile_rows(slot)],
            weights_out.at[tile_rows(row), pl.ds(pl.multiple_of(part * units, units), units)],
            tile_sems.at[slot],
        )

    def weight_tile(k):
        slot = lax.rem(k, 2)
        at = tile_rows(lax.rem(k, per_part))

        @pl.when(k >= 2)
        def _():
            tile_copy(k - 2, slot).wait()

        def fill(right):
            w_d[tile_rows(slot)] = dot(w_u[whole, at], right[...], ((0,), (0,)), bf16)

        @pl.when(k < per_part)
        def _():
            fill(gate)

        @pl.when(k >= per_part)
        def _():
            fill(up)

        tile_copy(k, slot).start()

    def down_copy(k):
        return pltpu.make_async_copy(hidden, down_full.at[tile_rows(k)], down_sem)

    hidden_in = pltpu.make_async_copy(hidden_out, grad, io_sems.at[0])

    def down_tile(k):
        @pl.when(k >= 1)
        def _():
            down_copy(k - 1).wait()

        hidden[...] = dot(down_low[:, tile_rows(k)], grad[...], ((0,), (0,)), bf16)
        down_copy(k).start()

    block = width // (n_xy[0] * n_ctx)
    pair_span = n_ctx * block

    def pair_copy(chip):
        rows_at = pl.ds(pl.multiple_of((2 * chip + 1 - core) * pair_span, pair_span), pair_span)
        return pltpu.make_async_remote_copy(
            src_ref=down_full.at[rows_at], dst_ref=down_pair.at[pl.ds(chip * pair_span, pair_span)],
            send_sem=pair_sems.at[0, chip], recv_sem=pair_sems.at[1, chip],
            device_id=other_core, device_id_type=pl.DeviceIdType.MESH,
        )

    def pair_unit(u):
        chip, inside = u * CHUNK // pair_span, u * CHUNK % pair_span
        if inside == 0:
            pair_copy(chip).wait_recv()
        mine = pl.ds(pl.multiple_of((2 * chip + core) * pair_span + inside, CHUNK), CHUNK)
        there = down_pair.at[pl.ds(u * CHUNK, CHUNK)]
        loads = local_copies([(down_full.at[mine], hidden), (there, mlp_rows)], io_sems)
        for load in loads:
            load.wait()
        mlp_rows[...] = (mlp_rows[...].astype(f32) + hidden[...].astype(f32)).astype(bf16)
        store = pltpu.make_async_copy(mlp_rows, there, down_sem)
        store.start()
        store.wait()

    def spot_rows(which):
        return down_pair.at[pl.ds(pl.multiple_of(which * block, block), block)]

    def peer_copies():
        copies = [pltpu.make_async_copy(spot_rows(spot), down_blocks.at[spots - 1], peer_sems.at[0, spots - 1])]
        for k, device in enumerate(peers):
            copies.append(
                pltpu.make_async_remote_copy(
                    src_ref=spot_rows(lax.rem(spot + k + 1, spots)), dst_ref=down_blocks.at[k],
                    send_sem=peer_sems.at[0, k], recv_sem=peer_sems.at[1, k],
                    device_id=device, device_id_type=pl.DeviceIdType.MESH,
                )
            )
        return copies

    def let_in():
        @pl.when(i >= 1)
        def _():
            pl.semaphore_signal(
                ready.at[1], inc=1, device_id={"tp": i - 1}, device_id_type=pl.DeviceIdType.MESH
            )

        @pl.when(i <= n - 2)
        def _():
            pl.semaphore_signal(
                ready.at[0], inc=1, device_id={"tp": i + 1}, device_id_type=pl.DeviceIdType.MESH
            )

    def pieces_out(group, out):
        return local_copies([(line.piece_ref(group, c), out.at[line.rows(group, c)]) for c in range(n)], piece_sems)

    def down_done(group):
        copies = pieces_out(group, down_out)
        for c in range(n):
            at = line.rows(group, c)
            branch = line.piece(group, c).astype(f32)
            r = scale_of(branch)
            g = grad[at].astype(f32)
            scaled = g * gain_m[...]
            inner = jnp.mean(scaled * branch, axis=-1, keepdims=True)
            gain_m_acc[...] += g * branch * r

            @pl.when(i == c)
            def _():
                mixed_own[pl.ds(pl.multiple_of(group * PIECE, PIECE), PIECE)] = g

            down_low[at] = (r * scaled - branch * (r * r * r) * inner).astype(bf16)
        for copy in copies:
            copy.wait()

    def attn_grad(group, total):
        at = pl.ds(pl.multiple_of(group * PIECE, PIECE), PIECE)
        mixed = mixed_own[at] + total
        mixed_own[at] = mixed
        branch = attn_own[at].astype(f32)
        r = scale_of(branch)
        scaled = mixed * gain_a[...]
        inner = jnp.mean(scaled * branch, axis=-1, keepdims=True)
        gain_a_acc[...] += mixed * branch * r
        return r * scaled - branch * (r * r * r) * inner

    def attn_done(group):
        for copy in pieces_out(group, attn_low_out):
            copy.wait()

    forward(0, True)
    down_weights.wait()
    grad_in.wait()
    forward_down(0)

    @pl.loop(0, offset + line.ticks())
    def _(t):
        back = t - offset

        @pl.when((back >= 0) & (back < groups) & (lax.rem(back + groups, per_chunk) == 0))
        def _():
            @pl.when(i >= 1)
            def _():
                pl.semaphore_wait(ready.at[0], 1)

            @pl.when(i <= n - 2)
            def _():
                pl.semaphore_wait(ready.at[1], 1)

        line.tick(back, attn_grad, attn_done)
        line.tick(t, lambda group, total: total, down_done)
        for ahead, work in ((2, forward), (1, forward_down)):
            due = t + ahead

            @pl.when((due >= per_chunk) & (due < groups) & (lax.rem(due, per_chunk) == 0))
            def _():
                work(lax.div(due, per_chunk))

        for ahead, work in ((2, backward), (1, backward_in)):
            due = t + ahead - offset

            @pl.when((due >= 0) & (due < groups) & (lax.rem(due + groups, per_chunk) == 0))
            def _():
                if ahead == 1:
                    let_in()
                work(lax.div(due, per_chunk))

        down_tick = groups + line.stages - 1
        down_ticks = per_part // DOWN_PER_TICK

        @pl.when((t >= down_tick) & (t < down_tick + down_ticks))
        def _():
            @pl.when(t == down_tick)
            def _():
                hidden_copy(rows // CHUNK - 1).wait()
                hidden_in.start()
                hidden_in.wait()

            for m in range(DOWN_PER_TICK):
                down_tile((t - down_tick) * DOWN_PER_TICK + m)

        @pl.when(t == down_tick + down_ticks - 1)
        def _():
            down_copy(per_part - 1).wait()
            for chip in range(n_xy[0] // 2):
                pair_copy(chip).start()

        pair_tick = down_tick + down_ticks + 1
        units_of_pair = width // 2 // CHUNK
        for u in range(units_of_pair):

            @pl.when(t == pair_tick + u // 2)
            def _():
                pair_unit(u)
                if u == units_of_pair - 1:
                    for copy in peer_copies():
                        copy.start()

        last = offset + groups - per_chunk - 1

        @pl.when(t == last)
        def _():
            late_in.start()

        @pl.when(t == last + 1)
        def _():
            late_in.wait()

        for m in range(TILES_PER_TICK):
            k = (t - last - 1) * TILES_PER_TICK + m

            @pl.when((k >= 0) & (k < 2 * per_part))
            def _():
                weight_tile(k)

    for k in (2 * per_part - 2, 2 * per_part - 1):
        tile_copy(k, k % 2).wait()
    for copy in peer_copies():
        copy.wait()
    for chip in range(n_xy[0] // 2):
        pair_copy(chip).wait_send()
    gain_m_sum[...] = jnp.sum(gain_m_acc[...], axis=0, keepdims=True)
    gain_a_sum[...] = jnp.sum(gain_a_acc[...], axis=0, keepdims=True)


def mlp(mlp_in, grad, attn_own, gain_m, gain_a, w_g, w_u, w_d, n, n_xy):
    rows, width = grad.shape
    units = w_g.shape[1]
    vmem, anywhere = pl.BlockSpec(memory_space=pltpu.VMEM), pl.BlockSpec(memory_space=pl.ANY)
    acts = jax.ShapeDtypeStruct((rows, width), bf16)
    inner = jax.ShapeDtypeStruct((rows, units), bf16)
    spots = n_xy[0] // 2 * n_xy[1]
    gain_shape = jax.ShapeDtypeStruct((1, width), f32)
    return pl.pallas_call(
        functools.partial(mlp_kernel, n, n_xy),
        out_shape=[
            acts, inner, acts, jax.ShapeDtypeStruct((width, 2 * units), bf16),
            jax.ShapeDtypeStruct((width, units), bf16), jax.ShapeDtypeStruct((width // 2, units), bf16),
            jax.ShapeDtypeStruct((spots, width // (2 * spots), units), bf16),
            jax.ShapeDtypeStruct((rows // n, width), f32), gain_shape, gain_shape,
        ],
        in_specs=[anywhere] * 2 + [vmem] * 3 + [anywhere] * 3,
        out_specs=[anywhere] * 7 + [vmem] * 3,
        scratch_shapes=line_scratch(n, rows, width) + [
            pltpu.VMEM(w_g.shape, bf16), pltpu.VMEM(w_u.shape, bf16), pltpu.VMEM(w_d.shape, bf16),
            pltpu.VMEM((CHUNK, width), bf16), pltpu.VMEM((CHUNK, units), bf16), pltpu.VMEM((rows, width), bf16),
            pltpu.VMEM((rows, units), bf16), pltpu.VMEM((rows, units), bf16),
            pltpu.SemaphoreType.REGULAR((2,)),
            pltpu.SemaphoreType.DMA((3, units // 512)), pltpu.SemaphoreType.DMA((2,)), pltpu.SemaphoreType.DMA((n,)),
            pltpu.SemaphoreType.DMA((2,)),
            pltpu.VMEM((PIECE, width), f32), pltpu.VMEM((PIECE, width), f32),
            pltpu.VMEM((rows, width), bf16),
            pltpu.SemaphoreType.DMA((2, n_xy[0] // 2)), pltpu.SemaphoreType.DMA((2, spots)), pltpu.SemaphoreType.DMA,
        ],
        compiler_params=params(2),
        cost_estimate=pl.CostEstimate(flops=200 * 10**9, bytes_accessed=60 << 20, transcendentals=0),
        name="mlp",
    )(mlp_in, grad, attn_own, gain_m, gain_a, w_g, w_u, w_d)


def peers_of(axis, n):
    i = lax.axis_index(axis)
    return [(k - 1, lax.rem(i + k, n)) for k in range(1, n)]


def meet(axes, others=()):
    barrier = pltpu.get_barrier_semaphore()
    count = len(others)
    for peer in others:
        pl.semaphore_signal(barrier, inc=1, device_id=peer, device_id_type=pl.DeviceIdType.MESH)
    for axis, n in axes:
        for _, peer in peers_of(axis, n):
            pl.semaphore_signal(barrier, inc=1, device_id={axis: peer}, device_id_type=pl.DeviceIdType.MESH)
            count += 1
    pl.semaphore_wait(barrier, count)


def swap(axis, n, pairs, send, recv):
    copies = []
    for k, (mine, theirs) in enumerate(pairs):
        for slot, peer in peers_of(axis, n):
            copy = pltpu.make_async_remote_copy(
                src_ref=mine, dst_ref=theirs.at[slot],
                send_sem=send.at[k, slot], recv_sem=recv.at[k, slot],
                device_id={axis: peer}, device_id_type=pl.DeviceIdType.MESH,
            )
            copy.start()
            copies.append(copy)
    for copy in copies:
        copy.wait()


def lanes_to_rows(columns):
    return jnp.transpose(columns)[:8]


def rows_to_lanes(packed):
    rows = packed.shape[1]
    return jnp.transpose(jnp.concatenate([packed, jnp.zeros((120, rows), f32)], axis=0))


def two_lanes(first, second):
    lane = lax.broadcasted_iota(jnp.int32, (first.shape[0], 128), 1)
    return jnp.where(lane == 0, first, jnp.where(lane == 1, second, 0.0))


def turn(values, cosine, sine):
    return values * cosine + pltpu.roll(values, HD // 2, 1) * sine


def heads_loop(heads, body):
    @pl.loop(0, heads)
    def _(h):
        body(h, lambda part, width: pl.ds(pl.multiple_of(part * width + h * HD, HD), HD))


class Gather:
    def __init__(self, n_xy, parts, full, local_sems, sems):
        n_fsdp, self.n_ctx = n_xy
        self.chips = n_fsdp // 2
        self.parts, self.full, self.local_sems, self.sems = parts, full, local_sems, sems
        fsdp = lax.axis_index("fsdp")
        self.chip, self.core = lax.div(fsdp, 2), lax.rem(fsdp, 2)
        self.ctx = lax.axis_index("ctx")
        self.block = parts[0].shape[0]

    def place(self, part, chip, core, ctx):
        columns = self.parts[part].shape[1]
        first = sum(p.shape[1] for p in self.parts[:part])
        row = ((2 * chip + core) * self.n_ctx + ctx) * self.block
        return self.full.at[pl.ds(pl.multiple_of(row, self.block), self.block), pl.ds(first, columns)]

    def send(self, part, slot, source, target, device):
        return pltpu.make_async_remote_copy(
            src_ref=source, dst_ref=target,
            send_sem=self.sems.at[0, part, slot], recv_sem=self.sems.at[1, part, slot],
            device_id=device, device_id_type=pl.DeviceIdType.MESH,
        )

    def keep(self, part):
        return pltpu.make_async_copy(
            self.parts[part], self.place(part, self.chip, self.core, self.ctx), self.local_sems.at[part]
        )

    def to_ctx(self, part, k):
        target = self.place(part, self.chip, self.core, self.ctx)
        return self.send(part, k - 1, self.parts[part], target, {"ctx": lax.rem(self.ctx + k, self.n_ctx)})

    def to_chip(self, part, c, k):
        ctx = lax.rem(self.ctx + self.n_ctx - c, self.n_ctx)
        target = self.place(part, self.chip, self.core, ctx)
        source = self.parts[part] if c == 0 else target
        slot = self.n_ctx - 1 + c * (self.chips - 1) + k - 1
        chip = lax.rem(self.chip + k, self.chips)
        return self.send(part, slot, source, target, {"fsdp": 2 * chip + self.core})

    def to_core(self, part, c, k):
        ctx = lax.rem(self.ctx + self.n_ctx - c, self.n_ctx)
        chip = lax.rem(self.chip + self.chips - k, self.chips)
        target = self.place(part, chip, self.core, ctx)
        source = self.parts[part] if c == 0 and k == 0 else target
        slot = self.n_ctx - 1 + self.n_ctx * (self.chips - 1) + c * self.chips + k
        return self.send(part, slot, source, target, {"fsdp": 2 * self.chip + 1 - self.core})

    def slots(self):
        return self.n_ctx - 1 + self.n_ctx * (self.chips - 1) + self.n_ctx * self.chips

    def start(self, part):
        self.keep(part).start()
        for k in range(1, self.n_ctx):
            self.to_ctx(part, k).start()
        for k in range(1, self.chips):
            self.to_chip(part, 0, k).start()
        self.to_core(part, 0, 0).start()

    def pass_on(self, part):
        for c in range(1, self.n_ctx):
            self.to_ctx(part, c).wait_recv()
            for k in range(1, self.chips):
                self.to_chip(part, c, k).start()
            self.to_core(part, c, 0).start()
        for c in range(self.n_ctx):
            for k in range(1, self.chips):
                self.to_chip(part, c, k).wait_recv()
                self.to_core(part, c, k).start()

    def end(self, part):
        for c in range(self.n_ctx):
            for k in range(self.chips):
                self.to_core(part, c, k).wait_recv()
        self.keep(part).wait()

    def sent(self, part):
        for k in range(1, self.n_ctx):
            self.to_ctx(part, k).wait_send()
        for c in range(self.n_ctx):
            for k in range(1, self.chips):
                self.to_chip(part, c, k).wait_send()
            for k in range(self.chips):
                self.to_core(part, c, k).wait_send()


def front_kernel(
    n_tp, n_xy, seqs, x_hbm, w_q, w_k, w_v, w_o, gain_q, gain_k, gain_a, cosine, sine,
    raw_out, low_out, prev_out, head_low_out, stats_out, attention_out, mlp_in_out, w_out, attn_own_out,
    buf, total, send, recv, x, w, raw, low, prev, head_low, stats, mlp_in, attn_own,
    sums, theirs, kv_send, kv_recv, sum_send, sum_recv, w_local_sems, w_sems, io_sems, piece_sems, group_sems,
):
    n_ctx = n_xy[1]
    rows_all, width = x.shape
    rows = rows_all // seqs
    local = w_q.shape[1]
    heads = local // HD
    me = lax.axis_index("ctx")
    scale = HD ** (-0.5)
    step = min(256, rows)
    fetch_x = pltpu.make_async_copy(x_hbm, x, io_sems.at[0])
    fetch_x.start()
    gather = Gather(n_xy, [w_v, w_k, w_q, w_o], w, w_local_sems, w_sems)
    value_at, key_at, query_at, out_at = 0, local, 2 * local, 3 * local
    fsdp = lax.axis_index("fsdp")
    meet(
        [("tp", n_tp), ("ctx", n_ctx)],
        [{"fsdp": 2 * lax.div(fsdp, 2) + 1 - lax.rem(fsdp, 2)}]
        + [{"fsdp": lax.rem(fsdp + 2 * k, n_xy[0])} for k in range(1, n_xy[0] // 2)],
    )
    for part in range(4):
        gather.start(part)

    def chunks(body):
        @pl.loop(0, rows_all // step)
        def _(k):
            at = pl.ds(pl.multiple_of(k * step, step), step)
            body(at, pl.ds(pl.multiple_of(me * rows + lax.rem(k, rows // step) * step, step), step))

    for j in range(1, n_ctx):

        @pl.when(me < j)
        def _():
            prev[j - 1] = jnp.zeros(prev.shape[1:], bf16)

    def kv_copy(j, part, seq):
        at = pl.ds(seq * rows, rows)
        return pltpu.make_async_remote_copy(
            src_ref=low.at[at, pl.ds((1 + part) * local, local)],
            dst_ref=prev.at[j - 1, at, pl.ds(part * local, local)],
            send_sem=kv_send.at[j - 1, part, seq], recv_sem=kv_recv.at[j - 1, part, seq],
            device_id={"ctx": lax.rem(me + j, n_ctx)}, device_id_type=pl.DeviceIdType.MESH,
        )

    def kv_each(method, part, seq, here):
        for j in range(1, n_ctx):

            @pl.when((me >= j) if here else (me + j < n_ctx))
            def _():
                getattr(kv_copy(j, part, seq), method)()

    gather.pass_on(0)
    gather.pass_on(1)
    gather.end(0)
    fetch_x.wait()

    def value_chunk(at, _):
        low[at, 2 * local :] = dot(x[at], w[:, value_at : value_at + local], ((1,), (0,)), bf16)

    chunks(value_chunk)
    for seq in range(seqs):
        kv_each("start", 1, seq, False)
    gather.pass_on(2)
    gather.end(1)

    def raw_chunk(part, first):
        def chunk(at, _):
            v = dot(x[at], w[:, first : first + local], ((1,), (0,)))
            raw[at, part * local : (part + 1) * local] = v
            square = jnp.sum(v * v, axis=-1, keepdims=True)
            lane = lax.broadcasted_iota(jnp.int32, (step, 128), 1)
            stats[at] = jnp.where(lane == part, square, stats[at] if part == 0 else 0.0)

        chunks(chunk)

    raw_chunk(1, key_at)
    gather.pass_on(3)
    gather.end(2)
    raw_chunk(0, query_at)

    def sums_chunk(at, _):
        sums[:, at] = lanes_to_rows(stats[at])

    chunks(sums_chunk)
    swap("tp", n_tp, [(sums, theirs)], sum_send, sum_recv)
    square_sums = sums[...]
    for slot in range(n_tp - 1):
        square_sums = square_sums + theirs[slot]
    stats[...] = rows_to_lanes(lax.rsqrt(square_sums / width + norm_eps))

    def turned(part, gain):
        def chunk(at, pos):
            r = stats[at, part : part + 1]
            for h in range(heads):
                cols = pl.ds(part * local + h * HD, HD)
                v = raw[at, cols] * r * gain[:, h * HD : (h + 1) * HD]
                low[at, cols] = turn(v, cosine[pos], sine[pos]).astype(bf16)

        chunks(chunk)

    turned(1, gain_k)
    for seq in range(seqs):
        kv_each("start", 0, seq, False)
    turned(0, gain_q)
    lane = lax.broadcasted_iota(jnp.int32, (step, 128), 1)

    def attention(seq):
        for part in range(2):
            kv_each("wait_recv", part, seq, True)
        seq_rows = pl.ds(seq * rows, rows)

        def one_head(h, cols):
            for tile in range(rows // step):
                at = pl.ds(seq * rows + tile * step, step)
                q = low[at, cols(0, local)]
                seen = (tile + 1) * step
                own = pl.ds(seq * rows, seen)
                s = dot(q, low[own, cols(1, local)], ((1,), (1,))) * scale
                i_pos = lax.broadcasted_iota(jnp.int32, (step, seen), 0) + tile * step
                j_pos = lax.broadcasted_iota(jnp.int32, (step, seen), 1)
                scores = [jnp.where(j_pos <= i_pos, s, masked_value)]
                values = [low[own, cols(2, local)]]
                for j in range(1, n_ctx):
                    s = dot(q, prev[j - 1, seq_rows, cols(0, local)], ((1,), (1,))) * scale
                    scores.append(jnp.where(me >= j, s, masked_value))
                    values.append(prev[j - 1, seq_rows, cols(1, local)])
                top = scores[0].max(-1, keepdims=True)
                for s in scores[1:]:
                    top = jnp.maximum(top, s.max(-1, keepdims=True))
                total, weighted = 0.0, 0.0
                for s, v in zip(scores, values):
                    e = jnp.exp(s - top)
                    total = total + e.sum(-1, keepdims=True)
                    weighted = weighted + dot(e.astype(bf16), v, ((1,), (0,)))
                head_low[at, cols(0, local)] = (weighted / total).astype(bf16)
                stats[at] = jnp.where(lane == h + 2, top + jnp.log(total), stats[at])

        heads_loop(heads, one_head)

    attention(0)
    gather.end(3)

    groups = rows_all // (n_tp * PIECE)
    line = Line("tp", n_tp, groups, buf, total, send, recv)
    per_chunk, per_seq = step // (n_tp * PIECE), rows // (n_tp * PIECE)
    tile = 512

    def group_rows(group):
        return pl.ds(pl.multiple_of(group * n_tp * PIECE, n_tp * PIECE), n_tp * PIECE)

    def mlp_copy(group):
        at = group_rows(group)
        return pltpu.make_async_copy(mlp_in.at[at], mlp_in_out.at[at], group_sems.at[group])

    def own(group, total):
        attn_own[pl.ds(pl.multiple_of(group * PIECE, PIECE), PIECE)] = total.astype(bf16)
        return total

    def done(group):
        copies = local_copies(
            [(line.piece_ref(group, c), attention_out.at[line.rows(group, c)]) for c in range(n_tp)], piece_sems
        )
        for c in range(n_tp):
            at = line.rows(group, c)
            a = line.piece(group, c).astype(f32)
            mlp_in[at] = (x[at].astype(f32) + a * scale_of(a) * gain_a[...]).astype(bf16)
        mlp_copy(group).start()
        for copy in copies:
            copy.wait()

    saves = [
        (raw, raw_out), (low, low_out), (prev, prev_out), (head_low, head_low_out), (stats, stats_out), (w, w_out),
    ]

    @pl.loop(0, line.ticks())
    def _(t):
        @pl.when((t < groups) & (lax.rem(t, per_chunk) == 0))
        def _():
            at = pl.ds(pl.multiple_of(t * n_tp * PIECE, step), step)

            @pl.loop(0, width // tile)
            def _(j):
                cols = pl.ds(pl.multiple_of(j * tile, tile), tile)
                buf[1, at, cols] = dot(head_low[at], w[cols, out_at : out_at + local], ((1,), (1,)), bf16)

        line.tick(t, own, done)
        for seq in range(1, seqs):

            @pl.when(t == seq * per_seq - 1)
            def _():
                attention(seq)

        @pl.when(t == (seqs - 1) * per_seq)
        def _():
            for k, (source, target) in enumerate(saves):
                pltpu.make_async_copy(source, target, io_sems.at[k]).start()

    own_out = pltpu.make_async_copy(attn_own, attn_own_out, piece_sems.at[0])
    own_out.start()
    for k, (source, target) in enumerate(saves):
        pltpu.make_async_copy(source, target, io_sems.at[k]).wait()
    own_out.wait()

    @pl.loop(0, groups)
    def _(group):
        mlp_copy(group).wait()

    for part in range(4):
        gather.sent(part)
    for seq in range(seqs):
        for part in range(2):
            kv_each("wait_send", part, seq, False)


def front(x, w_q, w_k, w_v, w_o, gain_q, gain_k, gain_a, cosine, sine, seqs, n_tp, n_xy):
    rows, width = x.shape
    local = w_q.shape[1]
    n_fsdp, n_ctx = n_xy
    chips = n_fsdp // 2
    vmem, anywhere = pl.BlockSpec(memory_space=pltpu.VMEM), pl.BlockSpec(memory_space=pl.ANY)
    shape = jax.ShapeDtypeStruct
    dma = pltpu.SemaphoreType.DMA
    saved = [
        shape((rows, 2 * local), f32), shape((rows, 3 * local), bf16),
        shape((max(n_ctx - 1, 1), rows, 2 * local), bf16),
        shape((rows, local), bf16), shape((rows, 128), f32),
    ]
    acts, full = shape(x.shape, bf16), shape((width, 4 * local), bf16)
    vmem_of = [pltpu.VMEM(a.shape, a.dtype) for a in saved]
    slots = n_ctx - 1 + n_ctx * (chips - 1) + n_ctx * chips
    kv_sems, sum_sems = dma((max(n_ctx - 1, 1), 2, seqs)), dma((1, n_tp - 1))
    return pl.pallas_call(
        functools.partial(front_kernel, n_tp, n_xy, seqs),
        out_shape=saved + [acts, acts, full, shape((rows // n_tp, width), bf16)],
        in_specs=[anywhere] + [vmem] * 9,
        out_specs=[anywhere] * 9,
        scratch_shapes=line_scratch(n_tp, rows, width) + [
            pltpu.VMEM(x.shape, bf16), pltpu.VMEM(full.shape, bf16), *vmem_of, pltpu.VMEM(x.shape, bf16),
            pltpu.VMEM((rows // n_tp, width), bf16),
            pltpu.VMEM((8, rows), f32), pltpu.VMEM((n_tp - 1, 8, rows), f32),
            kv_sems, kv_sems, sum_sems, sum_sems, dma((4,)), dma((2, 4, slots)), dma((7,)), dma((n_tp,)),
            dma((rows // (n_tp * PIECE),)),
        ],
        compiler_params=params(1),
        cost_estimate=pl.CostEstimate(flops=150 * 10**9, bytes_accessed=30 << 20, transcendentals=0),
        name="front",
    )(x, w_q, w_k, w_v, w_o, gain_q, gain_k, gain_a, cosine, sine)


class Owners:
    def __init__(self, n_xy, full, first, columns, pair_in, peer_in, stage, stage_sem, pair_sems, peer_sems):
        n_fsdp, self.n_ctx = n_xy
        self.chips = n_fsdp // 2
        self.first, self.columns = first, columns
        self.full, self.pair_in, self.peer_in = full, pair_in, peer_in
        self.stage, self.stage_sem = stage, stage_sem
        self.pair_sems, self.peer_sems = pair_sems, peer_sems
        fsdp = lax.axis_index("fsdp")
        self.chip, self.core = lax.div(fsdp, 2), lax.rem(fsdp, 2)
        self.place = self.chip * self.n_ctx + lax.axis_index("ctx")
        self.block = full.shape[0] // (n_fsdp * self.n_ctx)
        self.span = self.n_ctx * self.block

    def cols(self):
        return pl.ds(self.first, self.columns)

    def pair_copy(self, chip):
        there = 1 - self.core
        rows = pl.ds(pl.multiple_of((2 * chip + there) * self.span, self.span), self.span)
        return pltpu.make_async_remote_copy(
            src_ref=self.full.at[rows, self.cols()],
            dst_ref=self.pair_in.at[pl.ds(chip * self.span, self.span), self.cols()],
            send_sem=self.pair_sems.at[0, chip], recv_sem=self.pair_sems.at[1, chip],
            device_id={"fsdp": 2 * self.chip + there}, device_id_type=pl.DeviceIdType.MESH,
        )

    def peer_copy(self, k):
        place = lax.rem(self.place + k, self.chips * self.n_ctx)
        return pltpu.make_async_remote_copy(
            src_ref=self.pair_in.at[self.block_rows(place), self.cols()],
            dst_ref=self.peer_in.at[k - 1, :, self.cols()],
            send_sem=self.peer_sems.at[0, k - 1], recv_sem=self.peer_sems.at[1, k - 1],
            device_id={"fsdp": 2 * lax.div(place, self.n_ctx) + self.core, "ctx": lax.rem(place, self.n_ctx)},
            device_id_type=pl.DeviceIdType.MESH,
        )

    def block_rows(self, place):
        return pl.ds(pl.multiple_of(place * self.block, self.block), self.block)

    def start(self):
        for chip in range(self.chips):
            self.pair_copy(chip).start()

    def pass_on(self):
        unit = min(self.span, self.stage.shape[0])
        for chip in range(self.chips):
            for u in range(self.span // unit):
                mine = pl.multiple_of((2 * chip + self.core) * self.span + u * unit, unit)
                fetch = pltpu.make_async_copy(
                    self.full.at[pl.ds(mine, unit), self.cols()],
                    self.stage.at[pl.ds(0, unit), pl.ds(0, self.columns)], self.stage_sem,
                )
                fetch.start()
                if u == 0:
                    self.pair_copy(chip).wait_recv()
                fetch.wait()
                rows = pl.ds(chip * self.span + u * unit, unit)
                both = self.pair_in[rows, self.cols()].astype(f32) + self.stage[:unit, : self.columns].astype(f32)
                self.pair_in[rows, self.cols()] = both.astype(bf16)
        for k in range(1, self.chips * self.n_ctx):
            self.peer_copy(k).start()

    def end(self, result, width):
        for k in range(1, self.chips * self.n_ctx):
            self.peer_copy(k).wait()
        for part in range(self.first // width, (self.first + self.columns) // width):
            cols = pl.ds(part * width, width)
            sums = self.pair_in[self.block_rows(self.place), cols].astype(f32)
            for k in range(1, self.chips * self.n_ctx):
                sums = sums + self.peer_in[k - 1, :, cols].astype(f32)
            result[part * self.block : (part + 1) * self.block] = sums
        for chip in range(self.chips):
            self.pair_copy(chip).wait_send()


def back_kernel(
    n_tp, n_xy, seqs,
    attn_low_hbm, w_hbm, raw_hbm, low_hbm, prev_hbm, head_low_hbm, stats_hbm, x_hbm, mixed_own_hbm,
    attention_hbm, down_hbm, gain_q, gain_k, gain_a, gain_m, gain_a_own, gain_m_own, cosine, sine,
    grad_out, out_out, gains_sum, weights_own, weights_out,
    buf, total, send, recv, w, raw, low, kv, in_kv, head_low, stats, x, mixed_own, grad_heads, grad_q, grad_kv,
    grad_qkv, tiles, pair_in, peer_in, branches, outs, gains, gains_theirs, gain_qk,
    sums, theirs, gain_theirs, load_sems, kv_send, kv_recv, sum_send, sum_recv, tile_sems, stage_sem,
    pair_sems, peer_sems, gain_send, gain_recv, piece_sems, branch_sems, out_sems,
):
    n_fsdp, n_ctx = n_xy
    rows_all, width = x.shape
    rows = rows_all // seqs
    local = head_low.shape[1]
    heads = local // HD
    me = lax.axis_index("ctx")
    scale = HD ** (-0.5)
    step = min(256, rows)
    out_at = 3 * local
    groups = rows_all // (n_tp * PIECE)
    line = Line("tp", n_tp, groups, buf, total, send, recv)
    per_chunk, per_seq = step // (n_tp * PIECE), rows // (n_tp * PIECE)
    attn_low = buf.at[1]
    qkv_cols, out_cols = pl.ds(0, out_at), pl.ds(out_at, local)
    loads = local_copies(
        [
            (attn_low_hbm, attn_low), (w_hbm.at[:, out_cols], w.at[:, out_cols]), (prev_hbm, kv), (low_hbm, low),
            (head_low_hbm, head_low), (stats_hbm, stats), (raw_hbm, raw), (x_hbm, x),
            (w_hbm.at[:, qkv_cols], w.at[:, qkv_cols]), (mixed_own_hbm, mixed_own),
        ],
        load_sems,
    )
    place = lax.axis_index("fsdp") * n_ctx + me
    others = []
    for k in range(1, n_fsdp * n_ctx):
        peer = lax.rem(place + k, n_fsdp * n_ctx)
        others.append({"fsdp": lax.div(peer, n_ctx), "ctx": lax.rem(peer, n_ctx)})
    meet([("tp", n_tp)], others)

    def chunks(body, seq=None):
        count = rows_all if seq is None else rows
        first = 0 if seq is None else seq * rows

        @pl.loop(0, count // step)
        def _(k):
            at = pl.ds(pl.multiple_of(first + k * step, step), step)
            body(at, pl.ds(pl.multiple_of(me * rows + lax.rem(k, rows // step) * step, step), step))

    loads[0].wait()
    loads[1].wait()

    def heads_chunk(at, _):
        grad_heads[at] = dot(attn_low[at], w[:, out_cols], ((1,), (0,)), bf16)

    chunks(heads_chunk)
    grad_q[...] = jnp.zeros_like(grad_q)
    grad_kv[...] = jnp.zeros_like(grad_kv)
    gain_qk[...] = jnp.zeros_like(gain_qk)
    for load in loads[2:6]:
        load.wait()

    def kv_copy(j, seq):
        at = pl.ds(seq * rows, rows)
        return pltpu.make_async_remote_copy(
            src_ref=kv.at[j - 1, at], dst_ref=in_kv.at[j - 1, at],
            send_sem=kv_send.at[j - 1, seq], recv_sem=kv_recv.at[j - 1, seq],
            device_id={"ctx": lax.rem(me + n_ctx - j, n_ctx)}, device_id_type=pl.DeviceIdType.MESH,
        )

    def lane_of(at, index):
        lane = lax.broadcasted_iota(jnp.int32, (step, 128), 1)
        return jnp.sum(jnp.where(lane == index, stats[at], 0.0), axis=-1, keepdims=True)

    def block(h, cols, at, keys, values, mask):
        q, g = low[at, cols(0, local)], grad_heads[at, cols(0, local)]
        delta = jnp.sum(g.astype(f32) * head_low[at, cols(0, local)].astype(f32), axis=-1, keepdims=True)
        s = dot(q, keys, ((1,), (1,))) * scale
        p = jnp.exp(s - lane_of(at, h + 2))
        if mask is not None:
            p = jnp.where(mask, p, 0.0)
        dp = dot(g, values, ((1,), (1,)))
        ds = (p * (dp - delta)).astype(bf16)
        grad_q[at, cols(0, local)] += dot(ds, keys, ((1,), (0,))) * scale
        return dot(ds, q, ((0,), (0,))) * scale, dot(p.astype(bf16), g, ((0,), (0,)))

    for j in range(1, n_ctx):

        @pl.when(me >= j)
        def _():
            for seq in range(seqs):
                seq_rows = pl.ds(seq * rows, rows)

                def one_head(h, cols):
                    keys, values = kv[j - 1, seq_rows, cols(0, local)], kv[j - 1, seq_rows, cols(1, local)]
                    dk, dv = 0.0, 0.0
                    for tile in range(rows // step):
                        at = pl.ds(seq * rows + tile * step, step)
                        k_term, v_term = block(h, cols, at, keys, values, None)
                        dk, dv = dk + k_term, dv + v_term
                    kv[j - 1, seq_rows, cols(0, local)] = dk.astype(bf16)
                    kv[j - 1, seq_rows, cols(1, local)] = dv.astype(bf16)

                heads_loop(heads, one_head)
                kv_copy(j, seq).start()

    for seq in range(seqs):

        def one_head(h, cols):
            for tile in range(rows // step):
                at = pl.ds(seq * rows + tile * step, step)
                seen = (tile + 1) * step
                own = pl.ds(seq * rows, seen)
                i_pos = lax.broadcasted_iota(jnp.int32, (step, seen), 0) + tile * step
                j_pos = lax.broadcasted_iota(jnp.int32, (step, seen), 1)
                k_term, v_term = block(
                    h, cols, at, low[own, cols(1, local)], low[own, cols(2, local)], j_pos <= i_pos
                )
                grad_kv[own, cols(0, local)] += k_term
                grad_kv[own, cols(1, local)] += v_term

        heads_loop(heads, one_head)

    blocks = width // WEIGHT_ROWS

    def tile_copy(k, slot, first, columns):
        return pltpu.make_async_copy(
            tiles.at[slot, :, pl.ds(0, columns)],
            weights_out.at[
                pl.ds(pl.multiple_of(k * WEIGHT_ROWS, WEIGHT_ROWS), WEIGHT_ROWS), pl.ds(first, columns)
            ],
            tile_sems.at[slot],
        )

    def weight_tile(k, left, right, first, columns):
        slot = lax.rem(k, 2)

        @pl.when(k >= 2)
        def _():
            tile_copy(k - 2, slot, first, columns).wait()

        at = pl.ds(pl.multiple_of(k * WEIGHT_ROWS, WEIGHT_ROWS), WEIGHT_ROWS)
        tiles[slot, :, :columns] = dot(left[:, at], right[...], ((0,), (0,)), bf16)
        tile_copy(k, slot, first, columns).start()

    def tiles_end(first, columns):
        for k in (blocks - 2, blocks - 1):
            tile_copy(k, k % 2, first, columns).wait()

    def owners(index, first, columns):
        return Owners(
            n_xy, weights_out, first, columns, pair_in, peer_in, low, stage_sem,
            pair_sems.at[index], peer_sems.at[index],
        )

    owners_out, owners_qkv = owners(0, out_at, local), owners(1, 0, out_at)

    @pl.loop(0, blocks)
    def _(k):
        weight_tile(k, attn_low, head_low, out_at, local)

    tiles_end(out_at, local)
    owners_out.start()
    for load in loads[6:]:
        load.wait()

    def turned(at, pos, part, ref, gain):
        inner = 0.0
        for h in range(heads):
            cols = pl.ds(h * HD, HD)
            d = turn(ref[at, cols], cosine[pos], -sine[pos])
            ref[at, cols] = d
            weighted = d * raw[at, pl.ds(part * local + h * HD, HD)] * gain[:, h * HD : (h + 1) * HD]
            inner = inner + jnp.sum(weighted, axis=-1, keepdims=True)
        return inner

    def norm_back(seq):
        for j in range(1, n_ctx):

            @pl.when(me + j < n_ctx)
            def _():
                kv_copy(j, seq).wait_recv()
                at = pl.ds(seq * rows, rows)
                grad_kv[at] += in_kv[j - 1, at].astype(f32)

        def inner_chunk(at, pos):
            both = two_lanes(turned(at, pos, 0, grad_q, gain_q), turned(at, pos, 1, grad_kv, gain_k))
            sums[:, at] = lanes_to_rows(both)

        chunks(inner_chunk, seq)
        seq_rows = pl.ds(seq * rows, rows)
        pairs = [(sums.at[:, seq_rows], theirs.at[:, :, seq_rows])]
        if seq == 0:
            pairs.append((gain_a_own, gain_theirs))
        swap("tp", n_tp, pairs, sum_send.at[seq], sum_recv.at[seq])
        inner_sums = sums[:, seq_rows]
        for slot in range(n_tp - 1):
            inner_sums = inner_sums + theirs[slot, :, seq_rows]
        sums[:, seq_rows] = inner_sums / width

        def out_chunk(at, _):
            inner = rows_to_lanes(sums[:, at])
            for part, ref, gain in ((0, grad_q, gain_q), (1, grad_kv, gain_k)):
                r = stats[at, part : part + 1]
                d, v = ref[at, :local], raw[at, pl.ds(part * local, local)]
                grad_qkv[at, pl.ds((2 - part) * local, local)] = (
                    d * r * gain[...] - v * (r * r * r) * inner[:, part : part + 1]
                ).astype(bf16)
                gain_qk[part : part + 1] += jnp.sum(d * v * r, axis=0, keepdims=True)
            grad_qkv[at, :local] = grad_kv[at, local:].astype(bf16)

        chunks(out_chunk, seq)

    def gain_copies():
        return [
            pltpu.make_async_remote_copy(
                src_ref=gains, dst_ref=gains_theirs.at[k], send_sem=gain_send.at[k], recv_sem=gain_recv.at[k],
                device_id=peer, device_id_type=pl.DeviceIdType.MESH,
            )
            for k, peer in enumerate(others)
        ]

    def send_gains():
        gains[:, :local] = gain_qk[0:1]
        gains[:, local : 2 * local] = gain_qk[1:2]
        gain_total = gain_a_own[...]
        for slot in range(n_tp - 1):
            gain_total = gain_total + gain_theirs[slot]
        gains[:, 2 * local : 2 * local + width] = gain_total
        gains[:, 2 * local + width :] = gain_m_own[...]
        for copy in gain_copies():
            copy.start()

    norm_back(0)
    if seqs == 1:
        send_gains()

    span = n_tp * PIECE

    def group_rows(group):
        return pl.ds(pl.multiple_of(group * span, span), span)

    def branch_copies(group):
        at, slot = group_rows(group), lax.rem(group, 4)
        return [
            pltpu.make_async_copy(attention_hbm.at[at], branches.at[slot, 0], branch_sems.at[slot, 0]),
            pltpu.make_async_copy(down_hbm.at[at], branches.at[slot, 1], branch_sems.at[slot, 1]),
        ]

    def out_copy(group):
        slot = lax.rem(group, 2)
        return pltpu.make_async_copy(outs.at[slot], out_out.at[group_rows(group)], out_sems.at[slot])

    def own(group, total):
        for copy in branch_copies(group):
            copy.start()
        return total + mixed_own[pl.ds(pl.multiple_of(group * PIECE, PIECE), PIECE)]

    def done(group):
        copies = local_copies(
            [(line.piece_ref(group, c), grad_out.at[line.rows(group, c)]) for c in range(n_tp)], piece_sems
        )
        for copy in branch_copies(group):
            copy.wait()

        @pl.when(group >= 2)
        def _():
            out_copy(group - 2).wait()

        slot = lax.rem(group, 4)
        a, d = branches[slot, 0].astype(f32), branches[slot, 1].astype(f32)
        mixed = x[group_rows(group)].astype(f32) + a * scale_of(a) * gain_a[...]
        outs[lax.rem(group, 2)] = (mixed + d * scale_of(d) * gain_m[...]).astype(bf16)
        out_copy(group).start()
        for copy in copies:
            copy.wait()

    tile = 1024
    weights_tick = (seqs - 1) * per_seq
    weights_ticks = -(-blocks // WEIGHT_TILES)

    @pl.loop(0, line.ticks())
    def _(t):
        @pl.when((t < groups) & (lax.rem(t, per_chunk) == 0))
        def _():
            at = pl.ds(pl.multiple_of(t * span, step), step)

            @pl.loop(0, width // tile)
            def _(j):
                cols = pl.ds(pl.multiple_of(j * tile, tile), tile)
                buf[1, at, cols] = dot(grad_qkv[at], w[cols, qkv_cols], ((1,), (1,)), bf16)

        line.tick(t, own, done)

        @pl.when(t == 0)
        def _():
            owners_out.pass_on()

        for seq in range(1, seqs):

            @pl.when(t == seq * per_seq - 1)
            def _():
                norm_back(seq)
                if seq == seqs - 1:
                    send_gains()

        for m in range(WEIGHT_TILES):
            k = (t - weights_tick) * WEIGHT_TILES + m

            @pl.when((k >= 0) & (k < blocks))
            def _():
                weight_tile(k, x, grad_qkv, 0, out_at)

        @pl.when(t == weights_tick + weights_ticks - 1)
        def _():
            tiles_end(0, out_at)
            owners_qkv.start()

        @pl.when(t == weights_tick + weights_ticks)
        def _():
            owners_qkv.pass_on()

    for group in (groups - 2, groups - 1):
        out_copy(group).wait()
    gains_sum[...] = gains[...]
    for k, copy in enumerate(gain_copies()):
        copy.wait()
        gains_sum[...] += gains_theirs[k]
    owners_out.end(grad_q, local)
    owners_qkv.end(grad_q, local)
    result = pltpu.make_async_copy(grad_q.at[pl.ds(0, weights_own.shape[0])], weights_own, stage_sem)
    result.start()
    result.wait()
    for j in range(1, n_ctx):
        for seq in range(seqs):

            @pl.when(me >= j)
            def _():
                kv_copy(j, seq).wait_send()


def back(
    attn_low, w, raw, low, prev, head_low, stats, x, mixed_own, attention, down,
    gain_q, gain_k, gain_a, gain_m, gain_a_own, gain_m_own, cosine, sine, seqs, n_tp, n_xy,
):
    rows, width = x.shape
    local = head_low.shape[1]
    n_fsdp, n_ctx = n_xy
    vmem, anywhere = pl.BlockSpec(memory_space=pltpu.VMEM), pl.BlockSpec(memory_space=pl.ANY)
    shape, dma = jax.ShapeDtypeStruct, pltpu.SemaphoreType.DMA
    devices, peers = n_fsdp * n_ctx, n_fsdp // 2 * n_ctx - 1
    blocks = max(n_ctx - 1, 1)
    block = width // devices
    gains = (1, 2 * (local + width))
    acts = shape(x.shape, bf16)
    span = n_tp * PIECE
    like = lambda a: pltpu.VMEM(a.shape, a.dtype)
    return pl.pallas_call(
        functools.partial(back_kernel, n_tp, n_xy, seqs),
        out_shape=[
            acts, acts, shape(gains, f32), shape((4 * block, local), f32), shape((width, 4 * local), bf16),
        ],
        in_specs=[anywhere] * 11 + [vmem] * 8,
        out_specs=[anywhere, anywhere, vmem, anywhere, anywhere],
        scratch_shapes=line_scratch(n_tp, rows, width) + [
            like(w), like(raw), like(low), like(prev), like(prev), like(head_low), like(stats), like(x), like(mixed_own),
            pltpu.VMEM((rows, local), bf16), pltpu.VMEM((max(rows, 4 * block), local), f32),
            pltpu.VMEM((rows, 2 * local), f32),
            pltpu.VMEM((rows, 3 * local), bf16), pltpu.VMEM((2, WEIGHT_ROWS, 3 * local), bf16),
            pltpu.VMEM((width // 2, 4 * local), bf16), pltpu.VMEM((peers, block, 4 * local), bf16),
            pltpu.VMEM((4, 2, span, width), bf16), pltpu.VMEM((2, span, width), bf16),
            pltpu.VMEM(gains, f32), pltpu.VMEM((devices - 1,) + gains, f32), pltpu.VMEM((8, local), f32),
            pltpu.VMEM((8, rows), f32), pltpu.VMEM((n_tp - 1, 8, rows), f32), pltpu.VMEM((n_tp - 1, 1, width), f32),
            dma((10,)), dma((blocks, seqs)), dma((blocks, seqs)), dma((seqs, 2, n_tp - 1)), dma((seqs, 2, n_tp - 1)),
            dma((2,)), dma, dma((2, 2, n_fsdp // 2)), dma((2, 2, peers)), dma((devices - 1,)), dma((devices - 1,)),
            dma((n_tp,)), dma((4, 2)), dma((2,)),
        ],
        compiler_params=params(3),
        cost_estimate=pl.CostEstimate(flops=200 * 10**9, bytes_accessed=60 << 20, transcendentals=0),
        name="back",
    )(
        attn_low, w, raw, low, prev, head_low, stats, x, mixed_own, attention, down,
        gain_q, gain_k, gain_a, gain_m, gain_a_own, gain_m_own, cosine, sine,
    )


def rotation_tables(length):
    half = HD // 2
    frequency = rope_theta ** (-np.arange(half) * 2.0 / HD)
    angles = np.arange(length)[:, None] * frequency[None, :]
    cosine, sine = np.cos(angles), np.sin(angles)
    return (
        jnp.asarray(np.concatenate([cosine, cosine], axis=1), f32),
        jnp.asarray(np.concatenate([-sine, sine], axis=1), f32),
    )


def per_device(
    tokens, w_query, w_key, w_value, w_output, w_gate, w_up, w_down,
    gain_query, gain_key, gain_attn, gain_mlp, cotangent,
):
    micro_count, rows, width = tokens.shape
    local = w_query.shape[1]
    ctx = lax.axis_size("ctx")
    tp = lax.axis_size("tp")
    cosine, sine = rotation_tables(rows * ctx)
    gain_q = gain_query.astype(f32)
    gain_k = gain_key.astype(f32)
    gain_a = gain_attn.astype(f32)
    gain_m = gain_mlp.astype(f32)
    xy = ("fsdp", "ctx")

    def gather(w):
        return lax.all_gather(w, xy, axis=0, tiled=True)

    w_g = gather(w_gate)
    w_u = gather(w_up)
    w_down_t = gather(w_down.T)

    flat = (micro_count * rows, width)
    x_all, grad_all = tokens.reshape(flat), cotangent.reshape(flat)

    n_xy = (lax.axis_size("fsdp"), ctx)
    raw, low, prev, head_low, stats, attention, mlp_in, w_full, attn_own = front(
        x_all, w_query, w_key, w_value, w_output.T, gain_q[None], gain_k[None], gain_a[None], cosine, sine,
        micro_count, tp, n_xy
    )
    down, _, attn_low, mlp_weights, _, _, down_blocks, mixed_own, gain_m_sum, gain_a_sum = mlp(
        mlp_in, grad_all, attn_own, gain_m[None], gain_a[None], w_g, w_u, w_down_t, tp, n_xy
    )
    def scatter(full):
        return lax.psum_scatter(full, xy, scatter_dimension=0, tiled=True).astype(f32)

    units = w_gate.shape[1]
    d_mlp = scatter(mlp_weights)
    d_down = jnp.sum(down_blocks.astype(f32), axis=0).T
    d_gate, d_up = d_mlp[:, :units], d_mlp[:, units:]
    grad_tokens, out, gains, d_attn, _ = back(
        attn_low, w_full, raw, low, prev, head_low, stats, x_all, mixed_own, attention, down,
        gain_q[None], gain_k[None], gain_a[None], gain_m[None], gain_a_sum, gain_m_sum, cosine, sine,
        micro_count, tp, n_xy
    )
    gains = gains[0]
    block = w_query.shape[0]
    d_v, d_k, d_q, d_o = (d_attn[k * block : (k + 1) * block] for k in range(4))
    return (
        out.reshape(tokens.shape),
        grad_tokens.reshape(tokens.shape),
        d_q, d_k, d_v, d_o.T, d_gate, d_up, d_down,
        gains[:local], gains[local : 2 * local],
        gains[2 * local : 2 * local + width], gains[2 * local + width :],
    )


def solution(mesh):
    rows, cols = P(("fsdp", "ctx"), "tp"), P("tp", ("fsdp", "ctx"))
    acts = P("fsdp", "ctx", None)
    in_specs = (acts, rows, rows, rows, cols, rows, rows, cols, P("tp"), P("tp"), P(), P(), acts)
    out_specs = (acts, acts, rows, rows, rows, cols, rows, rows, cols, P("tp"), P("tp"), P(), P())
    return jax.shard_map(
        per_device, mesh=mesh, in_specs=in_specs, out_specs=out_specs, check_vma=False
    )
```
